512 devices in a mesh: node: 64 (over y, x, core), edge: 8 (over z).
Axes of the slice: x: 4, y: 8, z: 8, core: 2. Of those that a mesh axis runs over, the one named last changes fastest.
Arguments:
- embedding: bfloat16 [512, 128, 512], P('node'), may hold values from -6 to 6
- send_list: int32 [8, 64, 64], P('edge', 'node'), may hold values from -1 to 7, as said below
- edge_ends: int32 [2, 1048576], P(None, ('node', 'edge')), may hold values from 0 to 65535, as said below
- pair_index: int32 [1048576], P(('node', 'edge')), may hold values from 0 to 65535, as said below
- w_first: bfloat16 [1024, 512], replicated, may hold values from -0.1875 to 0.1875
- b_first: float32 [512], replicated, may hold values from -3 to 3
- w_second: bfloat16 [512], replicated, may hold values from -0.25 to 0.25
Outputs:
- edge_score: float32 [1048576], P(('node', 'edge'))
- pair_cost: float32 [65536], P(('node', 'edge'))
The draws below stay inside these ranges and needn't reach their ends.
Inputs may be any that keep to these rules, and one draw needn't show every extreme that they name: Each entry is -1 or a block index of the sending node index; send_list[e, k, k] is never -1. `edge_ends`: node ids; most ends lie in a block that the send list delivers to the edge's node group and edge index. `pair_index`: an edge of node group j has a pair in j * 1024 to (j + 1) * 1024 - 1.
All inputs are finite; a program needn't handle non-finite values.
Results may differ from the reference program's by a relative error of at most 0.0003.
Values may be sent and summed in bfloat16 or wider, within the bound.
A program may use at most 64 MiB of HBM per device.

```python
import jax
import jax.numpy as jnp
from jax import lax

F = 512
HID = 512
BLOCK = 128
NB_DEV = 8
E_DEV = 2048
PAIRS_ROW = 1024
NODE_BLOCKS = 512
NODES = 65536
EDGES = 1048576
PAIRS = 65536
N_NODE = 64
N_EDGE = 8


def routing(key):
    first_key, second_key = jax.random.split(jax.random.fold_in(key, 11), 2)
    shape_all = (N_EDGE, N_NODE, N_NODE)
    living = jax.random.randint(first_key, shape_all, 0, 5) < 3
    chosen = jax.random.randint(second_key, shape_all, 0, NB_DEV)
    source = jnp.arange(N_NODE)[None, :, None]
    target = jnp.arange(N_NODE)[None, None, :]
    diagonal = source == target
    chosen = jnp.where(diagonal & (source == 0), 0, chosen)
    chosen = jnp.where(diagonal & (source == N_NODE - 1), NB_DEV - 1, chosen)
    living = living | diagonal
    return jnp.where(living, chosen, -1).astype(jnp.int32)


def draw_send_list(key, part):
    return routing(key)


def draw_edge_ends(key, part):
    lists_all = routing(key)
    key_source, key_row, key_any, key_pick = jax.random.split(jax.random.fold_in(key, 23), 4)
    device = jnp.arange(EDGES) // E_DEV
    group = jnp.broadcast_to(device // N_EDGE, (2, EDGES))
    edge_pos = jnp.broadcast_to(device % N_EDGE, (2, EDGES))
    source = jax.random.randint(key_source, (2, EDGES), 0, N_NODE)
    block_here = lists_all[edge_pos, source, group]
    source = jnp.where(block_here >= 0, source, group)
    block_here = lists_all[edge_pos, source, group]
    row_here = jax.random.randint(key_row, (2, EDGES), 0, BLOCK)
    delivered = (source * NB_DEV + block_here) * BLOCK + row_here
    any_ids = jax.random.randint(key_any, (2, EDGES), 0, NODES)
    picker = jax.random.randint(key_pick, (2, EDGES), 0, 10) < 9
    node_ids = jnp.where(picker, delivered, any_ids)
    own_block = (group * NB_DEV + lists_all[edge_pos, group, group]) * BLOCK
    leading = (jnp.arange(EDGES) % E_DEV == 0)[None, :]
    fixed_ends = jnp.concatenate([own_block[:1], own_block[1:] + BLOCK - 1], axis=0)
    node_ids = jnp.where(leading, fixed_ends, node_ids)
    return node_ids.astype(jnp.int32)


def draw_pair_index(key, part):
    device = jnp.arange(EDGES) // E_DEV
    group = device // N_EDGE
    offset = jax.random.randint(jax.random.fold_in(key, 37), (EDGES,), 0, PAIRS_ROW)
    position = jnp.arange(EDGES) % E_DEV
    offset = jnp.where(position == 0, 0, offset)
    offset = jnp.where(position == 1, PAIRS_ROW - 1, offset)
    return (group * PAIRS_ROW + offset).astype(jnp.int32)


def level_of(key, dims, pieces, least, high):
    factor_of = 1.0
    for dim, parts in pieces:
        steps = jax.random.uniform(jax.random.fold_in(jax.random.fold_in(key, 6), dim), (parts,), jnp.float32, least / len(pieces), high / len(pieces))
        factor_of = factor_of * jnp.repeat(jnp.exp(steps), dims[dim] // parts).reshape((-1,) + (1,) * (len(dims) - 1 - dim))
    return factor_of


def centred(stream_key, dims, scale, limit, cuts=(), kind=jnp.bfloat16):
    drawn = jax.random.normal(stream_key, dims, jnp.float32) * scale
    if len(cuts) > 0:
        drawn = level_of(stream_key, dims, cuts, -0.22, 0.18) * drawn
    return jnp.clip(drawn, min=-limit, max=limit).astype(kind)


def setup_inputs(seed: int = 0) -> dict:
    seeds = jax.random.split(jax.random.key(seed), 8)
    embedding = centred(seeds[0], (NODE_BLOCKS, BLOCK, F), 1.0, 6.0, ((0, 64),))
    send_list = draw_send_list(jax.random.fold_in(seeds[7], 71), 0)
    edge_ends = draw_edge_ends(jax.random.fold_in(seeds[7], 71), 0)
    pair_index = draw_pair_index(jax.random.fold_in(seeds[7], 71), 0)
    w_first = centred(seeds[4], (2 * F, HID), (2 * F) ** -0.5, 0.1875)
    b_first = centred(seeds[5], (HID,), 0.5, 3.0, (), jnp.float32)
    w_second = centred(seeds[6], (HID,), HID ** -0.5, 0.25)
    return dict(embedding=embedding, send_list=send_list, edge_ends=edge_ends, pair_index=pair_index, w_first=w_first, b_first=b_first, w_second=w_second)


def reference(embedding, send_list, edge_ends, pair_index, w_first, b_first, w_second):
    flat_rows = embedding.reshape(NODES, F)
    upper = w_first[:F]
    bottom = w_first[F:]
    w_out = w_second.astype(jnp.float32)

    def device_scores(device):
        group = device // N_EDGE
        edge_pos = device % N_EDGE
        node_ids = lax.dynamic_slice(edge_ends, (jnp.int32(0), (device * E_DEV).astype(jnp.int32)), (2, E_DEV))
        block_ids = node_ids // BLOCK
        source = block_ids // NB_DEV
        lists_here = lax.dynamic_index_in_dim(send_list, edge_pos, 0, False)
        column = lax.dynamic_index_in_dim(lists_here, group, 1, False)
        present = jnp.take(column, source) == block_ids % NB_DEV
        end_rows = jnp.take(flat_rows, node_ids, axis=0)
        end_rows = jnp.where(present[..., None], end_rows, jnp.zeros_like(end_rows))
        preact = jnp.dot(end_rows[0], upper, preferred_element_type=jnp.float32)
        preact = preact + jnp.dot(end_rows[1], bottom, preferred_element_type=jnp.float32) + b_first
        hidden = jax.nn.gelu(preact, approximate=True)
        return jnp.dot(hidden, w_out, precision=lax.Precision.HIGHEST)

    scores = lax.map(device_scores, jnp.arange(EDGES // E_DEV, dtype=jnp.int32))
    edge_score = scores.reshape(EDGES)
    pair_cost = jnp.zeros((PAIRS,), jnp.float32).at[pair_index].add(edge_score)
    return edge_score, pair_cost
```

```python
import functools

import jax
import jax.numpy as jnp
from jax import lax
from jax.experimental import pallas as pl
from jax.experimental.pallas import tpu as pltpu
from jax.sharding import PartitionSpec as P

PAIRS_ROW = 1024
TILE = 256


def gelu_tanh(x):
    return x * (0.5 * (1.0 + jnp.tanh(0.7978845608028654 * (x + 0.044715 * (x * x * x)))))


def score_kernel(edges, pos_ref, table, mask_ref, wt_ref, wb_ref, bias_ref, wo_ref, pid_ref,
                 score_ref, pool_ref, buf, sems):
    step = pl.program_id(0)
    steps = pl.num_programs(0)

    def fetch(tile, slot):
        base = tile * TILE

        def one(r, carry):
            p0 = pos_ref[base + r]
            p1 = pos_ref[edges + base + r]
            pltpu.make_async_copy(table.at[pl.ds(p0, 1)], buf.at[0, slot, pl.ds(r, 1)], sems.at[0, slot]).start()
            pltpu.make_async_copy(table.at[pl.ds(p1, 1)], buf.at[1, slot, pl.ds(r, 1)], sems.at[1, slot]).start()
            return carry

        lax.fori_loop(0, TILE, one, 0, unroll=8)

    @pl.when(step == 0)
    def _():
        fetch(0, 0)
        pool_ref[...] = jnp.zeros_like(pool_ref)

    slot = step % 2

    @pl.when(step + 1 < steps)
    def _():
        fetch(step + 1, 1 - slot)

    for end in range(2):
        pltpu.make_async_copy(table.at[pl.ds(0, TILE)], buf.at[end, slot], sems.at[end, slot]).wait()

    mask = mask_ref[...]
    rows0 = buf[0, slot].astype(jnp.bfloat16)
    rows1 = buf[1, slot].astype(jnp.bfloat16)
    rows0 = jnp.where(mask[:, 0:1] > 0, rows0, jnp.zeros_like(rows0))
    rows1 = jnp.where(mask[:, 1:2] > 0, rows1, jnp.zeros_like(rows1))
    preact = jnp.dot(rows0, wt_ref[...], preferred_element_type=jnp.float32)
    preact = preact + jnp.dot(rows1, wb_ref[...], preferred_element_type=jnp.float32) + bias_ref[...]
    hidden = gelu_tanh(preact)
    scores = lax.dot_general(wo_ref[...], hidden, (((1,), (1,)), ((), ())),
                             precision=lax.Precision.HIGHEST, preferred_element_type=jnp.float32)
    score_ref[...] = scores[0:1]
    pair_range = lax.broadcasted_iota(jnp.int32, (TILE, PAIRS_ROW), 1)
    onehot = (pid_ref[...] == pair_range).astype(jnp.float32)
    pooled = jnp.dot(scores, onehot, precision=lax.Precision.HIGHEST, preferred_element_type=jnp.float32)
    pool_ref[...] += pooled[0:1]


def edge_scores(position, located, pair_ids, table, w_first, b_first, w_second):
    edges = position.shape[1]
    width = table.shape[1]
    hid = w_first.shape[1]
    tiles = edges // TILE
    pos_flat = position.reshape(2 * edges)
    mask = located.T.astype(jnp.float32)
    wo8 = jnp.broadcast_to(w_second.astype(jnp.float32)[None, :], (8, hid))
    grid_spec = pltpu.PrefetchScalarGridSpec(
        num_scalar_prefetch=1,
        grid=(tiles,),
        in_specs=[
            pl.BlockSpec(memory_space=pl.ANY),
            pl.BlockSpec((TILE, 2), lambda i, p: (i, 0)),
            pl.BlockSpec((width, hid), lambda i, p: (0, 0)),
            pl.BlockSpec((width, hid), lambda i, p: (1, 0)),
            pl.BlockSpec((1, hid), lambda i, p: (0, 0)),
            pl.BlockSpec((8, hid), lambda i, p: (0, 0)),
            pl.BlockSpec((TILE, 1), lambda i, p: (i, 0)),
        ],
        out_specs=[
            pl.BlockSpec((1, TILE), lambda i, p: (0, i)),
            pl.BlockSpec((1, PAIRS_ROW), lambda i, p: (0, 0)),
        ],
        scratch_shapes=[
            pltpu.VMEM((2, 2, TILE, width), table.dtype),
            pltpu.SemaphoreType.DMA((2, 2)),
        ],
    )
    scores, pooled = pl.pallas_call(
        functools.partial(score_kernel, edges),
        grid_spec=grid_spec,
        out_shape=[
            jax.ShapeDtypeStruct((1, edges), jnp.float32),
            jax.ShapeDtypeStruct((1, PAIRS_ROW), jnp.float32),
        ],
        compiler_params=pltpu.CompilerParams(dimension_semantics=("arbitrary",)),
        cost_estimate=pl.CostEstimate(
            flops=2 * edges * 2 * width * hid, transcendentals=edges * hid,
            bytes_accessed=2 * edges * width * table.dtype.itemsize),
    )(pos_flat, table, mask, w_first, w_first, b_first.reshape(1, hid), wo8, pair_ids.reshape(edges, 1))
    return scores.reshape(edges), pooled.reshape(PAIRS_ROW)


def body(embedding, send_list, edge_ends, pair_index, w_first, b_first, w_second):
    node_count = lax.axis_size("node")
    node_self = lax.axis_index("node")
    blocks_here = embedding.shape[0]
    block_rows = embedding.shape[1]
    feature_width = embedding.shape[2]
    wanted = send_list[0, 0]
    picked = jnp.take(embedding, jnp.clip(wanted, 0, blocks_here - 1), axis=0)
    labels = jnp.where(wanted >= 0, node_self * blocks_here + wanted, -1)
    arrived, slot_ids = (
        lax.all_to_all(picked, "node", split_axis=0, concat_axis=0, tiled=True),
        lax.all_to_all(labels, "node", split_axis=0, concat_axis=0, tiled=True),
    )
    table = arrived.reshape(node_count * block_rows, feature_width).astype(jnp.float32)
    target = edge_ends // block_rows
    within = edge_ends % block_rows
    matches = target[..., None] == slot_ids
    located = jnp.any(matches, axis=-1)
    slot_index = jnp.sum(jnp.where(matches, jnp.arange(node_count, dtype=jnp.int32), 0), axis=-1)
    position = slot_index * block_rows + within
    pair_ids = pair_index - node_self * PAIRS_ROW
    edge_score, pooled_sum = edge_scores(position, located, pair_ids, table, w_first, b_first, w_second)
    pair_cost = lax.psum_scatter(pooled_sum, "edge", scatter_dimension=0, tiled=True)
    return (edge_score, pair_cost)


def solution(mesh):
    return jax.shard_map(
        body,
        mesh=mesh,
        in_specs=(
            P("node", None, None),
            P("edge", "node", None),
            P(None, ("node", "edge")),
            P(("node", "edge")),
            P(),
            P(),
            P(),
        ),
        out_specs=(P(("node", "edge")), P(("node", "edge"))),
        check_vma=False,
    )
```

```python
import functools

import jax
import jax.numpy as jnp
from jax import lax
from jax.experimental import pallas as pl
from jax.experimental.pallas import tpu as pltpu
from jax.sharding import PartitionSpec as P

PAIRS_ROW = 1024
TILE = 256


def gelu_tanh(x):
    return x * (0.5 * (1.0 + jnp.tanh(0.7978845608028654 * (x + 0.044715 * (x * x * x)))))


def score_kernel(edges, pos_ref, table, mask_ref, wt_ref, wb_ref, bias_ref, wo_ref, pid_ref,
                 score_ref, pool_ref, buf, wide, sems):
    step = pl.program_id(0)
    steps = pl.num_programs(0)
    parts = buf.shape[2] // TILE

    def fetch(tile, slot):
        base = tile * TILE

        def one(r, carry):
            dst = pl.ds(pl.multiple_of(r * parts, parts), parts)
            for end in range(2):
                src = pl.ds(pl.multiple_of(pos_ref[end * edges + base + r], parts), parts)
                pltpu.make_async_copy(table.at[src], buf.at[end, slot, dst], sems.at[end, slot]).start()
            return carry

        lax.fori_loop(0, TILE, one, 0, unroll=8)

    @pl.when(step == 0)
    def _():
        fetch(0, 0)
        pool_ref[...] = jnp.zeros_like(pool_ref)

    slot = step % 2

    @pl.when(step + 1 < steps)
    def _():
        fetch(step + 1, 1 - slot)

    for end in range(2):
        pltpu.make_async_copy(table.at[pl.ds(0, TILE * parts)], buf.at[end, slot], sems.at[end, slot]).wait()

    mask = mask_ref[...]
    lanes = buf.shape[3]
    preact = bias_ref[...]
    for end, w_ref in ((0, wt_ref), (1, wb_ref)):
        wide[...] = buf[end, slot].astype(jnp.float32)
        keep = mask[:, end:end + 1] > 0
        for q in range(parts):
            piece = wide[pl.ds(q, TILE, stride=parts), :]
            piece = jnp.where(keep, piece, jnp.zeros_like(piece)).astype(jnp.bfloat16)
            preact = preact + jnp.dot(piece, w_ref[q * lanes:(q + 1) * lanes, :],
                                      preferred_element_type=jnp.float32)
    hidden = gelu_tanh(preact)
    scores = lax.dot_general(wo_ref[...], hidden, (((1,), (1,)), ((), ())),
                             precision=lax.Precision.HIGHEST, preferred_element_type=jnp.float32)
    score_ref[...] = scores[0:1]
    pair_range = lax.broadcasted_iota(jnp.int32, (TILE, PAIRS_ROW), 1)
    onehot = (pid_ref[...] == pair_range).astype(jnp.float32)
    pooled = jnp.dot(scores, onehot, precision=lax.Precision.HIGHEST, preferred_element_type=jnp.float32)
    pool_ref[...] += pooled[0:1]


def edge_scores(position, located, pair_ids, table, w_first, b_first, w_second):
    edges = position.shape[1]
    lanes = table.shape[1]
    width = w_first.shape[0] // 2
    parts = width // lanes
    hid = w_first.shape[1]
    tiles = edges // TILE
    pos_flat = position.reshape(2 * edges)
    mask = located.T.astype(jnp.float32)
    wo8 = jnp.broadcast_to(w_second.astype(jnp.float32)[None, :], (8, hid))
    grid_spec = pltpu.PrefetchScalarGridSpec(
        num_scalar_prefetch=1,
        grid=(tiles,),
        in_specs=[
            pl.BlockSpec(memory_space=pl.ANY),
            pl.BlockSpec((TILE, 2), lambda i, p: (i, 0)),
            pl.BlockSpec((width, hid), lambda i, p: (0, 0)),
            pl.BlockSpec((width, hid), lambda i, p: (1, 0)),
            pl.BlockSpec((1, hid), lambda i, p: (0, 0)),
            pl.BlockSpec((8, hid), lambda i, p: (0, 0)),
            pl.BlockSpec((TILE, 1), lambda i, p: (i, 0)),
        ],
        out_specs=[
            pl.BlockSpec((1, TILE), lambda i, p: (0, i)),
            pl.BlockSpec((1, PAIRS_ROW), lambda i, p: (0, 0)),
        ],
        scratch_shapes=[
            pltpu.VMEM((2, 2, TILE * parts, lanes), table.dtype),
            pltpu.VMEM((TILE * parts, lanes), jnp.float32),
            pltpu.SemaphoreType.DMA((2, 2)),
        ],
    )
    scores, pooled = pl.pallas_call(
        functools.partial(score_kernel, edges),
        grid_spec=grid_spec,
        out_shape=[
            jax.ShapeDtypeStruct((1, edges), jnp.float32),
            jax.ShapeDtypeStruct((1, PAIRS_ROW), jnp.float32),
        ],
        compiler_params=pltpu.CompilerParams(dimension_semantics=("arbitrary",)),
        cost_estimate=pl.CostEstimate(
            flops=2 * edges * 2 * width * hid, transcendentals=edges * hid,
            bytes_accessed=2 * edges * width * table.dtype.itemsize),
    )(pos_flat, table, mask, w_first, w_first, b_first.reshape(1, hid), wo8, pair_ids.reshape(edges, 1))
    return scores.reshape(edges), pooled.reshape(PAIRS_ROW)


def body(embedding, send_list, edge_ends, pair_index, w_first, b_first, w_second):
    node_count = lax.axis_size("node")
    node_self = lax.axis_index("node")
    blocks_here = embedding.shape[0]
    block_rows = embedding.shape[1]
    feature_width = embedding.shape[2]
    lanes = 128
    parts = feature_width // lanes
    block_len = block_rows * parts
    slot_len = block_len + 8
    wanted = send_list[0, 0]
    narrow = embedding.reshape(blocks_here, block_len, lanes)
    picked = jnp.take(narrow, jnp.clip(wanted, 0, blocks_here - 1), axis=0, mode="clip")
    label_rows = jnp.broadcast_to(wanted.astype(embedding.dtype)[:, None, None], (node_count, 8, lanes))
    picked = jnp.concatenate([picked, label_rows], axis=1)
    arrived = lax.all_to_all(picked, "node", split_axis=0, concat_axis=0, tiled=True)
    table = arrived.reshape(node_count * slot_len, lanes)
    source = edge_ends // (blocks_here * block_rows)
    block_of = (edge_ends // block_rows) % blocks_here
    position = source * slot_len + (edge_ends % block_rows) * parts
    sent = arrived[:, block_len, 0].astype(jnp.int32)
    located = jnp.any((source[..., None] == jnp.arange(node_count, dtype=jnp.int32))
                      & (block_of[..., None] == sent), axis=-1)
    pair_ids = pair_index - node_self * PAIRS_ROW
    edge_score, pooled_sum = edge_scores(position, located, pair_ids, table, w_first, b_first, w_second)
    pair_cost = lax.psum_scatter(pooled_sum, "edge", scatter_dimension=0, tiled=True)
    return (edge_score, pair_cost)


def solution(mesh):
    return jax.shard_map(
        body,
        mesh=mesh,
        in_specs=(
            P("node", None, None),
            P("edge", "node", None),
            P(None, ("node", "edge")),
            P(("node", "edge")),
            P(),
            P(),
            P(),
        ),
        out_specs=(P(("node", "edge")), P(("node", "edge"))),
        check_vma=False,
    )
```

```python
import functools

import jax
import jax.numpy as jnp
from jax import lax
from jax.experimental import pallas as pl
from jax.experimental.pallas import tpu as pltpu
from jax.sharding import PartitionSpec as P

PAIRS_ROW = 1024
TILE = 256


def gelu_tanh(x):
    return x * (0.5 * (1.0 + jnp.tanh(0.7978845608028654 * (x + 0.044715 * (x * x * x)))))


def score_kernel(edges, pos_ref, table, mask_ref, wt_ref, wb_ref, bias_ref, wo_ref, pid_ref,
                 score_ref, pool_ref, buf, wide, sems):
    step = pl.program_id(0)
    steps = pl.num_programs(0)
    parts = buf.shape[2] // TILE

    def fetch(tile, slot):
        base = tile * TILE

        def one(r, carry):
            dst = pl.ds(pl.multiple_of(r * parts, parts), parts)
            for end in range(2):
                src = pl.ds(pl.multiple_of(pos_ref[end * edges + base + r], parts), parts)
                pltpu.make_async_copy(table.at[src], buf.at[end, slot, dst], sems.at[end, slot]).start()
            return carry

        lax.fori_loop(0, TILE, one, 0, unroll=8)

    @pl.when(step == 0)
    def _():
        fetch(0, 0)
        pool_ref[...] = jnp.zeros_like(pool_ref)

    slot = step % 2

    @pl.when(step + 1 < steps)
    def _():
        fetch(step + 1, 1 - slot)

    for end in range(2):
        pltpu.make_async_copy(table.at[pl.ds(0, TILE * parts)], buf.at[end, slot], sems.at[end, slot]).wait()

    mask = mask_ref[...]
    lanes = buf.shape[3]
    preact = bias_ref[...]
    for end, w_ref in ((0, wt_ref), (1, wb_ref)):
        wide[...] = buf[end, slot].astype(jnp.float32)
        keep = mask[:, end:end + 1] > 0
        for q in range(parts):
            piece = wide[pl.ds(q, TILE, stride=parts), :]
            piece = jnp.where(keep, piece, jnp.zeros_like(piece)).astype(jnp.bfloat16)
            preact = preact + jnp.dot(piece, w_ref[q * lanes:(q + 1) * lanes, :],
                                      preferred_element_type=jnp.float32)
    hidden = gelu_tanh(preact)
    scores = jnp.sum(hidden * wo_ref[0:1, :], axis=1, keepdims=True)
    score_ref[...] = scores
    pair_range = lax.broadcasted_iota(jnp.int32, (TILE, PAIRS_ROW), 1)
    picked = jnp.where(pid_ref[...] == pair_range, scores, 0.0)
    pool_ref[...] += jnp.sum(picked, axis=0, keepdims=True)


def edge_scores(position, located, pair_ids, table, w_first, b_first, w_second):
    edges = position.shape[1]
    lanes = table.shape[1]
    width = w_first.shape[0] // 2
    parts = width // lanes
    hid = w_first.shape[1]
    tiles = edges // TILE
    pos_flat = position.reshape(2 * edges)
    mask = located.T.astype(jnp.float32)
    wo8 = jnp.broadcast_to(w_second.astype(jnp.float32)[None, :], (8, hid))
    grid_spec = pltpu.PrefetchScalarGridSpec(
        num_scalar_prefetch=1,
        grid=(tiles,),
        in_specs=[
            pl.BlockSpec(memory_space=pl.ANY),
            pl.BlockSpec((TILE, 2), lambda i, p: (i, 0)),
            pl.BlockSpec((width, hid), lambda i, p: (0, 0)),
            pl.BlockSpec((width, hid), lambda i, p: (1, 0)),
            pl.BlockSpec((1, hid), lambda i, p: (0, 0)),
            pl.BlockSpec((8, hid), lambda i, p: (0, 0)),
            pl.BlockSpec((TILE, 1), lambda i, p: (i, 0)),
        ],
        out_specs=[
            pl.BlockSpec((TILE, 1), lambda i, p: (i, 0)),
            pl.BlockSpec((1, PAIRS_ROW), lambda i, p: (0, 0)),
        ],
        scratch_shapes=[
            pltpu.VMEM((2, 2, TILE * parts, lanes), table.dtype),
            pltpu.VMEM((TILE * parts, lanes), jnp.float32),
            pltpu.SemaphoreType.DMA((2, 2)),
        ],
    )
    scores, pooled = pl.pallas_call(
        functools.partial(score_kernel, edges),
        grid_spec=grid_spec,
        out_shape=[
            jax.ShapeDtypeStruct((edges, 1), jnp.float32),
            jax.ShapeDtypeStruct((1, PAIRS_ROW), jnp.float32),
        ],
        compiler_params=pltpu.CompilerParams(dimension_semantics=("arbitrary",)),
        cost_estimate=pl.CostEstimate(
            flops=2 * edges * 2 * width * hid, transcendentals=edges * hid,
            bytes_accessed=2 * edges * width * table.dtype.itemsize),
    )(pos_flat, table, mask, w_first, w_first, b_first.reshape(1, hid), wo8, pair_ids.reshape(edges, 1))
    return scores.reshape(edges), pooled.reshape(PAIRS_ROW)


def body(embedding, send_list, edge_ends, pair_index, w_first, b_first, w_second):
    node_count = lax.axis_size("node")
    node_self = lax.axis_index("node")
    blocks_here = embedding.shape[0]
    block_rows = embedding.shape[1]
    feature_width = embedding.shape[2]
    lanes = 128
    parts = feature_width // lanes
    block_len = block_rows * parts
    slot_len = block_len + 8
    wanted = send_list[0, 0]
    narrow = embedding.reshape(blocks_here, block_len, lanes)
    narrow = jnp.concatenate([narrow, jnp.zeros((1, block_len, lanes), embedding.dtype)], axis=0)
    marks = jnp.arange(blocks_here + 1, dtype=jnp.int32)
    marks = jnp.where(marks < blocks_here, marks, -1).astype(embedding.dtype)
    marks = jnp.broadcast_to(marks[:, None, None], (blocks_here + 1, 8, lanes))
    source_blocks = jnp.concatenate([narrow, marks], axis=1)
    picked = jnp.take(source_blocks, jnp.where(wanted >= 0, wanted, blocks_here), axis=0, mode="clip")
    arrived = lax.all_to_all(picked, "node", split_axis=0, concat_axis=0, tiled=True)
    table = arrived.reshape(node_count * slot_len, lanes)
    source = edge_ends // (blocks_here * block_rows)
    block_of = (edge_ends // block_rows) % blocks_here
    position = source * slot_len + (edge_ends % block_rows) * parts
    sent = arrived[:, block_len, 0].astype(jnp.int32)
    located = jnp.any((source[..., None] == jnp.arange(node_count, dtype=jnp.int32))
                      & (block_of[..., None] == sent), axis=-1)
    pair_ids = pair_index - node_self * PAIRS_ROW
    edge_score, pooled_sum = edge_scores(position, located, pair_ids, table, w_first, b_first, w_second)
    pair_cost = lax.psum_scatter(pooled_sum, "edge", scatter_dimension=0, tiled=True)
    return (edge_score, pair_cost)


def solution(mesh):
    return jax.shard_map(
        body,
        mesh=mesh,
        in_specs=(
            P("node", None, None),
            P("edge", "node", None),
            P(None, ("node", "edge")),
            P(("node", "edge")),
            P(),
            P(),
            P(),
        ),
        out_specs=(P(("node", "edge")), P(("node", "edge"))),
        check_vma=False,
    )
```

```python
import functools

import jax
import jax.numpy as jnp
from jax import lax
from jax.experimental import pallas as pl
from jax.experimental.pallas import tpu as pltpu
from jax.sharding import PartitionSpec as P

PAIRS_ROW = 1024
TILE = 256


def gelu_tanh(x):
    return x * (0.5 * (1.0 + jnp.tanh(0.7978845608028654 * (x + 0.044715 * (x * x * x)))))


def score_kernel(edges, pos_ref, table, mask_ref, wt_ref, wb_ref, bias_ref, wo_ref, pid_ref,
                 score_ref, pool_ref, buf):
    step = pl.program_id(0)
    parts = buf.shape[1] // TILE
    base = step * TILE

    @pl.when(step == 0)
    def _():
        pool_ref[...] = jnp.zeros_like(pool_ref)

    half_rows = lax.broadcasted_iota(jnp.int32, (2 * parts, buf.shape[2]), 0) < parts

    def near(end, r, half):
        p = pos_ref[end * edges + base + r]
        group = table[pl.ds(pl.multiple_of((p // (2 * parts)) * (2 * parts), 2 * parts), 2 * parts), :]
        group = group.astype(jnp.float32)
        turned = pltpu.roll(group, parts, 0)
        return jnp.where((p // parts) % 2 == half, group, turned)

    def pair(s, carry):
        dst = pl.ds(pl.multiple_of(s * 2 * parts, 2 * parts), 2 * parts)
        for end in range(2):
            buf[end, dst, :] = jnp.where(half_rows, near(end, 2 * s, 0), near(end, 2 * s + 1, 1))
        return carry

    lax.fori_loop(0, TILE // 2, pair, 0, unroll=4)

    mask = mask_ref[...]
    lanes = buf.shape[2]
    preact = bias_ref[...]
    for end, w_ref in ((0, wt_ref), (1, wb_ref)):
        keep = mask[:, end:end + 1] > 0
        for q in range(parts):
            piece = buf[end, pl.ds(q, TILE, stride=parts), :]
            piece = jnp.where(keep, piece, jnp.zeros_like(piece)).astype(jnp.bfloat16)
            preact = preact + jnp.dot(piece, w_ref[q * lanes:(q + 1) * lanes, :],
                                      preferred_element_type=jnp.float32)
    hidden = gelu_tanh(preact)
    scores = jnp.sum(hidden * wo_ref[0:1, :], axis=1, keepdims=True)
    score_ref[...] = scores
    pair_range = lax.broadcasted_iota(jnp.int32, (TILE, PAIRS_ROW), 1)
    picked = jnp.where(pid_ref[...] == pair_range, scores, 0.0)
    pool_ref[...] += jnp.sum(picked, axis=0, keepdims=True)


def edge_scores(position, located, pair_ids, table, w_first, b_first, w_second):
    edges = position.shape[1]
    lanes = table.shape[1]
    width = w_first.shape[0] // 2
    parts = width // lanes
    hid = w_first.shape[1]
    tiles = edges // TILE
    pos_flat = position.reshape(2 * edges)
    mask = located.T.astype(jnp.float32)
    wo8 = jnp.broadcast_to(w_second.astype(jnp.float32)[None, :], (8, hid))
    grid_spec = pltpu.PrefetchScalarGridSpec(
        num_scalar_prefetch=1,
        grid=(tiles,),
        in_specs=[
            pl.BlockSpec(memory_space=pltpu.VMEM),
            pl.BlockSpec((TILE, 2), lambda i, p: (i, 0)),
            pl.BlockSpec((width, hid), lambda i, p: (0, 0)),
            pl.BlockSpec((width, hid), lambda i, p: (1, 0)),
            pl.BlockSpec((1, hid), lambda i, p: (0, 0)),
            pl.BlockSpec((8, hid), lambda i, p: (0, 0)),
            pl.BlockSpec((TILE, 1), lambda i, p: (i, 0)),
        ],
        out_specs=[
            pl.BlockSpec((TILE, 1), lambda i, p: (i, 0)),
            pl.BlockSpec((1, PAIRS_ROW), lambda i, p: (0, 0)),
        ],
        scratch_shapes=[
            pltpu.VMEM((2, TILE * parts, lanes), jnp.float32),
        ],
    )
    scores, pooled = pl.pallas_call(
        functools.partial(score_kernel, edges),
        grid_spec=grid_spec,
        out_shape=[
            jax.ShapeDtypeStruct((edges, 1), jnp.float32),
            jax.ShapeDtypeStruct((1, PAIRS_ROW), jnp.float32),
        ],
        compiler_params=pltpu.CompilerParams(dimension_semantics=("arbitrary",), vmem_limit_bytes=48 * 1024 * 1024),
        cost_estimate=pl.CostEstimate(
            flops=2 * edges * 2 * width * hid, transcendentals=edges * hid,
            bytes_accessed=2 * edges * width * table.dtype.itemsize),
    )(pos_flat, table, mask, w_first, w_first, b_first.reshape(1, hid), wo8, pair_ids.reshape(edges, 1))
    return scores.reshape(edges), pooled.reshape(PAIRS_ROW)


def body(embedding, send_list, edge_ends, pair_index, w_first, b_first, w_second):
    node_count = lax.axis_size("node")
    node_self = lax.axis_index("node")
    blocks_here = embedding.shape[0]
    block_rows = embedding.shape[1]
    feature_width = embedding.shape[2]
    lanes = 128
    parts = feature_width // lanes
    block_len = block_rows * parts
    slot_len = block_len + 8
    wanted = send_list[0, 0]
    narrow = embedding.reshape(blocks_here, block_len, lanes)
    narrow = jnp.concatenate([narrow, jnp.zeros((1, block_len, lanes), embedding.dtype)], axis=0)
    marks = jnp.arange(blocks_here + 1, dtype=jnp.int32)
    marks = jnp.where(marks < blocks_here, marks, -1).astype(embedding.dtype)
    marks = jnp.broadcast_to(marks[:, None, None], (blocks_here + 1, 8, lanes))
    source_blocks = jnp.concatenate([narrow, marks], axis=1)
    picked = jnp.take(source_blocks, jnp.where(wanted >= 0, wanted, blocks_here), axis=0, mode="clip")
    arrived = lax.all_to_all(picked, "node", split_axis=0, concat_axis=0, tiled=True)
    table = arrived.reshape(node_count * slot_len, lanes)
    source = edge_ends // (blocks_here * block_rows)
    block_of = (edge_ends // block_rows) % blocks_here
    position = source * slot_len + (edge_ends % block_rows) * parts
    sent = arrived[:, block_len, 0].astype(jnp.int32)
    located = jnp.any((source[..., None] == jnp.arange(node_count, dtype=jnp.int32))
                      & (block_of[..., None] == sent), axis=-1)
    pair_ids = pair_index - node_self * PAIRS_ROW
    edge_score, pooled_sum = edge_scores(position, located, pair_ids, table, w_first, b_first, w_second)
    pair_cost = lax.psum_scatter(pooled_sum, "edge", scatter_dimension=0, tiled=True)
    return (edge_score, pair_cost)


def solution(mesh):
    return jax.shard_map(
        body,
        mesh=mesh,
        in_specs=(
            P("node", None, None),
            P("edge", "node", None),
            P(None, ("node", "edge")),
            P(("node", "edge")),
            P(),
            P(),
            P(),
        ),
        out_specs=(P(("node", "edge")), P(("node", "edge"))),
        check_vma=False,
    )
```

```python
import functools

import jax
import jax.numpy as jnp
from jax import lax
from jax.experimental import pallas as pl
from jax.experimental.pallas import tpu as pltpu
from jax.sharding import PartitionSpec as P

PAIRS_ROW = 1024
TILE = 256
LATE_TILE = 128
EARLY_ROWS = 96


def gelu_tanh(x):
    return x * (0.5 * (1.0 + jnp.tanh(0.7978845608028654 * (x + 0.044715 * (x * x * x)))))


def early_kernel(edges, pos_ref, table, mask_ref, wt_ref, wb_ref, part_ref, buf, wide, sems):
    step = pl.program_id(0)
    steps = pl.num_programs(0)
    parts = buf.shape[2] // TILE
    lanes = buf.shape[3]

    def fetch(tile, slot):
        base = tile * TILE

        def one(r, carry):
            dst = pl.ds(pl.multiple_of(r * parts, parts), parts)
            for end in range(2):
                src = pl.ds(pl.multiple_of(pos_ref[end * edges + base + r], parts), parts)
                pltpu.make_async_copy(table.at[src], buf.at[end, slot, dst], sems.at[end, slot]).start()
            return carry

        lax.fori_loop(0, TILE, one, 0, unroll=8)

    @pl.when(step == 0)
    def _():
        fetch(0, 0)

    slot = step % 2

    @pl.when(step + 1 < steps)
    def _():
        fetch(step + 1, 1 - slot)

    for end in range(2):
        pltpu.make_async_copy(table.at[pl.ds(0, TILE * parts)], buf.at[end, slot], sems.at[end, slot]).wait()

    mask = mask_ref[...]
    total = None
    for end, w_ref in ((0, wt_ref), (1, wb_ref)):
        wide[...] = buf[end, slot].astype(jnp.float32)
        keep = mask[:, end:end + 1] > 0
        for q in range(parts):
            piece = wide[pl.ds(q, TILE, stride=parts), :]
            piece = jnp.where(keep, piece, jnp.zeros_like(piece)).astype(jnp.bfloat16)
            term = jnp.dot(piece, w_ref[q * lanes:(q + 1) * lanes, :], preferred_element_type=jnp.float32)
            total = term if total is None else total + term
    part_ref[...] = total


def late_kernel(edges, pos_ref, table, mask_ref, part_ref, wt_ref, wb_ref, bias_ref, wo_ref, pid_ref,
                score_ref, pool_ref, buf, wide, sems):
    step = pl.program_id(0)
    parts = buf.shape[1] // LATE_TILE
    lanes = buf.shape[2]
    base = step * LATE_TILE

    @pl.when(step == 0)
    def _():
        pool_ref[...] = jnp.zeros_like(pool_ref)

    def copy(end, r):
        src = pl.ds(pl.multiple_of(jnp.maximum(pos_ref[end * edges + base + r], 0), parts), parts)
        dst = pl.ds(pl.multiple_of(r * parts, parts), parts)
        return pltpu.make_async_copy(table.at[src], buf.at[end, dst], sems.at[end, r])

    def start(r, carry):
        for end in range(2):
            @pl.when(pos_ref[end * edges + base + r] >= 0)
            def _():
                copy(end, r).start()
        return carry

    def finish(r, carry):
        for end in range(2):
            @pl.when(pos_ref[end * edges + base + r] >= 0)
            def _():
                copy(end, r).wait()
        return carry

    lax.fori_loop(0, LATE_TILE, start, 0, unroll=8)
    lax.fori_loop(0, LATE_TILE, finish, 0, unroll=8)

    mask = mask_ref[...]
    preact = part_ref[...]
    for end, w_ref in ((0, wt_ref), (1, wb_ref)):
        wide[...] = buf[end].astype(jnp.float32)
        keep = mask[:, end:end + 1] > 0
        for q in range(parts):
            piece = wide[pl.ds(q, LATE_TILE, stride=parts), :]
            piece = jnp.where(keep, piece, jnp.zeros_like(piece)).astype(jnp.bfloat16)
            preact = preact + jnp.dot(piece, w_ref[q * lanes:(q + 1) * lanes, :],
                                      preferred_element_type=jnp.float32)
    hidden = gelu_tanh(preact + bias_ref[...])
    scores = jnp.sum(hidden * wo_ref[0:1, :], axis=1, keepdims=True)
    score_ref[...] = scores
    pair_range = lax.broadcasted_iota(jnp.int32, (LATE_TILE, PAIRS_ROW), 1)
    picked = jnp.where(pid_ref[...] == pair_range, scores, 0.0)
    pool_ref[...] += jnp.sum(picked, axis=0, keepdims=True)


def early_products(position, mask, table, w_first):
    edges = position.shape[1]
    lanes = table.shape[1]
    width = w_first.shape[0] // 2
    parts = width // lanes
    hid = w_first.shape[1]
    grid_spec = pltpu.PrefetchScalarGridSpec(
        num_scalar_prefetch=1,
        grid=(edges // TILE,),
        in_specs=[
            pl.BlockSpec(memory_space=pl.ANY),
            pl.BlockSpec((TILE, 2), lambda i, p: (i, 0)),
            pl.BlockSpec((width, hid), lambda i, p: (0, 0)),
            pl.BlockSpec((width, hid), lambda i, p: (1, 0)),
        ],
        out_specs=pl.BlockSpec((TILE, hid), lambda i, p: (i, 0)),
        scratch_shapes=[
            pltpu.VMEM((2, 2, TILE * parts, lanes), table.dtype),
            pltpu.VMEM((TILE * parts, lanes), jnp.float32),
            pltpu.SemaphoreType.DMA((2, 2)),
        ],
    )
    return pl.pallas_call(
        functools.partial(early_kernel, edges),
        grid_spec=grid_spec,
        out_shape=jax.ShapeDtypeStruct((edges, hid), jnp.float32),
        compiler_params=pltpu.CompilerParams(dimension_semantics=("arbitrary",)),
        cost_estimate=pl.CostEstimate(
            flops=2 * edges * 2 * width * hid, transcendentals=0,
            bytes_accessed=2 * edges * width * table.dtype.itemsize + edges * hid * 4),
    )(position.reshape(2 * edges), table, mask, w_first, w_first)


def late_scores(position, mask, partial, pair_ids, table, w_first, b_first, w_second):
    edges = position.shape[1]
    lanes = table.shape[1]
    width = w_first.shape[0] // 2
    parts = width // lanes
    hid = w_first.shape[1]
    wo8 = jnp.broadcast_to(w_second.astype(jnp.float32)[None, :], (8, hid))
    grid_spec = pltpu.PrefetchScalarGridSpec(
        num_scalar_prefetch=1,
        grid=(edges // LATE_TILE,),
        in_specs=[
            pl.BlockSpec(memory_space=pl.ANY),
            pl.BlockSpec((LATE_TILE, 2), lambda i, p: (i, 0)),
            pl.BlockSpec((LATE_TILE, hid), lambda i, p: (i, 0)),
            pl.BlockSpec((width, hid), lambda i, p: (0, 0)),
            pl.BlockSpec((width, hid), lambda i, p: (1, 0)),
            pl.BlockSpec((1, hid), lambda i, p: (0, 0)),
            pl.BlockSpec((8, hid), lambda i, p: (0, 0)),
            pl.BlockSpec((LATE_TILE, 1), lambda i, p: (i, 0)),
        ],
        out_specs=[
            pl.BlockSpec((LATE_TILE, 1), lambda i, p: (i, 0)),
            pl.BlockSpec((1, PAIRS_ROW), lambda i, p: (0, 0)),
        ],
        scratch_shapes=[
            pltpu.VMEM((2, LATE_TILE * parts, lanes), table.dtype),
            pltpu.VMEM((LATE_TILE * parts, lanes), jnp.float32),
            pltpu.SemaphoreType.DMA((2, LATE_TILE)),
        ],
    )
    scores, pooled = pl.pallas_call(
        functools.partial(late_kernel, edges),
        grid_spec=grid_spec,
        out_shape=[
            jax.ShapeDtypeStruct((edges, 1), jnp.float32),
            jax.ShapeDtypeStruct((1, PAIRS_ROW), jnp.float32),
        ],
        compiler_params=pltpu.CompilerParams(dimension_semantics=("arbitrary",)),
        cost_estimate=pl.CostEstimate(
            flops=2 * edges * 2 * width * hid, transcendentals=edges * hid,
            bytes_accessed=edges * width * table.dtype.itemsize + edges * hid * 4),
    )(position.reshape(2 * edges), table, mask, partial, w_first, w_first, b_first.reshape(1, hid), wo8,
      pair_ids.reshape(edges, 1))
    return scores.reshape(edges), pooled.reshape(PAIRS_ROW)


def body(embedding, send_list, edge_ends, pair_index, w_first, b_first, w_second):
    node_count = lax.axis_size("node")
    node_self = lax.axis_index("node")
    blocks_here = embedding.shape[0]
    block_rows = embedding.shape[1]
    feature_width = embedding.shape[2]
    lanes = 128
    parts = feature_width // lanes
    early_len = EARLY_ROWS * parts
    late_len = (block_rows - EARLY_ROWS) * parts
    slot_len = early_len + 8
    wanted = send_list[0, 0]
    pick = jnp.where(wanted >= 0, wanted, blocks_here)
    narrow = embedding.reshape(blocks_here, block_rows * parts, lanes)
    narrow = jnp.concatenate([narrow, jnp.zeros((1, block_rows * parts, lanes), embedding.dtype)], axis=0)
    marks = jnp.arange(blocks_here + 1, dtype=jnp.int32)
    marks = jnp.where(marks < blocks_here, marks, -1).astype(embedding.dtype)
    marks = jnp.broadcast_to(marks[:, None, None], (blocks_here + 1, 8, lanes))
    early_source = jnp.concatenate([narrow[:, :early_len], marks], axis=1)
    late_source = narrow[:, early_len:]
    early_picked = jnp.take(early_source, pick, axis=0, mode="clip")
    late_picked = jnp.take(late_source, pick, axis=0, mode="clip")
    early_arrived = lax.all_to_all(early_picked, "node", split_axis=0, concat_axis=0, tiled=True)
    late_picked, early_arrived = lax.optimization_barrier((late_picked, early_arrived))
    late_arrived = lax.all_to_all(late_picked, "node", split_axis=0, concat_axis=0, tiled=True)
    early_table = early_arrived.reshape(node_count * slot_len, lanes)
    late_table = late_arrived.reshape(node_count * late_len, lanes)
    source = edge_ends // (blocks_here * block_rows)
    block_of = (edge_ends // block_rows) % blocks_here
    within = edge_ends % block_rows
    early = within < EARLY_ROWS
    early_position = source * slot_len + jnp.where(early, within, 0) * parts
    late_position = jnp.where(early, -1, source * late_len + (within - EARLY_ROWS) * parts)
    sent = early_arrived[:, early_len, 0].astype(jnp.int32)
    located = jnp.any((source[..., None] == jnp.arange(node_count, dtype=jnp.int32))
                      & (block_of[..., None] == sent), axis=-1)
    early_mask = (located & early).T.astype(jnp.float32)
    late_mask = (located & ~early).T.astype(jnp.float32)
    partial = early_products(early_position, early_mask, early_table, w_first)
    pair_ids = pair_index - node_self * PAIRS_ROW
    edge_score, pooled_sum = late_scores(late_position, late_mask, partial, pair_ids, late_table,
                                         w_first, b_first, w_second)
    pair_cost = lax.psum_scatter(pooled_sum, "edge", scatter_dimension=0, tiled=True)
    return (edge_score, pair_cost)


def solution(mesh):
    return jax.shard_map(
        body,
        mesh=mesh,
        in_specs=(
            P("node", None, None),
            P("edge", "node", None),
            P(None, ("node", "edge")),
            P(("node", "edge")),
            P(),
            P(),
            P(),
        ),
        out_specs=(P(("node", "edge")), P(("node", "edge"))),
        check_vma=False,
    )
```

```python
import functools

import jax
import jax.numpy as jnp
from jax import lax
from jax.experimental import pallas as pl
from jax.experimental.pallas import tpu as pltpu
from jax.sharding import PartitionSpec as P

PAIRS_ROW = 1024
TILE = 256
LATE_TILE = 256
EARLY_ROWS = 96


def gelu_tanh(x):
    return x * (0.5 * (1.0 + jnp.tanh(0.7978845608028654 * (x + 0.044715 * (x * x * x)))))


def early_kernel(edges, pos_ref, table, mask_ref, wt_ref, wb_ref, part_ref, buf, wide, sems):
    step = pl.program_id(0)
    steps = pl.num_programs(0)
    parts = buf.shape[2] // TILE
    lanes = buf.shape[3]

    def fetch(tile, slot):
        base = tile * TILE

        def one(r, carry):
            dst = pl.ds(pl.multiple_of(r * parts, parts), parts)
            for end in range(2):
                src = pl.ds(pl.multiple_of(pos_ref[end * edges + base + r], parts), parts)
                pltpu.make_async_copy(table.at[src], buf.at[end, slot, dst], sems.at[end, slot]).start()
            return carry

        lax.fori_loop(0, TILE, one, 0, unroll=8)

    @pl.when(step == 0)
    def _():
        fetch(0, 0)

    slot = step % 2

    @pl.when(step + 1 < steps)
    def _():
        fetch(step + 1, 1 - slot)

    for end in range(2):
        pltpu.make_async_copy(table.at[pl.ds(0, TILE * parts)], buf.at[end, slot], sems.at[end, slot]).wait()

    mask = mask_ref[...]
    total = None
    for end, w_ref in ((0, wt_ref), (1, wb_ref)):
        wide[...] = buf[end, slot].astype(jnp.float32)
        keep = mask[:, end:end + 1] > 0
        for q in range(parts):
            piece = wide[pl.ds(q, TILE, stride=parts), :]
            piece = jnp.where(keep, piece, jnp.zeros_like(piece)).astype(jnp.bfloat16)
            term = jnp.dot(piece, w_ref[q * lanes:(q + 1) * lanes, :], preferred_element_type=jnp.float32)
            total = term if total is None else total + term
    part_ref[...] = total


def late_kernel(idx_ref, part_ref, table_ref, wt_ref, wb_ref, bias_ref, wo_ref, pid_ref, score_ref, pool_ref):
    step = pl.program_id(0)

    @pl.when(step == 0)
    def _():
        pool_ref[...] = jnp.zeros_like(pool_ref)

    idx = idx_ref[...]
    rows = table_ref.shape[0]
    slots = lax.broadcasted_iota(jnp.int32, (LATE_TILE, rows), 1)
    preact = part_ref[...]
    for end, w_ref in ((0, wt_ref), (1, wb_ref)):
        onehot = (idx[:, end:end + 1] == slots).astype(table_ref.dtype)
        picked = jnp.dot(onehot, table_ref[...], preferred_element_type=jnp.float32).astype(table_ref.dtype)
        preact = preact + jnp.dot(picked, w_ref[...], preferred_element_type=jnp.float32)
    hidden = gelu_tanh(preact + bias_ref[...])
    scores = jnp.sum(hidden * wo_ref[0:1, :], axis=1, keepdims=True)
    score_ref[...] = scores
    pair_range = lax.broadcasted_iota(jnp.int32, (LATE_TILE, PAIRS_ROW), 1)
    pooled = jnp.where(pid_ref[...] == pair_range, scores, 0.0)
    pool_ref[...] += jnp.sum(pooled, axis=0, keepdims=True)


def early_products(position, mask, table, w_first):
    edges = position.shape[1]
    lanes = table.shape[1]
    width = w_first.shape[0] // 2
    parts = width // lanes
    hid = w_first.shape[1]
    grid_spec = pltpu.PrefetchScalarGridSpec(
        num_scalar_prefetch=1,
        grid=(edges // TILE,),
        in_specs=[
            pl.BlockSpec(memory_space=pl.ANY),
            pl.BlockSpec((TILE, 2), lambda i, p: (i, 0)),
            pl.BlockSpec((width, hid), lambda i, p: (0, 0)),
            pl.BlockSpec((width, hid), lambda i, p: (1, 0)),
        ],
        out_specs=pl.BlockSpec((TILE, hid), lambda i, p: (i, 0)),
        scratch_shapes=[
            pltpu.VMEM((2, 2, TILE * parts, lanes), table.dtype),
            pltpu.VMEM((TILE * parts, lanes), jnp.float32),
            pltpu.SemaphoreType.DMA((2, 2)),
        ],
    )
    return pl.pallas_call(
        functools.partial(early_kernel, edges),
        grid_spec=grid_spec,
        out_shape=jax.ShapeDtypeStruct((edges, hid), jnp.float32),
        compiler_params=pltpu.CompilerParams(dimension_semantics=("arbitrary",)),
        cost_estimate=pl.CostEstimate(
            flops=2 * edges * 2 * width * hid, transcendentals=0,
            bytes_accessed=2 * edges * width * table.dtype.itemsize + edges * hid * 4),
    )(position.reshape(2 * edges), table, mask, w_first, w_first)


def late_scores(late_index, partial, pair_ids, table, w_first, b_first, w_second):
    edges = late_index.shape[1]
    rows, width = table.shape
    hid = w_first.shape[1]
    wo8 = jnp.broadcast_to(w_second.astype(jnp.float32)[None, :], (8, hid))
    scores, pooled = pl.pallas_call(
        late_kernel,
        grid=(edges // LATE_TILE,),
        in_specs=[
            pl.BlockSpec((LATE_TILE, 2), lambda i: (i, 0)),
            pl.BlockSpec((LATE_TILE, hid), lambda i: (i, 0)),
            pl.BlockSpec((rows, width), lambda i: (0, 0)),
            pl.BlockSpec((width, hid), lambda i: (0, 0)),
            pl.BlockSpec((width, hid), lambda i: (1, 0)),
            pl.BlockSpec((1, hid), lambda i: (0, 0)),
            pl.BlockSpec((8, hid), lambda i: (0, 0)),
            pl.BlockSpec((LATE_TILE, 1), lambda i: (i, 0)),
        ],
        out_specs=[
            pl.BlockSpec((LATE_TILE, 1), lambda i: (i, 0)),
            pl.BlockSpec((1, PAIRS_ROW), lambda i: (0, 0)),
        ],
        out_shape=[
            jax.ShapeDtypeStruct((edges, 1), jnp.float32),
            jax.ShapeDtypeStruct((1, PAIRS_ROW), jnp.float32),
        ],
        compiler_params=pltpu.CompilerParams(dimension_semantics=("arbitrary",)),
        cost_estimate=pl.CostEstimate(
            flops=2 * edges * 2 * (rows + hid) * width, transcendentals=edges * hid,
            bytes_accessed=rows * width * 2 + edges * hid * 4),
    )(late_index.T, partial, table, w_first, w_first, b_first.reshape(1, hid), wo8, pair_ids.reshape(edges, 1))
    return scores.reshape(edges), pooled.reshape(PAIRS_ROW)


def body(embedding, send_list, edge_ends, pair_index, w_first, b_first, w_second):
    node_count = lax.axis_size("node")
    node_self = lax.axis_index("node")
    blocks_here = embedding.shape[0]
    block_rows = embedding.shape[1]
    feature_width = embedding.shape[2]
    lanes = 128
    parts = feature_width // lanes
    early_len = EARLY_ROWS * parts
    slot_len = early_len + 8
    wanted = send_list[0, 0]
    pick = jnp.where(wanted >= 0, wanted, blocks_here)
    narrow = embedding.reshape(blocks_here, block_rows * parts, lanes)
    narrow = jnp.concatenate([narrow, jnp.zeros((1, block_rows * parts, lanes), embedding.dtype)], axis=0)
    marks = jnp.arange(blocks_here + 1, dtype=jnp.int32)
    marks = jnp.where(marks < blocks_here, marks, -1).astype(embedding.dtype)
    marks = jnp.broadcast_to(marks[:, None, None], (blocks_here + 1, 8, lanes))
    early_source = jnp.concatenate([narrow[:, :early_len], marks], axis=1)
    late_rows = block_rows - EARLY_ROWS
    late_source = jnp.concatenate([embedding[:, EARLY_ROWS:], jnp.zeros((1, late_rows, feature_width), embedding.dtype)], axis=0)
    early_picked = jnp.take(early_source, pick, axis=0, mode="clip")
    late_picked = jnp.take(late_source, pick, axis=0, mode="clip")
    early_arrived = lax.all_to_all(early_picked, "node", split_axis=0, concat_axis=0, tiled=True)
    late_picked, early_arrived = lax.optimization_barrier((late_picked, early_arrived))
    late_arrived = lax.all_to_all(late_picked, "node", split_axis=0, concat_axis=0, tiled=True)
    early_table = early_arrived.reshape(node_count * slot_len, lanes)
    late_table = late_arrived.reshape(node_count * late_rows, feature_width)
    source = edge_ends // (blocks_here * block_rows)
    block_of = (edge_ends // block_rows) % blocks_here
    within = edge_ends % block_rows
    early = within < EARLY_ROWS
    early_position = source * slot_len + jnp.where(early, within, 0) * parts
    sent = early_arrived[:, early_len, 0].astype(jnp.int32)
    located = jnp.any((source[..., None] == jnp.arange(node_count, dtype=jnp.int32))
                      & (block_of[..., None] == sent), axis=-1)
    early_mask = (located & early).T.astype(jnp.float32)
    late_index = jnp.where(located & ~early, source * late_rows + within - EARLY_ROWS, -1)
    partial = early_products(early_position, early_mask, early_table, w_first)
    pair_ids = pair_index - node_self * PAIRS_ROW
    edge_score, pooled_sum = late_scores(late_index, partial, pair_ids, late_table, w_first, b_first, w_second)
    pair_cost = lax.psum_scatter(pooled_sum, "edge", scatter_dimension=0, tiled=True)
    return (edge_score, pair_cost)


def solution(mesh):
    return jax.shard_map(
        body,
        mesh=mesh,
        in_specs=(
            P("node", None, None),
            P("edge", "node", None),
            P(None, ("node", "edge")),
            P(("node", "edge")),
            P(),
            P(),
            P(),
        ),
        out_specs=(P(("node", "edge")), P(("node", "edge"))),
        check_vma=False,
    )
```

```python
import functools

import jax
import jax.numpy as jnp
from jax import lax
from jax.experimental import pallas as pl
from jax.experimental.pallas import tpu as pltpu
from jax.sharding import PartitionSpec as P

PAIRS_ROW = 1024
TILE = 256
LATE_TILE = 256
EARLY_ROWS = 96


def gelu_tanh(x):
    return x * (0.5 * (1.0 + jnp.tanh(0.7978845608028654 * (x + 0.044715 * (x * x * x)))))


def early_kernel(edges, pos_ref, table, mask_ref, wt_ref, wb_ref, part_ref, buf, wide, sems):
    step = pl.program_id(0)
    steps = pl.num_programs(0)
    parts = buf.shape[2] // TILE
    lanes = buf.shape[3]

    def fetch(tile, slot):
        base = tile * TILE

        def one(r, carry):
            dst = pl.ds(pl.multiple_of(r * parts, parts), parts)
            for end in range(2):
                src = pl.ds(pl.multiple_of(pos_ref[end * edges + base + r], parts), parts)
                pltpu.make_async_copy(table.at[src], buf.at[end, slot, dst], sems.at[end, slot]).start()
            return carry

        lax.fori_loop(0, TILE, one, 0, unroll=8)

    @pl.when(step == 0)
    def _():
        fetch(0, 0)

    slot = step % 2

    @pl.when(step + 1 < steps)
    def _():
        fetch(step + 1, 1 - slot)

    for end in range(2):
        pltpu.make_async_copy(table.at[pl.ds(0, TILE * parts)], buf.at[end, slot], sems.at[end, slot]).wait()

    mask = mask_ref[...]
    total = None
    for end, w_ref in ((0, wt_ref), (1, wb_ref)):
        wide[...] = buf[end, slot].astype(jnp.float32)
        keep = mask[:, end:end + 1] > 0
        for q in range(parts):
            piece = wide[pl.ds(q, TILE, stride=parts), :]
            piece = jnp.where(keep, piece, jnp.zeros_like(piece)).astype(jnp.bfloat16)
            term = jnp.dot(piece, w_ref[q * lanes:(q + 1) * lanes, :], preferred_element_type=jnp.float32)
            total = term if total is None else total + term
    part_ref[...] = total


def late_kernel(idx_ref, part_ref, table_ref, wt_ref, wb_ref, bias_ref, wo_ref, pid_ref, score_ref, pool_ref):
    step = pl.program_id(0)

    @pl.when(step == 0)
    def _():
        pool_ref[...] = jnp.zeros_like(pool_ref)

    idx = idx_ref[...]
    rows = table_ref.shape[0]
    slots = lax.broadcasted_iota(jnp.int32, (LATE_TILE, rows), 1)
    preact = part_ref[...]
    for end, w_ref in ((0, wt_ref), (1, wb_ref)):
        onehot = (idx[:, end:end + 1] == slots).astype(table_ref.dtype)
        picked = jnp.dot(onehot, table_ref[...], preferred_element_type=jnp.float32).astype(table_ref.dtype)
        preact = preact + jnp.dot(picked, w_ref[...], preferred_element_type=jnp.float32)
    hidden = gelu_tanh(preact + bias_ref[...])
    scores = jnp.sum(hidden * wo_ref[0:1, :], axis=1, keepdims=True)
    score_ref[...] = scores
    pair_range = lax.broadcasted_iota(jnp.int32, (LATE_TILE, PAIRS_ROW), 1)
    pooled = jnp.where(pid_ref[...] == pair_range, scores, 0.0)
    pool_ref[...] += jnp.sum(pooled, axis=0, keepdims=True)


def exchange_kernel(src_ref, dst_ref, send_sems, recv_sems, own_sem):
    count = src_ref.shape[0]
    me = lax.axis_index("node")
    lane = lax.axis_index("edge")
    barrier = pltpu.get_barrier_semaphore()

    def greet(k, carry):
        pl.semaphore_signal(barrier, 1, device_id=((me + k) % count, lane), device_id_type=pl.DeviceIdType.MESH)
        return carry

    lax.fori_loop(1, count, greet, 0)
    pl.semaphore_wait(barrier, count - 1)
    own = pltpu.make_async_copy(src_ref.at[me], dst_ref.at[me], own_sem)
    own.start()

    def remote(target, slot):
        return pltpu.make_async_remote_copy(
            src_ref.at[target], dst_ref.at[slot], send_sems.at[target], recv_sems.at[slot],
            device_id=(target, lane), device_id_type=pl.DeviceIdType.MESH)

    def send(k, carry):
        remote((me + k) % count, me).start()
        return carry

    lax.fori_loop(1, count, send, 0)

    def finish(k, carry):
        remote((me + k) % count, me).wait_send()
        source = (me + count - k) % count
        remote(source, source).wait_recv()
        return carry

    lax.fori_loop(1, count, finish, 0)
    own.wait()


def exchange(picked):
    count = picked.shape[0]
    return pl.pallas_call(
        exchange_kernel,
        in_specs=[pl.BlockSpec(memory_space=pl.ANY)],
        out_specs=pl.BlockSpec(memory_space=pl.ANY),
        out_shape=jax.ShapeDtypeStruct(picked.shape, picked.dtype),
        scratch_shapes=[
            pltpu.SemaphoreType.DMA((count,)),
            pltpu.SemaphoreType.DMA((count,)),
            pltpu.SemaphoreType.DMA(()),
        ],
        compiler_params=pltpu.CompilerParams(collective_id=0, has_side_effects=True),
    )(picked)


def early_products(position, mask, table, w_first):
    edges = position.shape[1]
    lanes = table.shape[1]
    width = w_first.shape[0] // 2
    parts = width // lanes
    hid = w_first.shape[1]
    grid_spec = pltpu.PrefetchScalarGridSpec(
        num_scalar_prefetch=1,
        grid=(edges // TILE,),
        in_specs=[
            pl.BlockSpec(memory_space=pl.ANY),
            pl.BlockSpec((TILE, 2), lambda i, p: (i, 0)),
            pl.BlockSpec((width, hid), lambda i, p: (0, 0)),
            pl.BlockSpec((width, hid), lambda i, p: (1, 0)),
        ],
        out_specs=pl.BlockSpec((TILE, hid), lambda i, p: (i, 0)),
        scratch_shapes=[
            pltpu.VMEM((2, 2, TILE * parts, lanes), table.dtype),
            pltpu.VMEM((TILE * parts, lanes), jnp.float32),
            pltpu.SemaphoreType.DMA((2, 2)),
        ],
    )
    return pl.pallas_call(
        functools.partial(early_kernel, edges),
        grid_spec=grid_spec,
        out_shape=jax.ShapeDtypeStruct((edges, hid), jnp.float32),
        compiler_params=pltpu.CompilerParams(dimension_semantics=("arbitrary",)),
        cost_estimate=pl.CostEstimate(
            flops=2 * edges * 2 * width * hid, transcendentals=0,
            bytes_accessed=2 * edges * width * table.dtype.itemsize + edges * hid * 4),
    )(position.reshape(2 * edges), table, mask, w_first, w_first)


def late_scores(late_index, partial, pair_ids, table, w_first, b_first, w_second):
    edges = late_index.shape[1]
    rows, width = table.shape
    hid = w_first.shape[1]
    wo8 = jnp.broadcast_to(w_second.astype(jnp.float32)[None, :], (8, hid))
    scores, pooled = pl.pallas_call(
        late_kernel,
        grid=(edges // LATE_TILE,),
        in_specs=[
            pl.BlockSpec((LATE_TILE, 2), lambda i: (i, 0)),
            pl.BlockSpec((LATE_TILE, hid), lambda i: (i, 0)),
            pl.BlockSpec((rows, width), lambda i: (0, 0)),
            pl.BlockSpec((width, hid), lambda i: (0, 0)),
            pl.BlockSpec((width, hid), lambda i: (1, 0)),
            pl.BlockSpec((1, hid), lambda i: (0, 0)),
            pl.BlockSpec((8, hid), lambda i: (0, 0)),
            pl.BlockSpec((LATE_TILE, 1), lambda i: (i, 0)),
        ],
        out_specs=[
            pl.BlockSpec((LATE_TILE, 1), lambda i: (i, 0)),
            pl.BlockSpec((1, PAIRS_ROW), lambda i: (0, 0)),
        ],
        out_shape=[
            jax.ShapeDtypeStruct((edges, 1), jnp.float32),
            jax.ShapeDtypeStruct((1, PAIRS_ROW), jnp.float32),
        ],
        compiler_params=pltpu.CompilerParams(dimension_semantics=("arbitrary",)),
        cost_estimate=pl.CostEstimate(
            flops=2 * edges * 2 * (rows + hid) * width, transcendentals=edges * hid,
            bytes_accessed=rows * width * 2 + edges * hid * 4),
    )(late_index.T, partial, table, w_first, w_first, b_first.reshape(1, hid), wo8, pair_ids.reshape(edges, 1))
    return scores.reshape(edges), pooled.reshape(PAIRS_ROW)


def body(embedding, send_list, edge_ends, pair_index, w_first, b_first, w_second):
    node_count = lax.axis_size("node")
    node_self = lax.axis_index("node")
    blocks_here = embedding.shape[0]
    block_rows = embedding.shape[1]
    feature_width = embedding.shape[2]
    lanes = 128
    parts = feature_width // lanes
    early_len = EARLY_ROWS * parts
    slot_len = early_len + 8
    wanted = send_list[0, 0]
    pick = jnp.where(wanted >= 0, wanted, blocks_here)
    narrow = embedding.reshape(blocks_here, block_rows * parts, lanes)
    narrow = jnp.concatenate([narrow, jnp.zeros((1, block_rows * parts, lanes), embedding.dtype)], axis=0)
    marks = jnp.arange(blocks_here + 1, dtype=jnp.int32)
    marks = jnp.where(marks < blocks_here, marks, -1).astype(embedding.dtype)
    marks = jnp.broadcast_to(marks[:, None, None], (blocks_here + 1, 8, lanes))
    early_source = jnp.concatenate([narrow[:, :early_len], marks], axis=1)
    late_rows = block_rows - EARLY_ROWS
    late_source = jnp.concatenate([embedding[:, EARLY_ROWS:], jnp.zeros((1, late_rows, feature_width), embedding.dtype)], axis=0)
    early_picked = jnp.take(early_source, pick, axis=0, mode="clip")
    late_picked = jnp.take(late_source, pick, axis=0, mode="clip")
    early_arrived = exchange(early_picked)
    late_picked, early_arrived = lax.optimization_barrier((late_picked, early_arrived))
    late_arrived = lax.all_to_all(late_picked, "node", split_axis=0, concat_axis=0, tiled=True)
    early_table = early_arrived.reshape(node_count * slot_len, lanes)
    late_table = late_arrived.reshape(node_count * late_rows, feature_width)
    source = edge_ends // (blocks_here * block_rows)
    block_of = (edge_ends // block_rows) % blocks_here
    within = edge_ends % block_rows
    early = within < EARLY_ROWS
    early_position = source * slot_len + jnp.where(early, within, 0) * parts
    sent = early_arrived[:, early_len, 0].astype(jnp.int32)
    located = jnp.any((source[..., None] == jnp.arange(node_count, dtype=jnp.int32))
                      & (block_of[..., None] == sent), axis=-1)
    early_mask = (located & early).T.astype(jnp.float32)
    late_index = jnp.where(located & ~early, source * late_rows + within - EARLY_ROWS, -1)
    partial = early_products(early_position, early_mask, early_table, w_first)
    pair_ids = pair_index - node_self * PAIRS_ROW
    edge_score, pooled_sum = late_scores(late_index, partial, pair_ids, late_table, w_first, b_first, w_second)
    pair_cost = lax.psum_scatter(pooled_sum, "edge", scatter_dimension=0, tiled=True)
    return (edge_score, pair_cost)


def solution(mesh):
    return jax.shard_map(
        body,
        mesh=mesh,
        in_specs=(
            P("node", None, None),
            P("edge", "node", None),
            P(None, ("node", "edge")),
            P(("node", "edge")),
            P(),
            P(),
            P(),
        ),
        out_specs=(P(("node", "edge")), P(("node", "edge"))),
        check_vma=False,
    )
```

```python
import functools

import jax
import jax.numpy as jnp
from jax import lax
from jax.experimental import pallas as pl
from jax.experimental.pallas import tpu as pltpu
from jax.sharding import PartitionSpec as P

PAIRS_ROW = 1024
TILE = 256
LATE_TILE = 256
EARLY_ROWS = 88


def gelu_tanh(x):
    return x * (0.5 * (1.0 + jnp.tanh(0.7978845608028654 * (x + 0.044715 * (x * x * x)))))


def early_kernel(edges, pos_ref, table, mask_ref, wt_ref, wb_ref, part_ref, buf, wide, sems):
    step = pl.program_id(0)
    steps = pl.num_programs(0)
    parts = buf.shape[2] // TILE
    lanes = buf.shape[3]

    def fetch(tile, slot):
        base = tile * TILE

        def one(r, carry):
            dst = pl.ds(pl.multiple_of(r * parts, parts), parts)
            for end in range(2):
                src = pl.ds(pl.multiple_of(pos_ref[end * edges + base + r], parts), parts)
                pltpu.make_async_copy(table.at[src], buf.at[end, slot, dst], sems.at[end, slot]).start()
            return carry

        lax.fori_loop(0, TILE, one, 0, unroll=8)

    @pl.when(step == 0)
    def _():
        fetch(0, 0)

    slot = step % 2

    @pl.when(step + 1 < steps)
    def _():
        fetch(step + 1, 1 - slot)

    for end in range(2):
        pltpu.make_async_copy(table.at[pl.ds(0, TILE * parts)], buf.at[end, slot], sems.at[end, slot]).wait()

    mask = mask_ref[...]
    total = None
    for end, w_ref in ((0, wt_ref), (1, wb_ref)):
        wide[...] = buf[end, slot].astype(jnp.float32)
        keep = mask[:, end:end + 1] > 0
        for q in range(parts):
            piece = wide[pl.ds(q, TILE, stride=parts), :]
            piece = jnp.where(keep, piece, jnp.zeros_like(piece)).astype(jnp.bfloat16)
            term = jnp.dot(piece, w_ref[q * lanes:(q + 1) * lanes, :], preferred_element_type=jnp.float32)
            total = term if total is None else total + term
    part_ref[...] = total


def late_kernel(idx_ref, part_ref, table_ref, wt_ref, wb_ref, bias_ref, wo_ref, pid_ref, score_ref, pool_ref):
    step = pl.program_id(0)

    @pl.when(step == 0)
    def _():
        pool_ref[...] = jnp.zeros_like(pool_ref)

    idx = idx_ref[...]
    rows = table_ref.shape[0]
    slots = lax.broadcasted_iota(jnp.int32, (LATE_TILE, rows), 1)
    preact = part_ref[...]
    for end, w_ref in ((0, wt_ref), (1, wb_ref)):
        onehot = (idx[:, end:end + 1] == slots).astype(table_ref.dtype)
        picked = jnp.dot(onehot, table_ref[...], preferred_element_type=jnp.float32).astype(table_ref.dtype)
        preact = preact + jnp.dot(picked, w_ref[...], preferred_element_type=jnp.float32)
    hidden = gelu_tanh(preact + bias_ref[...])
    scores = jnp.sum(hidden * wo_ref[0:1, :], axis=1, keepdims=True)
    score_ref[...] = scores
    pair_range = lax.broadcasted_iota(jnp.int32, (LATE_TILE, PAIRS_ROW), 1)
    pooled = jnp.where(pid_ref[...] == pair_range, scores, 0.0)
    pool_ref[...] += jnp.sum(pooled, axis=0, keepdims=True)


def early_products(position, mask, table, w_first):
    edges = position.shape[1]
    lanes = table.shape[1]
    width = w_first.shape[0] // 2
    parts = width // lanes
    hid = w_first.shape[1]
    grid_spec = pltpu.PrefetchScalarGridSpec(
        num_scalar_prefetch=1,
        grid=(edges // TILE,),
        in_specs=[
            pl.BlockSpec(memory_space=pl.ANY),
            pl.BlockSpec((TILE, 2), lambda i, p: (i, 0)),
            pl.BlockSpec((width, hid), lambda i, p: (0, 0)),
            pl.BlockSpec((width, hid), lambda i, p: (1, 0)),
        ],
        out_specs=pl.BlockSpec((TILE, hid), lambda i, p: (i, 0)),
        scratch_shapes=[
            pltpu.VMEM((2, 2, TILE * parts, lanes), table.dtype),
            pltpu.VMEM((TILE * parts, lanes), jnp.float32),
            pltpu.SemaphoreType.DMA((2, 2)),
        ],
    )
    return pl.pallas_call(
        functools.partial(early_kernel, edges),
        grid_spec=grid_spec,
        out_shape=jax.ShapeDtypeStruct((edges, hid), jnp.float32),
        compiler_params=pltpu.CompilerParams(dimension_semantics=("arbitrary",)),
        cost_estimate=pl.CostEstimate(
            flops=2 * edges * 2 * width * hid, transcendentals=0,
            bytes_accessed=2 * edges * width * table.dtype.itemsize + edges * hid * 4),
    )(position.reshape(2 * edges), table, mask, w_first, w_first)


def late_scores(late_index, partial, pair_ids, table, w_first, b_first, w_second):
    edges = late_index.shape[1]
    rows, width = table.shape
    hid = w_first.shape[1]
    wo8 = jnp.broadcast_to(w_second.astype(jnp.float32)[None, :], (8, hid))
    scores, pooled = pl.pallas_call(
        late_kernel,
        grid=(edges // LATE_TILE,),
        in_specs=[
            pl.BlockSpec((LATE_TILE, 2), lambda i: (i, 0)),
            pl.BlockSpec((LATE_TILE, hid), lambda i: (i, 0)),
            pl.BlockSpec((rows, width), lambda i: (0, 0)),
            pl.BlockSpec((width, hid), lambda i: (0, 0)),
            pl.BlockSpec((width, hid), lambda i: (1, 0)),
            pl.BlockSpec((1, hid), lambda i: (0, 0)),
            pl.BlockSpec((8, hid), lambda i: (0, 0)),
            pl.BlockSpec((LATE_TILE, 1), lambda i: (i, 0)),
        ],
        out_specs=[
            pl.BlockSpec((LATE_TILE, 1), lambda i: (i, 0)),
            pl.BlockSpec((1, PAIRS_ROW), lambda i: (0, 0)),
        ],
        out_shape=[
            jax.ShapeDtypeStruct((edges, 1), jnp.float32),
            jax.ShapeDtypeStruct((1, PAIRS_ROW), jnp.float32),
        ],
        compiler_params=pltpu.CompilerParams(dimension_semantics=("arbitrary",)),
        cost_estimate=pl.CostEstimate(
            flops=2 * edges * 2 * (rows + hid) * width, transcendentals=edges * hid,
            bytes_accessed=rows * width * 2 + edges * hid * 4),
    )(late_index.T, partial, table, w_first, w_first, b_first.reshape(1, hid), wo8, pair_ids.reshape(edges, 1))
    return scores.reshape(edges), pooled.reshape(PAIRS_ROW)


def scatter_kernel(part_ref, out_ref, recv, send_sems, recv_sems):
    count = part_ref.shape[0]
    me = lax.axis_index("edge")
    node = lax.axis_index("node")
    barrier = pltpu.get_barrier_semaphore()

    def greet(k, carry):
        pl.semaphore_signal(barrier, 1, device_id=(node, (me + k) % count), device_id_type=pl.DeviceIdType.MESH)
        return carry

    lax.fori_loop(1, count, greet, 0)
    pl.semaphore_wait(barrier, count - 1)

    def remote(target, slot):
        return pltpu.make_async_remote_copy(
            part_ref.at[pl.ds(target, 1)], recv.at[pl.ds(slot, 1)], send_sems.at[target], recv_sems.at[slot],
            device_id=(node, target), device_id_type=pl.DeviceIdType.MESH)

    def send(k, carry):
        remote((me + k) % count, me).start()
        return carry

    lax.fori_loop(1, count, send, 0)

    def finish(k, carry):
        remote((me + k) % count, me).wait_send()
        source = (me + count - k) % count
        remote(source, source).wait_recv()
        return carry

    lax.fori_loop(1, count, finish, 0)
    rows = lax.broadcasted_iota(jnp.int32, part_ref.shape, 0)
    out_ref[...] = jnp.sum(jnp.where(rows == me, part_ref[...], recv[...]), axis=0, keepdims=True)


def reduce_scatter(pooled, count):
    width = pooled.shape[0] // count
    out = pl.pallas_call(
        scatter_kernel,
        in_specs=[pl.BlockSpec(memory_space=pltpu.VMEM)],
        out_specs=pl.BlockSpec(memory_space=pltpu.VMEM),
        out_shape=jax.ShapeDtypeStruct((1, width), pooled.dtype),
        scratch_shapes=[
            pltpu.VMEM((count, width), pooled.dtype),
            pltpu.SemaphoreType.DMA((count,)),
            pltpu.SemaphoreType.DMA((count,)),
        ],
        compiler_params=pltpu.CompilerParams(collective_id=0, has_side_effects=True),
    )(pooled.reshape(count, width))
    return out.reshape(width)


def body(embedding, send_list, edge_ends, pair_index, w_first, b_first, w_second):
    node_count = lax.axis_size("node")
    node_self = lax.axis_index("node")
    blocks_here = embedding.shape[0]
    block_rows = embedding.shape[1]
    feature_width = embedding.shape[2]
    lanes = 128
    parts = feature_width // lanes
    early_len = EARLY_ROWS * parts
    slot_len = early_len + 8
    wanted = send_list[0, 0]
    pick = jnp.where(wanted >= 0, wanted, blocks_here)
    narrow = embedding.reshape(blocks_here, block_rows * parts, lanes)
    narrow = jnp.concatenate([narrow, jnp.zeros((1, block_rows * parts, lanes), embedding.dtype)], axis=0)
    marks = jnp.arange(blocks_here + 1, dtype=jnp.int32)
    marks = jnp.where(marks < blocks_here, marks, -1).astype(embedding.dtype)
    marks = jnp.broadcast_to(marks[:, None, None], (blocks_here + 1, 8, lanes))
    early_source = jnp.concatenate([narrow[:, :early_len], marks], axis=1)
    late_rows = block_rows - EARLY_ROWS
    late_source = jnp.concatenate([embedding[:, EARLY_ROWS:], jnp.zeros((1, late_rows, feature_width), embedding.dtype)], axis=0)
    early_picked = jnp.take(early_source, pick, axis=0, mode="clip")
    late_picked = jnp.take(late_source, pick, axis=0, mode="clip")
    early_arrived = lax.all_to_all(early_picked, "node", split_axis=0, concat_axis=0, tiled=True)
    late_picked, early_arrived = lax.optimization_barrier((late_picked, early_arrived))
    late_arrived = lax.all_to_all(late_picked, "node", split_axis=0, concat_axis=0, tiled=True)
    early_table = early_arrived.reshape(node_count * slot_len, lanes)
    late_table = late_arrived.reshape(node_count * late_rows, feature_width)
    source = edge_ends // (blocks_here * block_rows)
    block_of = (edge_ends // block_rows) % blocks_here
    within = edge_ends % block_rows
    early = within < EARLY_ROWS
    early_position = source * slot_len + jnp.where(early, within, 0) * parts
    sent = early_arrived[:, early_len, 0].astype(jnp.int32)
    located = jnp.any((source[..., None] == jnp.arange(node_count, dtype=jnp.int32))
                      & (block_of[..., None] == sent), axis=-1)
    early_mask = (located & early).T.astype(jnp.float32)
    late_index = jnp.where(located & ~early, source * late_rows + within - EARLY_ROWS, -1)
    partial = early_products(early_position, early_mask, early_table, w_first)
    pair_ids = pair_index - node_self * PAIRS_ROW
    edge_score, pooled_sum = late_scores(late_index, partial, pair_ids, late_table, w_first, b_first, w_second)
    pair_cost = reduce_scatter(pooled_sum, lax.axis_size("edge"))
    return (edge_score, pair_cost)


def solution(mesh):
    return jax.shard_map(
        body,
        mesh=mesh,
        in_specs=(
            P("node", None, None),
            P("edge", "node", None),
            P(None, ("node", "edge")),
            P(("node", "edge")),
            P(),
            P(),
            P(),
        ),
        out_specs=(P(("node", "edge")), P(("node", "edge"))),
        check_vma=False,
    )
```

```python
import functools

import jax
import jax.numpy as jnp
from jax import lax
from jax.experimental import pallas as pl
from jax.experimental.pallas import tpu as pltpu
from jax.sharding import PartitionSpec as P

PAIRS_ROW = 1024
TILE = 256
LATE_TILE = 256
EARLY_ROWS = 96


def gelu_tanh(x):
    return x * (0.5 * (1.0 + jnp.tanh(0.7978845608028654 * (x + 0.044715 * (x * x * x)))))


def early_kernel(edges, pos_ref, table, mask_ref, wt_ref, wb_ref, part_ref, buf, wide, sems):
    step = pl.program_id(0)
    steps = pl.num_programs(0)
    parts = buf.shape[2] // TILE
    lanes = buf.shape[3]

    def fetch(tile, slot):
        base = tile * TILE

        def one(r, carry):
            dst = pl.ds(pl.multiple_of(r * parts, parts), parts)
            for end in range(2):
                src = pl.ds(pl.multiple_of(pos_ref[end * edges + base + r], parts), parts)
                pltpu.make_async_copy(table.at[src], buf.at[end, slot, dst], sems.at[end, slot]).start()
            return carry

        lax.fori_loop(0, TILE, one, 0, unroll=8)

    @pl.when(step == 0)
    def _():
        fetch(0, 0)

    slot = step % 2

    @pl.when(step + 1 < steps)
    def _():
        fetch(step + 1, 1 - slot)

    for end in range(2):
        pltpu.make_async_copy(table.at[pl.ds(0, TILE * parts)], buf.at[end, slot], sems.at[end, slot]).wait()

    mask = mask_ref[...]
    total = None
    for end, w_ref in ((0, wt_ref), (1, wb_ref)):
        wide[...] = buf[end, slot].astype(jnp.float32)
        keep = mask[:, end:end + 1] > 0
        for q in range(parts):
            piece = wide[pl.ds(q, TILE, stride=parts), :]
            piece = jnp.where(keep, piece, jnp.zeros_like(piece)).astype(jnp.bfloat16)
            term = jnp.dot(piece, w_ref[q * lanes:(q + 1) * lanes, :], preferred_element_type=jnp.float32)
            total = term if total is None else total + term
    part_ref[...] = total


def late_kernel(idx_ref, part_ref, table_ref, wt_ref, wb_ref, bias_ref, wo_ref, pid_ref, score_ref, pool_ref):
    step = pl.program_id(0)

    @pl.when(step == 0)
    def _():
        pool_ref[...] = jnp.zeros_like(pool_ref)

    idx = idx_ref[...]
    rows = table_ref.shape[0]
    slots = lax.broadcasted_iota(jnp.int32, (LATE_TILE, rows), 1)
    preact = part_ref[...]
    for end, w_ref in ((0, wt_ref), (1, wb_ref)):
        onehot = (idx[:, end:end + 1] == slots).astype(table_ref.dtype)
        picked = jnp.dot(onehot, table_ref[...], preferred_element_type=jnp.float32).astype(table_ref.dtype)
        preact = preact + jnp.dot(picked, w_ref[...], preferred_element_type=jnp.float32)
    hidden = gelu_tanh(preact + bias_ref[...])
    scores = jnp.sum(hidden * wo_ref[0:1, :], axis=1, keepdims=True)
    score_ref[...] = scores
    pair_range = lax.broadcasted_iota(jnp.int32, (LATE_TILE, PAIRS_ROW), 1)
    pooled = jnp.where(pid_ref[...] == pair_range, scores, 0.0)
    pool_ref[...] += jnp.sum(pooled, axis=0, keepdims=True)


def early_products(position, mask, table, w_first):
    edges = position.shape[1]
    lanes = table.shape[1]
    width = w_first.shape[0] // 2
    parts = width // lanes
    hid = w_first.shape[1]
    grid_spec = pltpu.PrefetchScalarGridSpec(
        num_scalar_prefetch=1,
        grid=(edges // TILE,),
        in_specs=[
            pl.BlockSpec(memory_space=pl.ANY),
            pl.BlockSpec((TILE, 2), lambda i, p: (i, 0)),
            pl.BlockSpec((width, hid), lambda i, p: (0, 0)),
            pl.BlockSpec((width, hid), lambda i, p: (1, 0)),
        ],
        out_specs=pl.BlockSpec((TILE, hid), lambda i, p: (i, 0)),
        scratch_shapes=[
            pltpu.VMEM((2, 2, TILE * parts, lanes), table.dtype),
            pltpu.VMEM((TILE * parts, lanes), jnp.float32),
            pltpu.SemaphoreType.DMA((2, 2)),
        ],
    )
    return pl.pallas_call(
        functools.partial(early_kernel, edges),
        grid_spec=grid_spec,
        out_shape=jax.ShapeDtypeStruct((edges, hid), jnp.float32),
        compiler_params=pltpu.CompilerParams(dimension_semantics=("arbitrary",)),
        cost_estimate=pl.CostEstimate(
            flops=2 * edges * 2 * width * hid, transcendentals=0,
            bytes_accessed=2 * edges * width * table.dtype.itemsize + edges * hid * 4),
    )(position.reshape(2 * edges), table, mask, w_first, w_first)


def late_scores(late_index, partial, pair_ids, table, w_first, b_first, w_second):
    edges = late_index.shape[1]
    rows, width = table.shape
    hid = w_first.shape[1]
    wo8 = jnp.broadcast_to(w_second.astype(jnp.float32)[None, :], (8, hid))
    scores, pooled = pl.pallas_call(
        late_kernel,
        grid=(edges // LATE_TILE,),
        in_specs=[
            pl.BlockSpec((LATE_TILE, 2), lambda i: (i, 0)),
            pl.BlockSpec((LATE_TILE, hid), lambda i: (i, 0)),
            pl.BlockSpec((rows, width), lambda i: (0, 0)),
            pl.BlockSpec((width, hid), lambda i: (0, 0)),
            pl.BlockSpec((width, hid), lambda i: (1, 0)),
            pl.BlockSpec((1, hid), lambda i: (0, 0)),
            pl.BlockSpec((8, hid), lambda i: (0, 0)),
            pl.BlockSpec((LATE_TILE, 1), lambda i: (i, 0)),
        ],
        out_specs=[
            pl.BlockSpec((LATE_TILE, 1), lambda i: (i, 0)),
            pl.BlockSpec((1, PAIRS_ROW), lambda i: (0, 0)),
        ],
        out_shape=[
            jax.ShapeDtypeStruct((edges, 1), jnp.float32),
            jax.ShapeDtypeStruct((1, PAIRS_ROW), jnp.float32),
        ],
        compiler_params=pltpu.CompilerParams(dimension_semantics=("arbitrary",)),
        cost_estimate=pl.CostEstimate(
            flops=2 * edges * 2 * (rows + hid) * width, transcendentals=edges * hid,
            bytes_accessed=rows * width * 2 + edges * hid * 4),
    )(late_index.T, partial, table, w_first, w_first, b_first.reshape(1, hid), wo8, pair_ids.reshape(edges, 1))
    return scores.reshape(edges), pooled.reshape(PAIRS_ROW)


def scatter_kernel(part_ref, out_ref, recv, send_sems, recv_sems):
    count = part_ref.shape[0]
    me = lax.axis_index("edge")
    node = lax.axis_index("node")
    barrier = pltpu.get_barrier_semaphore()

    def greet(k, carry):
        pl.semaphore_signal(barrier, 1, device_id=(node, (me + k) % count), device_id_type=pl.DeviceIdType.MESH)
        return carry

    lax.fori_loop(1, count, greet, 0)
    pl.semaphore_wait(barrier, count - 1)

    def remote(target, slot):
        return pltpu.make_async_remote_copy(
            part_ref.at[pl.ds(target, 1)], recv.at[pl.ds(slot, 1)], send_sems.at[target], recv_sems.at[slot],
            device_id=(node, target), device_id_type=pl.DeviceIdType.MESH)

    def send(k, carry):
        remote((me + k) % count, me).start()
        return carry

    lax.fori_loop(1, count, send, 0)

    def finish(k, carry):
        remote((me + k) % count, me).wait_send()
        source = (me + count - k) % count
        remote(source, source).wait_recv()
        return carry

    lax.fori_loop(1, count, finish, 0)
    rows = lax.broadcasted_iota(jnp.int32, part_ref.shape, 0)
    out_ref[...] = jnp.sum(jnp.where(rows == me, part_ref[...], recv[...]), axis=0, keepdims=True)


def reduce_scatter(pooled, count):
    width = pooled.shape[0] // count
    out = pl.pallas_call(
        scatter_kernel,
        in_specs=[pl.BlockSpec(memory_space=pltpu.VMEM)],
        out_specs=pl.BlockSpec(memory_space=pltpu.VMEM),
        out_shape=jax.ShapeDtypeStruct((1, width), pooled.dtype),
        scratch_shapes=[
            pltpu.VMEM((count, width), pooled.dtype),
            pltpu.SemaphoreType.DMA((count,)),
            pltpu.SemaphoreType.DMA((count,)),
        ],
        compiler_params=pltpu.CompilerParams(collective_id=0, has_side_effects=True),
    )(pooled.reshape(count, width))
    return out.reshape(width)


def body(embedding, send_list, edge_ends, pair_index, w_first, b_first, w_second):
    node_count = lax.axis_size("node")
    node_self = lax.axis_index("node")
    blocks_here = embedding.shape[0]
    block_rows = embedding.shape[1]
    feature_width = embedding.shape[2]
    lanes = 128
    parts = feature_width // lanes
    early_len = EARLY_ROWS * parts
    late_rows = block_rows - EARLY_ROWS
    slot_len = early_len + 8
    wanted = send_list[0, 0]
    pick = jnp.where(wanted >= 0, wanted, blocks_here)
    narrow = embedding.reshape(blocks_here, block_rows * parts, lanes)
    narrow = jnp.concatenate([narrow, jnp.zeros((1, block_rows * parts, lanes), embedding.dtype)], axis=0)
    marks = jnp.arange(blocks_here + 1, dtype=jnp.int32)
    marks = jnp.where(marks < blocks_here, marks, -1).astype(embedding.dtype)
    marks = jnp.broadcast_to(marks[:, None, None], (blocks_here + 1, 8, lanes))
    early_source = jnp.concatenate([narrow[:, :early_len], marks], axis=1)
    late_source = jnp.concatenate([embedding[:, EARLY_ROWS:], jnp.zeros((1, late_rows, feature_width), embedding.dtype)], axis=0)
    early_picked = jnp.take(early_source, pick, axis=0, mode="clip")
    late_picked = jnp.take(late_source, pick, axis=0, mode="clip")
    early_arrived = lax.all_to_all(early_picked, "node", split_axis=0, concat_axis=0, tiled=True)
    source = edge_ends // (blocks_here * block_rows)
    block_of = (edge_ends // block_rows) % blocks_here
    within = edge_ends % block_rows
    early = within < EARLY_ROWS
    early_position = source * slot_len + jnp.where(early, within, 0) * parts
    late_rows = block_rows - EARLY_ROWS
    late_spot = source * late_rows + within - EARLY_ROWS
    pair_ids = (pair_index - node_self * PAIRS_ROW).reshape(-1, 1)
    late_picked, early_arrived, early_position, late_spot, pair_ids = lax.optimization_barrier(
        (late_picked, early_arrived, early_position, late_spot, pair_ids))
    late_arrived = lax.all_to_all(late_picked, "node", split_axis=0, concat_axis=0, tiled=True)
    early_table = early_arrived.reshape(node_count * slot_len, lanes)
    late_table = late_arrived.reshape(node_count * late_rows, feature_width)
    sent = early_arrived[:, early_len, 0].astype(jnp.int32)
    located = jnp.any((source[..., None] == jnp.arange(node_count, dtype=jnp.int32))
                      & (block_of[..., None] == sent), axis=-1)
    early_mask = (located & early).T.astype(jnp.float32)
    late_index = jnp.where(located & ~early, late_spot, -1)
    partial = early_products(early_position, early_mask, early_table, w_first)
    edge_score, pooled_sum = late_scores(late_index, partial, pair_ids, late_table, w_first, b_first, w_second)
    pair_cost = reduce_scatter(pooled_sum, lax.axis_size("edge"))
    return (edge_score, pair_cost)


def solution(mesh):
    return jax.shard_map(
        body,
        mesh=mesh,
        in_specs=(
            P("node", None, None),
            P("edge", "node", None),
            P(None, ("node", "edge")),
            P(("node", "edge")),
            P(),
            P(),
            P(),
        ),
        out_specs=(P(("node", "edge")), P(("node", "edge"))),
        check_vma=False,
    )
```

```python
import functools

import jax
import jax.numpy as jnp
from jax import lax
from jax.experimental import pallas as pl
from jax.experimental.pallas import tpu as pltpu
from jax.sharding import PartitionSpec as P

PAIRS_ROW = 1024
TILE = 256
LATE_TILE = 256
EARLY_ROWS = 96


def gelu_tanh(x):
    return x * (0.5 * (1.0 + jnp.tanh(0.7978845608028654 * (x + 0.044715 * (x * x * x)))))


def early_kernel(edges, pos_ref, table, mask_ref, wt_ref, wb_ref, part_ref, buf, wide, sems):
    step = pl.program_id(0)
    steps = pl.num_programs(0)
    parts = buf.shape[2] // TILE
    lanes = buf.shape[3]

    def fetch(tile, slot):
        base = tile * TILE

        def one(r, carry):
            dst = pl.ds(pl.multiple_of(r * parts, parts), parts)
            for end in range(2):
                src = pl.ds(pl.multiple_of(pos_ref[end * edges + base + r], parts), parts)
                pltpu.make_async_copy(table.at[src], buf.at[end, slot, dst], sems.at[end, slot]).start()
            return carry

        lax.fori_loop(0, TILE, one, 0, unroll=8)

    @pl.when(step == 0)
    def _():
        fetch(0, 0)

    slot = step % 2

    @pl.when(step + 1 < steps)
    def _():
        fetch(step + 1, 1 - slot)

    for end in range(2):
        pltpu.make_async_copy(table.at[pl.ds(0, TILE * parts)], buf.at[end, slot], sems.at[end, slot]).wait()

    mask = mask_ref[...]
    total = None
    for end, w_ref in ((0, wt_ref), (1, wb_ref)):
        wide[...] = buf[end, slot].astype(jnp.float32)
        keep = mask[:, end:end + 1] > 0
        for q in range(parts):
            piece = wide[pl.ds(q, TILE, stride=parts), :]
            piece = jnp.where(keep, piece, jnp.zeros_like(piece)).astype(jnp.bfloat16)
            term = jnp.dot(piece, w_ref[q * lanes:(q + 1) * lanes, :], preferred_element_type=jnp.float32)
            total = term if total is None else total + term
    part_ref[...] = total


def late_kernel(idx_ref, part_ref, table_ref, wt_ref, wb_ref, bias_ref, wo_ref, pid_ref, score_ref, pool_ref):
    step = pl.program_id(0)

    @pl.when(step == 0)
    def _():
        pool_ref[...] = jnp.zeros_like(pool_ref)

    idx = idx_ref[...]
    rows = table_ref.shape[0]
    slots = lax.broadcasted_iota(jnp.int32, (LATE_TILE, rows), 1)
    preact = part_ref[...]
    for end, w_ref in ((0, wt_ref), (1, wb_ref)):
        onehot = (idx[:, end:end + 1] == slots).astype(table_ref.dtype)
        picked = jnp.dot(onehot, table_ref[...], preferred_element_type=jnp.float32).astype(table_ref.dtype)
        preact = preact + jnp.dot(picked, w_ref[...], preferred_element_type=jnp.float32)
    hidden = gelu_tanh(preact + bias_ref[...])
    scores = jnp.sum(hidden * wo_ref[0:1, :], axis=1, keepdims=True)
    score_ref[...] = jnp.broadcast_to(scores, (LATE_TILE, 128)).T[0:1, :]
    pair_range = lax.broadcasted_iota(jnp.int32, (LATE_TILE, PAIRS_ROW), 1)
    pooled = jnp.where(pid_ref[...] == pair_range, scores, 0.0)
    pool_ref[...] += jnp.sum(pooled, axis=0, keepdims=True)


def early_products(position, mask, table, w_first):
    edges = position.shape[1]
    lanes = table.shape[1]
    width = w_first.shape[0] // 2
    parts = width // lanes
    hid = w_first.shape[1]
    grid_spec = pltpu.PrefetchScalarGridSpec(
        num_scalar_prefetch=1,
        grid=(edges // TILE,),
        in_specs=[
            pl.BlockSpec(memory_space=pl.ANY),
            pl.BlockSpec((TILE, 2), lambda i, p: (i, 0)),
            pl.BlockSpec((width, hid), lambda i, p: (0, 0)),
            pl.BlockSpec((width, hid), lambda i, p: (1, 0)),
        ],
        out_specs=pl.BlockSpec((TILE, hid), lambda i, p: (i, 0)),
        scratch_shapes=[
            pltpu.VMEM((2, 2, TILE * parts, lanes), table.dtype),
            pltpu.VMEM((TILE * parts, lanes), jnp.float32),
            pltpu.SemaphoreType.DMA((2, 2)),
        ],
    )
    return pl.pallas_call(
        functools.partial(early_kernel, edges),
        grid_spec=grid_spec,
        out_shape=jax.ShapeDtypeStruct((edges, hid), jnp.float32),
        compiler_params=pltpu.CompilerParams(dimension_semantics=("arbitrary",)),
        cost_estimate=pl.CostEstimate(
            flops=2 * edges * 2 * width * hid, transcendentals=0,
            bytes_accessed=2 * edges * width * table.dtype.itemsize + edges * hid * 4),
    )(position.reshape(2 * edges), table, mask, w_first, w_first)


def late_scores(late_index, partial, pair_ids, table, w_first, b_first, w_second):
    edges = late_index.shape[1]
    rows, width = table.shape
    hid = w_first.shape[1]
    wo8 = jnp.broadcast_to(w_second.astype(jnp.float32)[None, :], (8, hid))
    scores, pooled = pl.pallas_call(
        late_kernel,
        grid=(edges // LATE_TILE,),
        in_specs=[
            pl.BlockSpec((LATE_TILE, 2), lambda i: (i, 0)),
            pl.BlockSpec((LATE_TILE, hid), lambda i: (i, 0)),
            pl.BlockSpec((rows, width), lambda i: (0, 0)),
            pl.BlockSpec((width, hid), lambda i: (0, 0)),
            pl.BlockSpec((width, hid), lambda i: (1, 0)),
            pl.BlockSpec((1, hid), lambda i: (0, 0)),
            pl.BlockSpec((8, hid), lambda i: (0, 0)),
            pl.BlockSpec((LATE_TILE, 1), lambda i: (i, 0)),
        ],
        out_specs=[
            pl.BlockSpec((1, LATE_TILE), lambda i: (0, i)),
            pl.BlockSpec((1, PAIRS_ROW), lambda i: (0, 0)),
        ],
        out_shape=[
            jax.ShapeDtypeStruct((1, edges), jnp.float32),
            jax.ShapeDtypeStruct((1, PAIRS_ROW), jnp.float32),
        ],
        compiler_params=pltpu.CompilerParams(dimension_semantics=("arbitrary",)),
        cost_estimate=pl.CostEstimate(
            flops=2 * edges * 2 * (rows + hid) * width, transcendentals=edges * hid,
            bytes_accessed=rows * width * 2 + edges * hid * 4),
    )(late_index.T, partial, table, w_first, w_first, b_first.reshape(1, hid), wo8, pair_ids.reshape(edges, 1))
    return scores.reshape(edges), pooled.reshape(PAIRS_ROW)


def scatter_kernel(part_ref, out_ref, recv, send_sems, recv_sems):
    count = part_ref.shape[0]
    me = lax.axis_index("edge")
    node = lax.axis_index("node")
    barrier = pltpu.get_barrier_semaphore()

    def greet(k, carry):
        pl.semaphore_signal(barrier, 1, device_id=(node, (me + k) % count), device_id_type=pl.DeviceIdType.MESH)
        return carry

    lax.fori_loop(1, count, greet, 0)
    pl.semaphore_wait(barrier, count - 1)

    def remote(target, slot):
        return pltpu.make_async_remote_copy(
            part_ref.at[pl.ds(target, 1)], recv.at[pl.ds(slot, 1)], send_sems.at[target], recv_sems.at[slot],
            device_id=(node, target), device_id_type=pl.DeviceIdType.MESH)

    def send(k, carry):
        remote((me + k) % count, me).start()
        return carry

    lax.fori_loop(1, count, send, 0)

    def finish(k, carry):
        remote((me + k) % count, me).wait_send()
        source = (me + count - k) % count
        remote(source, source).wait_recv()
        return carry

    lax.fori_loop(1, count, finish, 0)
    rows = lax.broadcasted_iota(jnp.int32, part_ref.shape, 0)
    out_ref[...] = jnp.sum(jnp.where(rows == me, part_ref[...], recv[...]), axis=0)


def reduce_scatter(pooled, count):
    width = pooled.shape[0] // count
    out = pl.pallas_call(
        scatter_kernel,
        in_specs=[pl.BlockSpec(memory_space=pltpu.VMEM)],
        out_specs=pl.BlockSpec(memory_space=pltpu.VMEM),
        out_shape=jax.ShapeDtypeStruct((width,), pooled.dtype),
        scratch_shapes=[
            pltpu.VMEM((count, width), pooled.dtype),
            pltpu.SemaphoreType.DMA((count,)),
            pltpu.SemaphoreType.DMA((count,)),
        ],
        compiler_params=pltpu.CompilerParams(collective_id=0, has_side_effects=True),
    )(pooled.reshape(count, width))
    return out


def body(embedding, send_list, edge_ends, pair_index, w_first, b_first, w_second):
    node_count = lax.axis_size("node")
    node_self = lax.axis_index("node")
    blocks_here = embedding.shape[0]
    block_rows = embedding.shape[1]
    feature_width = embedding.shape[2]
    lanes = 128
    parts = feature_width // lanes
    early_len = EARLY_ROWS * parts
    late_rows = block_rows - EARLY_ROWS
    slot_len = early_len + 8
    wanted = send_list[0, 0]
    pick = jnp.where(wanted >= 0, wanted, blocks_here)
    narrow = embedding.reshape(blocks_here, block_rows * parts, lanes)
    narrow = jnp.concatenate([narrow, jnp.zeros((1, block_rows * parts, lanes), embedding.dtype)], axis=0)
    marks = jnp.arange(blocks_here + 1, dtype=jnp.int32)
    marks = jnp.where(marks < blocks_here, marks, -1).astype(embedding.dtype)
    marks = jnp.broadcast_to(marks[:, None, None], (blocks_here + 1, 8, lanes))
    early_source = jnp.concatenate([narrow[:, :early_len], marks], axis=1)
    late_source = jnp.concatenate([embedding[:, EARLY_ROWS:], jnp.zeros((1, late_rows, feature_width), embedding.dtype)], axis=0)
    early_picked = jnp.take(early_source, pick, axis=0, mode="clip")
    late_picked = jnp.take(late_source, pick, axis=0, mode="clip")
    early_arrived = lax.all_to_all(early_picked, "node", split_axis=0, concat_axis=0, tiled=True)
    source = edge_ends // (blocks_here * block_rows)
    block_of = (edge_ends // block_rows) % blocks_here
    within = edge_ends % block_rows
    early = within < EARLY_ROWS
    early_position = source * slot_len + jnp.where(early, within, 0) * parts
    late_rows = block_rows - EARLY_ROWS
    late_spot = source * late_rows + within - EARLY_ROWS
    pair_ids = (pair_index - node_self * PAIRS_ROW).reshape(-1, 1)
    late_picked, early_arrived, early_position, late_spot, pair_ids = lax.optimization_barrier(
        (late_picked, early_arrived, early_position, late_spot, pair_ids))
    late_arrived = lax.all_to_all(late_picked, "node", split_axis=0, concat_axis=0, tiled=True)
    early_table = early_arrived.reshape(node_count * slot_len, lanes)
    late_table = late_arrived.reshape(node_count * late_rows, feature_width)
    sent = early_arrived[:, early_len, 0].astype(jnp.int32)
    located = jnp.any((source[..., None] == jnp.arange(node_count, dtype=jnp.int32))
                      & (block_of[..., None] == sent), axis=-1)
    early_mask = (located & early).T.astype(jnp.float32)
    late_index = jnp.where(located & ~early, late_spot, -1)
    partial = early_products(early_position, early_mask, early_table, w_first)
    edge_score, pooled_sum = late_scores(late_index, partial, pair_ids, late_table, w_first, b_first, w_second)
    pair_cost = reduce_scatter(pooled_sum, lax.axis_size("edge"))
    return (edge_score, pair_cost)


def solution(mesh):
    return jax.shard_map(
        body,
        mesh=mesh,
        in_specs=(
            P("node", None, None),
            P("edge", "node", None),
            P(None, ("node", "edge")),
            P(("node", "edge")),
            P(),
            P(),
            P(),
        ),
        out_specs=(P(("node", "edge")), P(("node", "edge"))),
        check_vma=False,
    )
```

```python
import functools

import jax
import jax.numpy as jnp
from jax import lax
from jax.experimental import pallas as pl
from jax.experimental.pallas import tpu as pltpu
from jax.sharding import PartitionSpec as P

PAIRS_ROW = 1024
TILE = 256
LATE_TILE = 256
EARLY_ROWS = 96


def gelu_tanh(x):
    return x * (0.5 * (1.0 + jnp.tanh(0.7978845608028654 * (x + 0.044715 * (x * x * x)))))


def early_kernel(edges, pos_ref, table, mask_ref, wt_ref, wb_ref, part_ref, buf, wide, sems):
    step = pl.program_id(0)
    steps = pl.num_programs(0)
    parts = buf.shape[2] // TILE
    lanes = buf.shape[3]

    def fetch(tile, slot):
        base = tile * TILE

        def one(r, carry):
            dst = pl.ds(pl.multiple_of(r * parts, parts), parts)
            for end in range(2):
                src = pl.ds(pl.multiple_of(pos_ref[end * edges + base + r], parts), parts)
                pltpu.make_async_copy(table.at[src], buf.at[end, slot, dst], sems.at[end, slot]).start()
            return carry

        lax.fori_loop(0, TILE, one, 0, unroll=8)

    @pl.when(step == 0)
    def _():
        fetch(0, 0)

    slot = step % 2

    @pl.when(step + 1 < steps)
    def _():
        fetch(step + 1, 1 - slot)

    for end in range(2):
        pltpu.make_async_copy(table.at[pl.ds(0, TILE * parts)], buf.at[end, slot], sems.at[end, slot]).wait()

    mask = mask_ref[...]
    total = None
    for end, w_ref in ((0, wt_ref), (1, wb_ref)):
        wide[...] = buf[end, slot].astype(jnp.float32)
        keep = mask[:, end:end + 1] > 0
        for q in range(parts):
            piece = wide[pl.ds(q, TILE, stride=parts), :]
            piece = jnp.where(keep, piece, jnp.zeros_like(piece)).astype(jnp.bfloat16)
            term = jnp.dot(piece, w_ref[q * lanes:(q + 1) * lanes, :], preferred_element_type=jnp.float32)
            total = term if total is None else total + term
    part_ref[...] = total


def late_kernel(idx_ref, part_ref, table_ref, wt_ref, wb_ref, bias_ref, wo_ref, pid_ref, score_ref, cost_ref,
                pool, chunks, recv, send_sems, recv_sems):
    step = pl.program_id(0)
    steps = pl.num_programs(0)
    count = recv.shape[0]
    width = recv.shape[1]
    me = lax.axis_index("edge")
    node = lax.axis_index("node")
    barrier = pltpu.get_barrier_semaphore()

    @pl.when(step == 0)
    def _():
        def greet(k, carry):
            pl.semaphore_signal(barrier, 1, device_id=(node, (me + k) % count), device_id_type=pl.DeviceIdType.MESH)
            return carry

        lax.fori_loop(1, count, greet, 0)
        pool[...] = jnp.zeros_like(pool)

    idx = idx_ref[...]
    rows = table_ref.shape[0]
    slots = lax.broadcasted_iota(jnp.int32, (LATE_TILE, rows), 1)
    preact = part_ref[...]
    for end, w_ref in ((0, wt_ref), (1, wb_ref)):
        onehot = (idx[:, end:end + 1] == slots).astype(table_ref.dtype)
        picked = jnp.dot(onehot, table_ref[...], preferred_element_type=jnp.float32).astype(table_ref.dtype)
        preact = preact + jnp.dot(picked, w_ref[...], preferred_element_type=jnp.float32)
    hidden = gelu_tanh(preact + bias_ref[...])
    scores = jnp.sum(hidden * wo_ref[0:1, :], axis=1, keepdims=True)
    score_ref[...] = jnp.broadcast_to(scores, (LATE_TILE, 128)).T[0:1, :]
    pair_range = lax.broadcasted_iota(jnp.int32, (LATE_TILE, PAIRS_ROW), 1)
    pooled = jnp.where(pid_ref[...] == pair_range, scores, 0.0)
    pool[...] += jnp.sum(pooled, axis=0, keepdims=True)

    @pl.when(step == steps - 1)
    def _():
        for t in range(count):
            chunks[t:t + 1, :] = pool[:, t * width:(t + 1) * width]
        pl.semaphore_wait(barrier, count - 1)

        def remote(target, slot):
            return pltpu.make_async_remote_copy(
                chunks.at[pl.ds(target, 1)], recv.at[pl.ds(slot, 1)], send_sems.at[target], recv_sems.at[slot],
                device_id=(node, target), device_id_type=pl.DeviceIdType.MESH)

        def send(k, carry):
            remote((me + k) % count, me).start()
            return carry

        lax.fori_loop(1, count, send, 0)

        def finish(k, carry):
            remote((me + k) % count, me).wait_send()
            source = (me + count - k) % count
            remote(source, source).wait_recv()
            return carry

        lax.fori_loop(1, count, finish, 0)
        here = lax.broadcasted_iota(jnp.int32, (count, width), 0)
        cost_ref[...] = jnp.sum(jnp.where(here == me, chunks[...], recv[...]), axis=0)


def early_products(position, mask, table, w_first):
    edges = position.shape[1]
    lanes = table.shape[1]
    width = w_first.shape[0] // 2
    parts = width // lanes
    hid = w_first.shape[1]
    grid_spec = pltpu.PrefetchScalarGridSpec(
        num_scalar_prefetch=1,
        grid=(edges // TILE,),
        in_specs=[
            pl.BlockSpec(memory_space=pl.ANY),
            pl.BlockSpec((TILE, 2), lambda i, p: (i, 0)),
            pl.BlockSpec((width, hid), lambda i, p: (0, 0)),
            pl.BlockSpec((width, hid), lambda i, p: (1, 0)),
        ],
        out_specs=pl.BlockSpec((TILE, hid), lambda i, p: (i, 0)),
        scratch_shapes=[
            pltpu.VMEM((2, 2, TILE * parts, lanes), table.dtype),
            pltpu.VMEM((TILE * parts, lanes), jnp.float32),
            pltpu.SemaphoreType.DMA((2, 2)),
        ],
    )
    return pl.pallas_call(
        functools.partial(early_kernel, edges),
        grid_spec=grid_spec,
        out_shape=jax.ShapeDtypeStruct((edges, hid), jnp.float32),
        compiler_params=pltpu.CompilerParams(dimension_semantics=("arbitrary",)),
        cost_estimate=pl.CostEstimate(
            flops=2 * edges * 2 * width * hid, transcendentals=0,
            bytes_accessed=2 * edges * width * table.dtype.itemsize + edges * hid * 4),
    )(position.reshape(2 * edges), table, mask, w_first, w_first)


def late_scores(late_index, partial, pair_ids, table, w_first, b_first, w_second, count):
    edges = late_index.shape[1]
    rows, width = table.shape
    hid = w_first.shape[1]
    share = PAIRS_ROW // count
    wo8 = jnp.broadcast_to(w_second.astype(jnp.float32)[None, :], (8, hid))
    scores, cost = pl.pallas_call(
        late_kernel,
        grid=(edges // LATE_TILE,),
        in_specs=[
            pl.BlockSpec((LATE_TILE, 2), lambda i: (i, 0)),
            pl.BlockSpec((LATE_TILE, hid), lambda i: (i, 0)),
            pl.BlockSpec((rows, width), lambda i: (0, 0)),
            pl.BlockSpec((width, hid), lambda i: (0, 0)),
            pl.BlockSpec((width, hid), lambda i: (1, 0)),
            pl.BlockSpec((1, hid), lambda i: (0, 0)),
            pl.BlockSpec((8, hid), lambda i: (0, 0)),
            pl.BlockSpec((LATE_TILE, 1), lambda i: (i, 0)),
        ],
        out_specs=[
            pl.BlockSpec((1, LATE_TILE), lambda i: (0, i)),
            pl.BlockSpec((share,), lambda i: (0,)),
        ],
        out_shape=[
            jax.ShapeDtypeStruct((1, edges), jnp.float32),
            jax.ShapeDtypeStruct((share,), jnp.float32),
        ],
        scratch_shapes=[
            pltpu.VMEM((1, PAIRS_ROW), jnp.float32),
            pltpu.VMEM((count, share), jnp.float32),
            pltpu.VMEM((count, share), jnp.float32),
            pltpu.SemaphoreType.DMA((count,)),
            pltpu.SemaphoreType.DMA((count,)),
        ],
        compiler_params=pltpu.CompilerParams(
            dimension_semantics=("arbitrary",), collective_id=0, has_side_effects=True),
        cost_estimate=pl.CostEstimate(
            flops=2 * edges * 2 * (rows + hid) * width, transcendentals=edges * hid,
            bytes_accessed=rows * width * 2 + edges * hid * 4),
    )(late_index.T, partial, table, w_first, w_first, b_first.reshape(1, hid), wo8, pair_ids)
    return scores.reshape(edges), cost


def body(embedding, send_list, edge_ends, pair_index, w_first, b_first, w_second):
    node_count = lax.axis_size("node")
    node_self = lax.axis_index("node")
    blocks_here = embedding.shape[0]
    block_rows = embedding.shape[1]
    feature_width = embedding.shape[2]
    lanes = 128
    parts = feature_width // lanes
    early_len = EARLY_ROWS * parts
    late_rows = block_rows - EARLY_ROWS
    slot_len = early_len + 8
    wanted = send_list[0, 0]
    pick = jnp.where(wanted >= 0, wanted, blocks_here)
    narrow = embedding.reshape(blocks_here, block_rows * parts, lanes)
    narrow = jnp.concatenate([narrow, jnp.zeros((1, block_rows * parts, lanes), embedding.dtype)], axis=0)
    marks = jnp.arange(blocks_here + 1, dtype=jnp.int32)
    marks = jnp.where(marks < blocks_here, marks, -1).astype(embedding.dtype)
    marks = jnp.broadcast_to(marks[:, None, None], (blocks_here + 1, 8, lanes))
    early_source = jnp.concatenate([narrow[:, :early_len], marks], axis=1)
    late_source = jnp.concatenate([embedding[:, EARLY_ROWS:], jnp.zeros((1, late_rows, feature_width), embedding.dtype)], axis=0)
    early_picked = jnp.take(early_source, pick, axis=0, mode="clip")
    late_picked = jnp.take(late_source, pick, axis=0, mode="clip")
    early_arrived = lax.all_to_all(early_picked, "node", split_axis=0, concat_axis=0, tiled=True)
    source = edge_ends // (blocks_here * block_rows)
    block_of = (edge_ends // block_rows) % blocks_here
    within = edge_ends % block_rows
    early = within < EARLY_ROWS
    early_position = source * slot_len + jnp.where(early, within, 0) * parts
    late_rows = block_rows - EARLY_ROWS
    late_spot = source * late_rows + within - EARLY_ROWS
    pair_ids = (pair_index - node_self * PAIRS_ROW).reshape(-1, 1)
    late_picked, early_arrived, early_position, late_spot, pair_ids = lax.optimization_barrier(
        (late_picked, early_arrived, early_position, late_spot, pair_ids))
    late_arrived = lax.all_to_all(late_picked, "node", split_axis=0, concat_axis=0, tiled=True)
    early_table = early_arrived.reshape(node_count * slot_len, lanes)
    late_table = late_arrived.reshape(node_count * late_rows, feature_width)
    sent = early_arrived[:, early_len, 0].astype(jnp.int32)
    located = jnp.any((source[..., None] == jnp.arange(node_count, dtype=jnp.int32))
                      & (block_of[..., None] == sent), axis=-1)
    early_mask = (located & early).T.astype(jnp.float32)
    late_index = jnp.where(located & ~early, late_spot, -1)
    partial = early_products(early_position, early_mask, early_table, w_first)
    edge_score, pair_cost = late_scores(late_index, partial, pair_ids, late_table, w_first, b_first, w_second,
                                        lax.axis_size("edge"))
    return (edge_score, pair_cost)


def solution(mesh):
    return jax.shard_map(
        body,
        mesh=mesh,
        in_specs=(
            P("node", None, None),
            P("edge", "node", None),
            P(None, ("node", "edge")),
            P(("node", "edge")),
            P(),
            P(),
            P(),
        ),
        out_specs=(P(("node", "edge")), P(("node", "edge"))),
        check_vma=False,
    )
```

```python
import functools

import jax
import jax.numpy as jnp
from jax import lax
from jax.experimental import pallas as pl
from jax.experimental.pallas import tpu as pltpu
from jax.sharding import PartitionSpec as P

PAIRS_ROW = 1024
TILE = 256
LATE_TILE = 256
EARLY_ROWS = 96


def gelu_tanh(x):
    return x * (0.5 * (1.0 + jnp.tanh(0.7978845608028654 * (x + 0.044715 * (x * x * x)))))


def early_kernel(edges, pos_ref, table, mask_ref, wt_ref, wb_ref, part_ref, buf, wide, sems):
    step = pl.program_id(0)
    steps = pl.num_programs(0)
    parts = buf.shape[2] // TILE
    lanes = buf.shape[3]

    def fetch(tile, slot):
        base = tile * TILE

        def one(r, carry):
            dst = pl.ds(pl.multiple_of(r * parts, parts), parts)
            for end in range(2):
                src = pl.ds(pl.multiple_of(pos_ref[end * edges + base + r], parts), parts)
                pltpu.make_async_copy(table.at[src], buf.at[end, slot, dst], sems.at[end, slot]).start()
            return carry

        lax.fori_loop(0, TILE, one, 0, unroll=8)

    @pl.when(step == 0)
    def _():
        fetch(0, 0)

    slot = step % 2

    @pl.when(step + 1 < steps)
    def _():
        fetch(step + 1, 1 - slot)

    for end in range(2):
        pltpu.make_async_copy(table.at[pl.ds(0, TILE * parts)], buf.at[end, slot], sems.at[end, slot]).wait()

    mask = mask_ref[...].T
    total = None
    for end, w_ref in ((0, wt_ref), (1, wb_ref)):
        wide[...] = buf[end, slot].astype(jnp.float32)
        keep = mask[:, end:end + 1] > 0
        for q in range(parts):
            piece = wide[pl.ds(q, TILE, stride=parts), :]
            piece = jnp.where(keep, piece, jnp.zeros_like(piece)).astype(jnp.bfloat16)
            term = jnp.dot(piece, w_ref[q * lanes:(q + 1) * lanes, :], preferred_element_type=jnp.float32)
            total = term if total is None else total + term
    part_ref[...] = total


def late_kernel(idx_ref, part_ref, table_ref, wt_ref, wb_ref, bias_ref, wo_ref, pid_ref, score_ref, cost_ref,
                pool, chunks, recv, send_sems, recv_sems):
    step = pl.program_id(0)
    steps = pl.num_programs(0)
    count = recv.shape[0]
    width = recv.shape[1]
    me = lax.axis_index("edge")
    node = lax.axis_index("node")
    barrier = pltpu.get_barrier_semaphore()

    @pl.when(step == 0)
    def _():
        def greet(k, carry):
            pl.semaphore_signal(barrier, 1, device_id=(node, (me + k) % count), device_id_type=pl.DeviceIdType.MESH)
            return carry

        lax.fori_loop(1, count, greet, 0)
        pool[...] = jnp.zeros_like(pool)

    idx = idx_ref[...].T
    rows = table_ref.shape[0]
    slots = lax.broadcasted_iota(jnp.int32, (LATE_TILE, rows), 1)
    preact = part_ref[...]
    for end, w_ref in ((0, wt_ref), (1, wb_ref)):
        onehot = (idx[:, end:end + 1] == slots).astype(table_ref.dtype)
        picked = jnp.dot(onehot, table_ref[...], preferred_element_type=jnp.float32).astype(table_ref.dtype)
        preact = preact + jnp.dot(picked, w_ref[...], preferred_element_type=jnp.float32)
    hidden = gelu_tanh(preact + bias_ref[...])
    scores = jnp.sum(hidden * wo_ref[0:1, :], axis=1, keepdims=True)
    score_ref[...] = jnp.broadcast_to(scores, (LATE_TILE, 128)).T[0:1, :]
    pair_range = lax.broadcasted_iota(jnp.int32, (LATE_TILE, PAIRS_ROW), 1)
    pooled = jnp.where(pid_ref[...] == pair_range, scores, 0.0)
    pool[...] += jnp.sum(pooled, axis=0, keepdims=True)

    @pl.when(step == steps - 1)
    def _():
        for t in range(count):
            chunks[t:t + 1, :] = pool[:, t * width:(t + 1) * width]
        pl.semaphore_wait(barrier, count - 1)

        def remote(target, slot):
            return pltpu.make_async_remote_copy(
                chunks.at[pl.ds(target, 1)], recv.at[pl.ds(slot, 1)], send_sems.at[target], recv_sems.at[slot],
                device_id=(node, target), device_id_type=pl.DeviceIdType.MESH)

        def send(k, carry):
            remote((me + k) % count, me).start()
            return carry

        lax.fori_loop(1, count, send, 0)

        def finish(k, carry):
            remote((me + k) % count, me).wait_send()
            source = (me + count - k) % count
            remote(source, source).wait_recv()
            return carry

        lax.fori_loop(1, count, finish, 0)
        here = lax.broadcasted_iota(jnp.int32, (count, width), 0)
        cost_ref[...] = jnp.sum(jnp.where(here == me, chunks[...], recv[...]), axis=0)


def early_products(position, mask, table, w_first):
    edges = position.shape[1]
    lanes = table.shape[1]
    width = w_first.shape[0] // 2
    parts = width // lanes
    hid = w_first.shape[1]
    grid_spec = pltpu.PrefetchScalarGridSpec(
        num_scalar_prefetch=1,
        grid=(edges // TILE,),
        in_specs=[
            pl.BlockSpec(memory_space=pl.ANY),
            pl.BlockSpec((2, TILE), lambda i, p: (0, i)),
            pl.BlockSpec((width, hid), lambda i, p: (0, 0)),
            pl.BlockSpec((width, hid), lambda i, p: (1, 0)),
        ],
        out_specs=pl.BlockSpec((TILE, hid), lambda i, p: (i, 0)),
        scratch_shapes=[
            pltpu.VMEM((2, 2, TILE * parts, lanes), table.dtype),
            pltpu.VMEM((TILE * parts, lanes), jnp.float32),
            pltpu.SemaphoreType.DMA((2, 2)),
        ],
    )
    return pl.pallas_call(
        functools.partial(early_kernel, edges),
        grid_spec=grid_spec,
        out_shape=jax.ShapeDtypeStruct((edges, hid), jnp.float32),
        compiler_params=pltpu.CompilerParams(dimension_semantics=("arbitrary",)),
        cost_estimate=pl.CostEstimate(
            flops=2 * edges * 2 * width * hid, transcendentals=0,
            bytes_accessed=2 * edges * width * table.dtype.itemsize + edges * hid * 4),
    )(position.reshape(2 * edges), table, mask, w_first, w_first)


def late_scores(late_index, partial, pair_ids, table, w_first, b_first, w_second, count):
    edges = late_index.shape[1]
    rows, width = table.shape
    hid = w_first.shape[1]
    share = PAIRS_ROW // count
    wo8 = jnp.broadcast_to(w_second.astype(jnp.float32)[None, :], (8, hid))
    scores, cost = pl.pallas_call(
        late_kernel,
        grid=(edges // LATE_TILE,),
        in_specs=[
            pl.BlockSpec((2, LATE_TILE), lambda i: (0, i)),
            pl.BlockSpec((LATE_TILE, hid), lambda i: (i, 0)),
            pl.BlockSpec((rows, width), lambda i: (0, 0)),
            pl.BlockSpec((width, hid), lambda i: (0, 0)),
            pl.BlockSpec((width, hid), lambda i: (1, 0)),
            pl.BlockSpec((1, hid), lambda i: (0, 0)),
            pl.BlockSpec((8, hid), lambda i: (0, 0)),
            pl.BlockSpec((LATE_TILE, 1), lambda i: (i, 0)),
        ],
        out_specs=[
            pl.BlockSpec((1, LATE_TILE), lambda i: (0, i)),
            pl.BlockSpec((share,), lambda i: (0,)),
        ],
        out_shape=[
            jax.ShapeDtypeStruct((1, edges), jnp.float32),
            jax.ShapeDtypeStruct((share,), jnp.float32),
        ],
        scratch_shapes=[
            pltpu.VMEM((1, PAIRS_ROW), jnp.float32),
            pltpu.VMEM((count, share), jnp.float32),
            pltpu.VMEM((count, share), jnp.float32),
            pltpu.SemaphoreType.DMA((count,)),
            pltpu.SemaphoreType.DMA((count,)),
        ],
        compiler_params=pltpu.CompilerParams(
            dimension_semantics=("arbitrary",), collective_id=0, has_side_effects=True),
        cost_estimate=pl.CostEstimate(
            flops=2 * edges * 2 * (rows + hid) * width, transcendentals=edges * hid,
            bytes_accessed=rows * width * 2 + edges * hid * 4),
    )(late_index, partial, table, w_first, w_first, b_first.reshape(1, hid), wo8, pair_ids)
    return scores.reshape(edges), cost


def body(embedding, send_list, edge_ends, pair_index, w_first, b_first, w_second):
    node_count = lax.axis_size("node")
    node_self = lax.axis_index("node")
    blocks_here = embedding.shape[0]
    block_rows = embedding.shape[1]
    feature_width = embedding.shape[2]
    lanes = 128
    parts = feature_width // lanes
    early_len = EARLY_ROWS * parts
    late_rows = block_rows - EARLY_ROWS
    slot_len = early_len + 8
    wanted = send_list[0, 0]
    pick = jnp.where(wanted >= 0, wanted, blocks_here)
    narrow = embedding.reshape(blocks_here, block_rows * parts, lanes)
    narrow = jnp.concatenate([narrow, jnp.zeros((1, block_rows * parts, lanes), embedding.dtype)], axis=0)
    marks = jnp.arange(blocks_here + 1, dtype=jnp.int32)
    marks = jnp.where(marks < blocks_here, marks, -1).astype(embedding.dtype)
    marks = jnp.broadcast_to(marks[:, None, None], (blocks_here + 1, 8, lanes))
    early_source = jnp.concatenate([narrow[:, :early_len], marks], axis=1)
    late_source = jnp.concatenate([embedding[:, EARLY_ROWS:], jnp.zeros((1, late_rows, feature_width), embedding.dtype)], axis=0)
    early_picked = jnp.take(early_source, pick, axis=0, mode="clip")
    late_picked = jnp.take(late_source, pick, axis=0, mode="clip")
    early_arrived = lax.all_to_all(early_picked, "node", split_axis=0, concat_axis=0, tiled=True)
    source = edge_ends // (blocks_here * block_rows)
    block_of = (edge_ends // block_rows) % blocks_here
    within = edge_ends % block_rows
    early = within < EARLY_ROWS
    early_position = source * slot_len + jnp.where(early, within, 0) * parts
    late_rows = block_rows - EARLY_ROWS
    late_spot = source * late_rows + within - EARLY_ROWS
    pair_ids = (pair_index - node_self * PAIRS_ROW).reshape(-1, 1)
    late_picked, early_arrived, early_position, late_spot, pair_ids = lax.optimization_barrier(
        (late_picked, early_arrived, early_position, late_spot, pair_ids))
    late_arrived = lax.all_to_all(late_picked, "node", split_axis=0, concat_axis=0, tiled=True)
    early_table = early_arrived.reshape(node_count * slot_len, lanes)
    late_table = late_arrived.reshape(node_count * late_rows, feature_width)
    sent = early_arrived[:, early_len, 0].astype(jnp.int32)
    located = jnp.any((source[..., None] == jnp.arange(node_count, dtype=jnp.int32))
                      & (block_of[..., None] == sent), axis=-1)
    early_mask = (located & early).astype(jnp.float32)
    late_index = jnp.where(located & ~early, late_spot, -1)
    partial = early_products(early_position, early_mask, early_table, w_first)
    edge_score, pair_cost = late_scores(late_index, partial, pair_ids, late_table, w_first, b_first, w_second,
                                        lax.axis_size("edge"))
    return (edge_score, pair_cost)


def solution(mesh):
    return jax.shard_map(
        body,
        mesh=mesh,
        in_specs=(
            P("node", None, None),
            P("edge", "node", None),
            P(None, ("node", "edge")),
            P(("node", "edge")),
            P(),
            P(),
            P(),
        ),
        out_specs=(P(("node", "edge")), P(("node", "edge"))),
        check_vma=False,
    )
```

```python
import functools

import jax
import jax.numpy as jnp
from jax import lax
from jax.experimental import pallas as pl
from jax.experimental.pallas import tpu as pltpu
from jax.sharding import PartitionSpec as P

PAIRS_ROW = 1024
TILE = 256
LATE_TILE = 256
EARLY_ROWS = 96


def gelu_tanh(x):
    return x * (0.5 * (1.0 + jnp.tanh(0.7978845608028654 * (x + 0.044715 * (x * x * x)))))


def early_kernel(edges, pos_ref, table, mask_ref, wt_ref, wb_ref, part_ref, buf, wide, sems):
    step = pl.program_id(0)
    steps = pl.num_programs(0)
    parts = buf.shape[2] // TILE
    lanes = buf.shape[3]

    def fetch(tile, slot):
        base = tile * TILE

        def one(r, carry):
            dst = pl.ds(pl.multiple_of(r * parts, parts), parts)
            for end in range(2):
                src = pl.ds(pl.multiple_of(pos_ref[end * edges + base + r], parts), parts)
                pltpu.make_async_copy(table.at[src], buf.at[end, slot, dst], sems.at[end, slot]).start()
            return carry

        lax.fori_loop(0, TILE, one, 0, unroll=8)

    @pl.when(step == 0)
    def _():
        fetch(0, 0)

    slot = step % 2

    @pl.when(step + 1 < steps)
    def _():
        fetch(step + 1, 1 - slot)

    for end in range(2):
        pltpu.make_async_copy(table.at[pl.ds(0, TILE * parts)], buf.at[end, slot], sems.at[end, slot]).wait()

    mask = mask_ref[...]
    total = None
    for end, w_ref in ((0, wt_ref), (1, wb_ref)):
        wide[...] = buf[end, slot].astype(jnp.float32)
        keep = mask[:, end:end + 1] > 0
        for q in range(parts):
            piece = wide[pl.ds(q, TILE, stride=parts), :]
            piece = jnp.where(keep, piece, jnp.zeros_like(piece)).astype(jnp.bfloat16)
            term = jnp.dot(piece, w_ref[q * lanes:(q + 1) * lanes, :], preferred_element_type=jnp.float32)
            total = term if total is None else total + term
    part_ref[...] = total


def late_kernel(idx_ref, part_ref, table_ref, wt_ref, wb_ref, bias_ref, wo_ref, pid_ref, score_ref, cost_ref,
                pool, chunks, recv, send_sems, recv_sems):
    step = pl.program_id(0)
    steps = pl.num_programs(0)
    count = recv.shape[0]
    width = recv.shape[1]
    me = lax.axis_index("edge")
    node = lax.axis_index("node")
    barrier = pltpu.get_barrier_semaphore()

    @pl.when(step == 0)
    def _():
        def greet(k, carry):
            pl.semaphore_signal(barrier, 1, device_id=(node, (me + k) % count), device_id_type=pl.DeviceIdType.MESH)
            return carry

        lax.fori_loop(1, count, greet, 0)
        pool[...] = jnp.zeros_like(pool)

    idx = idx_ref[...]
    rows = table_ref.shape[0]
    slots = lax.broadcasted_iota(jnp.int32, (LATE_TILE, rows), 1)
    preact = part_ref[...]
    for end, w_ref in ((0, wt_ref), (1, wb_ref)):
        onehot = (idx[:, end:end + 1] == slots).astype(table_ref.dtype)
        picked = jnp.dot(onehot, table_ref[...], preferred_element_type=jnp.float32).astype(table_ref.dtype)
        preact = preact + jnp.dot(picked, w_ref[...], preferred_element_type=jnp.float32)
    hidden = gelu_tanh(preact + bias_ref[...])
    scores = jnp.sum(hidden * wo_ref[0:1, :], axis=1, keepdims=True)
    score_ref[...] = jnp.broadcast_to(scores, (LATE_TILE, 128)).T[0:1, :]
    pair_range = lax.broadcasted_iota(jnp.int32, (LATE_TILE, PAIRS_ROW), 1)
    pooled = jnp.where(pid_ref[...] == pair_range, scores, 0.0)
    pool[...] += jnp.sum(pooled, axis=0, keepdims=True)

    @pl.when(step == steps - 1)
    def _():
        for t in range(count):
            chunks[t:t + 1, :] = pool[:, t * width:(t + 1) * width]
        pl.semaphore_wait(barrier, count - 1)

        def remote(target, slot):
            return pltpu.make_async_remote_copy(
                chunks.at[pl.ds(target, 1)], recv.at[pl.ds(slot, 1)], send_sems.at[target], recv_sems.at[slot],
                device_id=(node, target), device_id_type=pl.DeviceIdType.MESH)

        def send(k, carry):
            remote((me + k) % count, me).start()
            return carry

        lax.fori_loop(1, count, send, 0)

        def finish(k, carry):
            remote((me + k) % count, me).wait_send()
            source = (me + count - k) % count
            remote(source, source).wait_recv()
            return carry

        lax.fori_loop(1, count, finish, 0)
        here = lax.broadcasted_iota(jnp.int32, (count, width), 0)
        cost_ref[...] = jnp.sum(jnp.where(here == me, chunks[...], recv[...]), axis=0)


def early_products(position, mask, table, w_first):
    edges = position.shape[1]
    lanes = table.shape[1]
    width = w_first.shape[0] // 2
    parts = width // lanes
    hid = w_first.shape[1]
    grid_spec = pltpu.PrefetchScalarGridSpec(
        num_scalar_prefetch=1,
        grid=(edges // TILE,),
        in_specs=[
            pl.BlockSpec(memory_space=pl.ANY),
            pl.BlockSpec((TILE, 2), lambda i, p: (i, 0)),
            pl.BlockSpec((width, hid), lambda i, p: (0, 0)),
            pl.BlockSpec((width, hid), lambda i, p: (1, 0)),
        ],
        out_specs=pl.BlockSpec((TILE, hid), lambda i, p: (i, 0)),
        scratch_shapes=[
            pltpu.VMEM((2, 2, TILE * parts, lanes), table.dtype),
            pltpu.VMEM((TILE * parts, lanes), jnp.float32),
            pltpu.SemaphoreType.DMA((2, 2)),
        ],
    )
    return pl.pallas_call(
        functools.partial(early_kernel, edges),
        grid_spec=grid_spec,
        out_shape=jax.ShapeDtypeStruct((edges, hid), jnp.float32),
        compiler_params=pltpu.CompilerParams(dimension_semantics=("arbitrary",)),
        cost_estimate=pl.CostEstimate(
            flops=2 * edges * 2 * width * hid, transcendentals=0,
            bytes_accessed=2 * edges * width * table.dtype.itemsize + edges * hid * 4),
    )(position.reshape(2 * edges), table, mask, w_first, w_first)


def late_scores(late_index, partial, pair_ids, table, w_first, b_first, w_second, count):
    edges = late_index.shape[1]
    rows, width = table.shape
    hid = w_first.shape[1]
    share = PAIRS_ROW // count
    wo8 = jnp.broadcast_to(w_second.astype(jnp.float32)[None, :], (8, hid))
    scores, cost = pl.pallas_call(
        late_kernel,
        grid=(edges // LATE_TILE,),
        in_specs=[
            pl.BlockSpec((LATE_TILE, 2), lambda i: (i, 0)),
            pl.BlockSpec((LATE_TILE, hid), lambda i: (i, 0)),
            pl.BlockSpec((rows, width), lambda i: (0, 0)),
            pl.BlockSpec((width, hid), lambda i: (0, 0)),
            pl.BlockSpec((width, hid), lambda i: (1, 0)),
            pl.BlockSpec((1, hid), lambda i: (0, 0)),
            pl.BlockSpec((8, hid), lambda i: (0, 0)),
            pl.BlockSpec((LATE_TILE, 1), lambda i: (i, 0)),
        ],
        out_specs=[
            pl.BlockSpec((1, LATE_TILE), lambda i: (0, i)),
            pl.BlockSpec((share,), lambda i: (0,)),
        ],
        out_shape=[
            jax.ShapeDtypeStruct((1, edges), jnp.float32),
            jax.ShapeDtypeStruct((share,), jnp.float32),
        ],
        scratch_shapes=[
            pltpu.VMEM((1, PAIRS_ROW), jnp.float32),
            pltpu.VMEM((count, share), jnp.float32),
            pltpu.VMEM((count, share), jnp.float32),
            pltpu.SemaphoreType.DMA((count,)),
            pltpu.SemaphoreType.DMA((count,)),
        ],
        compiler_params=pltpu.CompilerParams(
            dimension_semantics=("arbitrary",), collective_id=0, has_side_effects=True),
        cost_estimate=pl.CostEstimate(
            flops=2 * edges * 2 * (rows + hid) * width, transcendentals=edges * hid,
            bytes_accessed=rows * width * 2 + edges * hid * 4),
    )(late_index.T, partial, table, w_first, w_first, b_first.reshape(1, hid), wo8, pair_ids)
    return scores.reshape(edges), cost


def body(embedding, send_list, edge_ends, pair_index, w_first, b_first, w_second):
    node_count = lax.axis_size("node")
    node_self = lax.axis_index("node")
    blocks_here = embedding.shape[0]
    block_rows = embedding.shape[1]
    feature_width = embedding.shape[2]
    lanes = 128
    parts = feature_width // lanes
    early_len = EARLY_ROWS * parts
    late_rows = block_rows - EARLY_ROWS
    slot_len = early_len
    wanted = send_list[0, 0]
    pick = jnp.where(wanted >= 0, wanted, blocks_here)
    narrow = embedding.reshape(blocks_here, block_rows * parts, lanes)
    narrow = jnp.concatenate([narrow, jnp.zeros((1, block_rows * parts, lanes), embedding.dtype)], axis=0)
    early_source = narrow[:, :early_len]
    late_source = jnp.concatenate([embedding[:, EARLY_ROWS:], jnp.zeros((1, late_rows, feature_width), embedding.dtype)], axis=0)
    early_picked = jnp.take(early_source, pick, axis=0, mode="clip")
    late_picked = jnp.take(late_source, pick, axis=0, mode="clip")
    early_arrived = lax.all_to_all(early_picked, "node", split_axis=0, concat_axis=0, tiled=True)
    lists = lax.all_gather(wanted, "node")
    sent = lax.dynamic_index_in_dim(lists, node_self, axis=1, keepdims=False)
    source = edge_ends // (blocks_here * block_rows)
    block_of = (edge_ends // block_rows) % blocks_here
    within = edge_ends % block_rows
    early = within < EARLY_ROWS
    early_position = source * slot_len + jnp.where(early, within, 0) * parts
    late_spot = source * late_rows + within - EARLY_ROWS
    pair_ids = (pair_index - node_self * PAIRS_ROW).reshape(-1, 1)
    located = jnp.any((source[..., None] == jnp.arange(node_count, dtype=jnp.int32))
                      & (block_of[..., None] == sent), axis=-1)
    early_mask = (located & early).T.astype(jnp.float32)
    late_index = jnp.where(located & ~early, late_spot, -1)
    late_picked, early_arrived, early_position, early_mask, late_index, pair_ids = lax.optimization_barrier(
        (late_picked, early_arrived, early_position, early_mask, late_index, pair_ids))
    late_arrived = lax.all_to_all(late_picked, "node", split_axis=0, concat_axis=0, tiled=True)
    early_table = early_arrived.reshape(node_count * slot_len, lanes)
    late_table = late_arrived.reshape(node_count * late_rows, feature_width)
    partial = early_products(early_position, early_mask, early_table, w_first)
    edge_score, pair_cost = late_scores(late_index, partial, pair_ids, late_table, w_first, b_first, w_second,
                                        lax.axis_size("edge"))
    return (edge_score, pair_cost)


def solution(mesh):
    return jax.shard_map(
        body,
        mesh=mesh,
        in_specs=(
            P("node", None, None),
            P("edge", "node", None),
            P(None, ("node", "edge")),
            P(("node", "edge")),
            P(),
            P(),
            P(),
        ),
        out_specs=(P(("node", "edge")), P(("node", "edge"))),
        check_vma=False,
    )
```

```python
import functools

import jax
import jax.numpy as jnp
from jax import lax
from jax.experimental import pallas as pl
from jax.experimental.pallas import tpu as pltpu
from jax.sharding import PartitionSpec as P

PAIRS_ROW = 1024
TILE = 256
LATE_TILE = 512
EARLY_ROWS = 96


def gelu_tanh(x):
    return x * (0.5 * (1.0 + jnp.tanh(0.7978845608028654 * (x + 0.044715 * (x * x * x)))))


def early_kernel(edges, pos_ref, table, mask_ref, wt_ref, wb_ref, part_ref, buf, wide, sems):
    step = pl.program_id(0)
    steps = pl.num_programs(0)
    parts = buf.shape[2] // TILE
    lanes = buf.shape[3]

    def fetch(tile, slot):
        base = tile * TILE

        def one(r, carry):
            dst = pl.ds(pl.multiple_of(r * parts, parts), parts)
            for end in range(2):
                src = pl.ds(pl.multiple_of(pos_ref[end * edges + base + r], parts), parts)
                pltpu.make_async_copy(table.at[src], buf.at[end, slot, dst], sems.at[end, slot]).start()
            return carry

        lax.fori_loop(0, TILE, one, 0, unroll=8)

    @pl.when(step == 0)
    def _():
        fetch(0, 0)

    slot = step % 2

    @pl.when(step + 1 < steps)
    def _():
        fetch(step + 1, 1 - slot)

    for end in range(2):
        pltpu.make_async_copy(table.at[pl.ds(0, TILE * parts)], buf.at[end, slot], sems.at[end, slot]).wait()

    mask = mask_ref[...]
    total = None
    for end, w_ref in ((0, wt_ref), (1, wb_ref)):
        wide[...] = buf[end, slot].astype(jnp.float32)
        keep = mask[:, end:end + 1] > 0
        for q in range(parts):
            piece = wide[pl.ds(q, TILE, stride=parts), :]
            piece = jnp.where(keep, piece, jnp.zeros_like(piece)).astype(jnp.bfloat16)
            term = jnp.dot(piece, w_ref[q * lanes:(q + 1) * lanes, :], preferred_element_type=jnp.float32)
            total = term if total is None else total + term
    part_ref[...] = total


def late_kernel(idx_ref, part_ref, table_ref, wt_ref, wb_ref, bias_ref, wo_ref, pid_ref, score_ref, cost_ref,
                pool, chunks, recv, send_sems, recv_sems):
    step = pl.program_id(0)
    steps = pl.num_programs(0)
    count = recv.shape[0]
    width = recv.shape[1]
    me = lax.axis_index("edge")
    node = lax.axis_index("node")
    barrier = pltpu.get_barrier_semaphore()

    @pl.when(step == 0)
    def _():
        def greet(k, carry):
            pl.semaphore_signal(barrier, 1, device_id=(node, (me + k) % count), device_id_type=pl.DeviceIdType.MESH)
            return carry

        lax.fori_loop(1, count, greet, 0)
        pool[...] = jnp.zeros_like(pool)

    idx = idx_ref[...]
    rows = table_ref.shape[0]
    slots = lax.broadcasted_iota(jnp.int32, (LATE_TILE, rows), 1)
    preact = part_ref[...]
    for end, w_ref in ((0, wt_ref), (1, wb_ref)):
        onehot = (idx[:, end:end + 1] == slots).astype(table_ref.dtype)
        picked = jnp.dot(onehot, table_ref[...], preferred_element_type=jnp.float32).astype(table_ref.dtype)
        preact = preact + jnp.dot(picked, w_ref[...], preferred_element_type=jnp.float32)
    hidden = gelu_tanh(preact + bias_ref[...])
    scores = jnp.sum(hidden * wo_ref[0:1, :], axis=1, keepdims=True)
    score_ref[...] = jnp.broadcast_to(scores, (LATE_TILE, 128)).T[0:1, :]
    pair_range = lax.broadcasted_iota(jnp.int32, (LATE_TILE, PAIRS_ROW), 1)
    pooled = jnp.where(pid_ref[...] == pair_range, scores, 0.0)
    pool[...] += jnp.sum(pooled, axis=0, keepdims=True)

    @pl.when(step == steps - 1)
    def _():
        for t in range(count):
            chunks[t:t + 1, :] = pool[:, t * width:(t + 1) * width]
        pl.semaphore_wait(barrier, count - 1)

        def remote(target, slot):
            return pltpu.make_async_remote_copy(
                chunks.at[pl.ds(target, 1)], recv.at[pl.ds(slot, 1)], send_sems.at[target], recv_sems.at[slot],
                device_id=(node, target), device_id_type=pl.DeviceIdType.MESH)

        def send(k, carry):
            remote((me + k) % count, me).start()
            return carry

        lax.fori_loop(1, count, send, 0)

        def finish(k, carry):
            remote((me + k) % count, me).wait_send()
            source = (me + count - k) % count
            remote(source, source).wait_recv()
            return carry

        lax.fori_loop(1, count, finish, 0)
        here = lax.broadcasted_iota(jnp.int32, (count, width), 0)
        cost_ref[...] = jnp.sum(jnp.where(here == me, chunks[...], recv[...]), axis=0)


def early_products(position, mask, table, w_first):
    edges = position.shape[1]
    lanes = table.shape[1]
    width = w_first.shape[0] // 2
    parts = width // lanes
    hid = w_first.shape[1]
    grid_spec = pltpu.PrefetchScalarGridSpec(
        num_scalar_prefetch=1,
        grid=(edges // TILE,),
        in_specs=[
            pl.BlockSpec(memory_space=pl.ANY),
            pl.BlockSpec((TILE, 2), lambda i, p: (i, 0)),
            pl.BlockSpec((width, hid), lambda i, p: (0, 0)),
            pl.BlockSpec((width, hid), lambda i, p: (1, 0)),
        ],
        out_specs=pl.BlockSpec((TILE, hid), lambda i, p: (i, 0)),
        scratch_shapes=[
            pltpu.VMEM((2, 2, TILE * parts, lanes), table.dtype),
            pltpu.VMEM((TILE * parts, lanes), jnp.float32),
            pltpu.SemaphoreType.DMA((2, 2)),
        ],
    )
    return pl.pallas_call(
        functools.partial(early_kernel, edges),
        grid_spec=grid_spec,
        out_shape=jax.ShapeDtypeStruct((edges, hid), jnp.float32),
        compiler_params=pltpu.CompilerParams(dimension_semantics=("arbitrary",)),
        cost_estimate=pl.CostEstimate(
            flops=2 * edges * 2 * width * hid, transcendentals=0,
            bytes_accessed=2 * edges * width * table.dtype.itemsize + edges * hid * 4),
    )(position.reshape(2 * edges), table, mask, w_first, w_first)


def late_scores(late_index, partial, pair_ids, table, w_first, b_first, w_second, count):
    edges = late_index.shape[1]
    rows, width = table.shape
    hid = w_first.shape[1]
    share = PAIRS_ROW // count
    wo8 = jnp.broadcast_to(w_second.astype(jnp.float32)[None, :], (8, hid))
    scores, cost = pl.pallas_call(
        late_kernel,
        grid=(edges // LATE_TILE,),
        in_specs=[
            pl.BlockSpec((LATE_TILE, 2), lambda i: (i, 0)),
            pl.BlockSpec((LATE_TILE, hid), lambda i: (i, 0)),
            pl.BlockSpec((rows, width), lambda i: (0, 0)),
            pl.BlockSpec((width, hid), lambda i: (0, 0)),
            pl.BlockSpec((width, hid), lambda i: (1, 0)),
            pl.BlockSpec((1, hid), lambda i: (0, 0)),
            pl.BlockSpec((8, hid), lambda i: (0, 0)),
            pl.BlockSpec((LATE_TILE, 1), lambda i: (i, 0)),
        ],
        out_specs=[
            pl.BlockSpec((1, LATE_TILE), lambda i: (0, i)),
            pl.BlockSpec((share,), lambda i: (0,)),
        ],
        out_shape=[
            jax.ShapeDtypeStruct((1, edges), jnp.float32),
            jax.ShapeDtypeStruct((share,), jnp.float32),
        ],
        scratch_shapes=[
            pltpu.VMEM((1, PAIRS_ROW), jnp.float32),
            pltpu.VMEM((count, share), jnp.float32),
            pltpu.VMEM((count, share), jnp.float32),
            pltpu.SemaphoreType.DMA((count,)),
            pltpu.SemaphoreType.DMA((count,)),
        ],
        compiler_params=pltpu.CompilerParams(
            dimension_semantics=("arbitrary",), collective_id=0, has_side_effects=True),
        cost_estimate=pl.CostEstimate(
            flops=2 * edges * 2 * (rows + hid) * width, transcendentals=edges * hid,
            bytes_accessed=rows * width * 2 + edges * hid * 4),
    )(late_index.T, partial, table, w_first, w_first, b_first.reshape(1, hid), wo8, pair_ids)
    return scores.reshape(edges), cost


def body(embedding, send_list, edge_ends, pair_index, w_first, b_first, w_second):
    node_count = lax.axis_size("node")
    node_self = lax.axis_index("node")
    blocks_here = embedding.shape[0]
    block_rows = embedding.shape[1]
    feature_width = embedding.shape[2]
    lanes = 128
    parts = feature_width // lanes
    early_len = EARLY_ROWS * parts
    late_rows = block_rows - EARLY_ROWS
    slot_len = early_len + 8
    wanted = send_list[0, 0]
    pick = jnp.where(wanted >= 0, wanted, blocks_here)
    narrow = embedding.reshape(blocks_here, block_rows * parts, lanes)
    narrow = jnp.concatenate([narrow, jnp.zeros((1, block_rows * parts, lanes), embedding.dtype)], axis=0)
    marks = jnp.arange(blocks_here + 1, dtype=jnp.int32)
    marks = jnp.where(marks < blocks_here, marks, -1).astype(embedding.dtype)
    marks = jnp.broadcast_to(marks[:, None, None], (blocks_here + 1, 8, lanes))
    early_source = jnp.concatenate([narrow[:, :early_len], marks], axis=1)
    late_source = jnp.concatenate([embedding[:, EARLY_ROWS:], jnp.zeros((1, late_rows, feature_width), embedding.dtype)], axis=0)
    early_picked = jnp.take(early_source, pick, axis=0, mode="clip")
    late_picked = jnp.take(late_source, pick, axis=0, mode="clip")
    early_arrived = lax.all_to_all(early_picked, "node", split_axis=0, concat_axis=0, tiled=True)
    source = edge_ends // (blocks_here * block_rows)
    block_of = (edge_ends // block_rows) % blocks_here
    within = edge_ends % block_rows
    early = within < EARLY_ROWS
    early_position = source * slot_len + jnp.where(early, within, 0) * parts
    late_rows = block_rows - EARLY_ROWS
    late_spot = source * late_rows + within - EARLY_ROWS
    pair_ids = (pair_index - node_self * PAIRS_ROW).reshape(-1, 1)
    late_picked, early_arrived, early_position, late_spot, pair_ids = lax.optimization_barrier(
        (late_picked, early_arrived, early_position, late_spot, pair_ids))
    late_arrived = lax.all_to_all(late_picked, "node", split_axis=0, concat_axis=0, tiled=True)
    early_table = early_arrived.reshape(node_count * slot_len, lanes)
    late_table = late_arrived.reshape(node_count * late_rows, feature_width)
    sent = early_arrived[:, early_len, 0].astype(jnp.int32)
    located = jnp.any((source[..., None] == jnp.arange(node_count, dtype=jnp.int32))
                      & (block_of[..., None] == sent), axis=-1)
    early_mask = (located & early).T.astype(jnp.float32)
    late_index = jnp.where(located & ~early, late_spot, -1)
    partial = early_products(early_position, early_mask, early_table, w_first)
    edge_score, pair_cost = late_scores(late_index, partial, pair_ids, late_table, w_first, b_first, w_second,
                                        lax.axis_size("edge"))
    return (edge_score, pair_cost)


def solution(mesh):
    return jax.shard_map(
        body,
        mesh=mesh,
        in_specs=(
            P("node", None, None),
            P("edge", "node", None),
            P(None, ("node", "edge")),
            P(("node", "edge")),
            P(),
            P(),
            P(),
        ),
        out_specs=(P(("node", "edge")), P(("node", "edge"))),
        check_vma=False,
    )
```

```python
import functools

import jax
import jax.numpy as jnp
from jax import lax
from jax.experimental import pallas as pl
from jax.experimental.pallas import tpu as pltpu
from jax.sharding import PartitionSpec as P

PAIRS_ROW = 1024
TILE = 256
LATE_TILE = 1024
EARLY_ROWS = 96


def gelu_tanh(x):
    return x * (0.5 * (1.0 + jnp.tanh(0.7978845608028654 * (x + 0.044715 * (x * x * x)))))


def early_kernel(edges, pos_ref, table, mask_ref, wt_ref, wb_ref, part_ref, buf, wide, sems):
    step = pl.program_id(0)
    steps = pl.num_programs(0)
    parts = buf.shape[2] // TILE
    lanes = buf.shape[3]

    def fetch(tile, slot):
        base = tile * TILE

        def one(r, carry):
            dst = pl.ds(pl.multiple_of(r * parts, parts), parts)
            for end in range(2):
                src = pl.ds(pl.multiple_of(pos_ref[end * edges + base + r], parts), parts)
                pltpu.make_async_copy(table.at[src], buf.at[end, slot, dst], sems.at[end, slot]).start()
            return carry

        lax.fori_loop(0, TILE, one, 0, unroll=8)

    @pl.when(step == 0)
    def _():
        fetch(0, 0)

    slot = step % 2

    @pl.when(step + 1 < steps)
    def _():
        fetch(step + 1, 1 - slot)

    for end in range(2):
        pltpu.make_async_copy(table.at[pl.ds(0, TILE * parts)], buf.at[end, slot], sems.at[end, slot]).wait()

    mask = mask_ref[...]
    total = None
    for end, w_ref in ((0, wt_ref), (1, wb_ref)):
        wide[...] = buf[end, slot].astype(jnp.float32)
        keep = mask[:, end:end + 1] > 0
        for q in range(parts):
            piece = wide[pl.ds(q, TILE, stride=parts), :]
            piece = jnp.where(keep, piece, jnp.zeros_like(piece)).astype(jnp.bfloat16)
            term = jnp.dot(piece, w_ref[q * lanes:(q + 1) * lanes, :], preferred_element_type=jnp.float32)
            total = term if total is None else total + term
    part_ref[...] = total


def late_kernel(idx_ref, part_ref, table_ref, wt_ref, wb_ref, bias_ref, wo_ref, pid_ref, score_ref, cost_ref,
                pool, chunks, recv, send_sems, recv_sems):
    step = pl.program_id(0)
    steps = pl.num_programs(0)
    count = recv.shape[0]
    width = recv.shape[1]
    me = lax.axis_index("edge")
    node = lax.axis_index("node")
    barrier = pltpu.get_barrier_semaphore()

    @pl.when(step == 0)
    def _():
        def greet(k, carry):
            pl.semaphore_signal(barrier, 1, device_id=(node, (me + k) % count), device_id_type=pl.DeviceIdType.MESH)
            return carry

        lax.fori_loop(1, count, greet, 0)
        pool[...] = jnp.zeros_like(pool)

    idx = idx_ref[...]
    rows = table_ref.shape[0]
    slots = lax.broadcasted_iota(jnp.int32, (LATE_TILE, rows), 1)
    preact = part_ref[...]
    for end, w_ref in ((0, wt_ref), (1, wb_ref)):
        onehot = (idx[:, end:end + 1] == slots).astype(table_ref.dtype)
        picked = jnp.dot(onehot, table_ref[...], preferred_element_type=jnp.float32).astype(table_ref.dtype)
        preact = preact + jnp.dot(picked, w_ref[...], preferred_element_type=jnp.float32)
    hidden = gelu_tanh(preact + bias_ref[...])
    scores = jnp.sum(hidden * wo_ref[0:1, :], axis=1, keepdims=True)
    score_ref[...] = jnp.broadcast_to(scores, (LATE_TILE, 128)).T[0:1, :]
    pair_range = lax.broadcasted_iota(jnp.int32, (LATE_TILE, PAIRS_ROW), 1)
    pooled = jnp.where(pid_ref[...] == pair_range, scores, 0.0)
    pool[...] += jnp.sum(pooled, axis=0, keepdims=True)

    @pl.when(step == steps - 1)
    def _():
        for t in range(count):
            chunks[t:t + 1, :] = pool[:, t * width:(t + 1) * width]
        pl.semaphore_wait(barrier, count - 1)

        def remote(target, slot):
            return pltpu.make_async_remote_copy(
                chunks.at[pl.ds(target, 1)], recv.at[pl.ds(slot, 1)], send_sems.at[target], recv_sems.at[slot],
                device_id=(node, target), device_id_type=pl.DeviceIdType.MESH)

        def send(k, carry):
            remote((me + k) % count, me).start()
            return carry

        lax.fori_loop(1, count, send, 0)

        def finish(k, carry):
            remote((me + k) % count, me).wait_send()
            source = (me + count - k) % count
            remote(source, source).wait_recv()
            return carry

        lax.fori_loop(1, count, finish, 0)
        here = lax.broadcasted_iota(jnp.int32, (count, width), 0)
        cost_ref[...] = jnp.sum(jnp.where(here == me, chunks[...], recv[...]), axis=0)


def early_products(position, mask, table, w_first):
    edges = position.shape[1]
    lanes = table.shape[1]
    width = w_first.shape[0] // 2
    parts = width // lanes
    hid = w_first.shape[1]
    grid_spec = pltpu.PrefetchScalarGridSpec(
        num_scalar_prefetch=1,
        grid=(edges // TILE,),
        in_specs=[
            pl.BlockSpec(memory_space=pl.ANY),
            pl.BlockSpec((TILE, 2), lambda i, p: (i, 0)),
            pl.BlockSpec((width, hid), lambda i, p: (0, 0)),
            pl.BlockSpec((width, hid), lambda i, p: (1, 0)),
        ],
        out_specs=pl.BlockSpec((TILE, hid), lambda i, p: (i, 0)),
        scratch_shapes=[
            pltpu.VMEM((2, 2, TILE * parts, lanes), table.dtype),
            pltpu.VMEM((TILE * parts, lanes), jnp.float32),
            pltpu.SemaphoreType.DMA((2, 2)),
        ],
    )
    return pl.pallas_call(
        functools.partial(early_kernel, edges),
        grid_spec=grid_spec,
        out_shape=jax.ShapeDtypeStruct((edges, hid), jnp.float32),
        compiler_params=pltpu.CompilerParams(dimension_semantics=("arbitrary",)),
        cost_estimate=pl.CostEstimate(
            flops=2 * edges * 2 * width * hid, transcendentals=0,
            bytes_accessed=2 * edges * width * table.dtype.itemsize + edges * hid * 4),
    )(position.reshape(2 * edges), table, mask, w_first, w_first)


def late_scores(late_index, partial, pair_ids, table, w_first, b_first, w_second, count):
    edges = late_index.shape[1]
    rows, width = table.shape
    hid = w_first.shape[1]
    share = PAIRS_ROW // count
    wo8 = jnp.broadcast_to(w_second.astype(jnp.float32)[None, :], (8, hid))
    scores, cost = pl.pallas_call(
        late_kernel,
        grid=(edges // LATE_TILE,),
        in_specs=[
            pl.BlockSpec((LATE_TILE, 2), lambda i: (i, 0)),
            pl.BlockSpec((LATE_TILE, hid), lambda i: (i, 0)),
            pl.BlockSpec((rows, width), lambda i: (0, 0)),
            pl.BlockSpec((width, hid), lambda i: (0, 0)),
            pl.BlockSpec((width, hid), lambda i: (1, 0)),
            pl.BlockSpec((1, hid), lambda i: (0, 0)),
            pl.BlockSpec((8, hid), lambda i: (0, 0)),
            pl.BlockSpec((LATE_TILE, 1), lambda i: (i, 0)),
        ],
        out_specs=[
            pl.BlockSpec((1, LATE_TILE), lambda i: (0, i)),
            pl.BlockSpec((share,), lambda i: (0,)),
        ],
        out_shape=[
            jax.ShapeDtypeStruct((1, edges), jnp.float32),
            jax.ShapeDtypeStruct((share,), jnp.float32),
        ],
        scratch_shapes=[
            pltpu.VMEM((1, PAIRS_ROW), jnp.float32),
            pltpu.VMEM((count, share), jnp.float32),
            pltpu.VMEM((count, share), jnp.float32),
            pltpu.SemaphoreType.DMA((count,)),
            pltpu.SemaphoreType.DMA((count,)),
        ],
        compiler_params=pltpu.CompilerParams(
            dimension_semantics=("arbitrary",), collective_id=0, has_side_effects=True),
        cost_estimate=pl.CostEstimate(
            flops=2 * edges * 2 * (rows + hid) * width, transcendentals=edges * hid,
            bytes_accessed=rows * width * 2 + edges * hid * 4),
    )(late_index.T, partial, table, w_first, w_first, b_first.reshape(1, hid), wo8, pair_ids)
    return scores.reshape(edges), cost


def body(embedding, send_list, edge_ends, pair_index, w_first, b_first, w_second):
    node_count = lax.axis_size("node")
    node_self = lax.axis_index("node")
    blocks_here = embedding.shape[0]
    block_rows = embedding.shape[1]
    feature_width = embedding.shape[2]
    lanes = 128
    parts = feature_width // lanes
    early_len = EARLY_ROWS * parts
    late_rows = block_rows - EARLY_ROWS
    slot_len = early_len + 8
    wanted = send_list[0, 0]
    pick = jnp.where(wanted >= 0, wanted, blocks_here)
    narrow = embedding.reshape(blocks_here, block_rows * parts, lanes)
    narrow = jnp.concatenate([narrow, jnp.zeros((1, block_rows * parts, lanes), embedding.dtype)], axis=0)
    marks = jnp.arange(blocks_here + 1, dtype=jnp.int32)
    marks = jnp.where(marks < blocks_here, marks, -1).astype(embedding.dtype)
    marks = jnp.broadcast_to(marks[:, None, None], (blocks_here + 1, 8, lanes))
    early_source = jnp.concatenate([narrow[:, :early_len], marks], axis=1)
    late_source = jnp.concatenate([embedding[:, EARLY_ROWS:], jnp.zeros((1, late_rows, feature_width), embedding.dtype)], axis=0)
    early_picked = jnp.take(early_source, pick, axis=0, mode="clip")
    late_picked = jnp.take(late_source, pick, axis=0, mode="clip")
    early_arrived = lax.all_to_all(early_picked, "node", split_axis=0, concat_axis=0, tiled=True)
    source = edge_ends // (blocks_here * block_rows)
    block_of = (edge_ends // block_rows) % blocks_here
    within = edge_ends % block_rows
    early = within < EARLY_ROWS
    early_position = source * slot_len + jnp.where(early, within, 0) * parts
    late_rows = block_rows - EARLY_ROWS
    late_spot = source * late_rows + within - EARLY_ROWS
    pair_ids = (pair_index - node_self * PAIRS_ROW).reshape(-1, 1)
    late_picked, early_arrived, early_position, late_spot, pair_ids = lax.optimization_barrier(
        (late_picked, early_arrived, early_position, late_spot, pair_ids))
    late_arrived = lax.all_to_all(late_picked, "node", split_axis=0, concat_axis=0, tiled=True)
    early_table = early_arrived.reshape(node_count * slot_len, lanes)
    late_table = late_arrived.reshape(node_count * late_rows, feature_width)
    sent = early_arrived[:, early_len, 0].astype(jnp.int32)
    located = jnp.any((source[..., None] == jnp.arange(node_count, dtype=jnp.int32))
                      & (block_of[..., None] == sent), axis=-1)
    early_mask = (located & early).T.astype(jnp.float32)
    late_index = jnp.where(located & ~early, late_spot, -1)
    partial = early_products(early_position, early_mask, early_table, w_first)
    edge_score, pair_cost = late_scores(late_index, partial, pair_ids, late_table, w_first, b_first, w_second,
                                        lax.axis_size("edge"))
    return (edge_score, pair_cost)


def solution(mesh):
    return jax.shard_map(
        body,
        mesh=mesh,
        in_specs=(
            P("node", None, None),
            P("edge", "node", None),
            P(None, ("node", "edge")),
            P(("node", "edge")),
            P(),
            P(),
            P(),
        ),
        out_specs=(P(("node", "edge")), P(("node", "edge"))),
        check_vma=False,
    )
```

```python
import functools

import jax
import jax.numpy as jnp
from jax import lax
from jax.experimental import pallas as pl
from jax.experimental.pallas import tpu as pltpu
from jax.sharding import PartitionSpec as P

PAIRS_ROW = 1024
TILE = 512
LATE_TILE = 512
EARLY_ROWS = 96


def gelu_tanh(x):
    return x * (0.5 * (1.0 + jnp.tanh(0.7978845608028654 * (x + 0.044715 * (x * x * x)))))


def early_kernel(edges, pos_ref, table, mask_ref, wt_ref, wb_ref, part_ref, buf, wide, sems):
    step = pl.program_id(0)
    steps = pl.num_programs(0)
    parts = buf.shape[2] // TILE
    lanes = buf.shape[3]

    def fetch(tile, slot):
        base = tile * TILE

        def one(r, carry):
            dst = pl.ds(pl.multiple_of(r * parts, parts), parts)
            for end in range(2):
                src = pl.ds(pl.multiple_of(pos_ref[end * edges + base + r], parts), parts)
                pltpu.make_async_copy(table.at[src], buf.at[end, slot, dst], sems.at[end, slot]).start()
            return carry

        lax.fori_loop(0, TILE, one, 0, unroll=8)

    @pl.when(step == 0)
    def _():
        fetch(0, 0)

    slot = step % 2

    @pl.when(step + 1 < steps)
    def _():
        fetch(step + 1, 1 - slot)

    for end in range(2):
        pltpu.make_async_copy(table.at[pl.ds(0, TILE * parts)], buf.at[end, slot], sems.at[end, slot]).wait()

    mask = mask_ref[...]
    total = None
    for end, w_ref in ((0, wt_ref), (1, wb_ref)):
        wide[...] = buf[end, slot].astype(jnp.float32)
        keep = mask[:, end:end + 1] > 0
        for q in range(parts):
            piece = wide[pl.ds(q, TILE, stride=parts), :]
            piece = jnp.where(keep, piece, jnp.zeros_like(piece)).astype(jnp.bfloat16)
            term = jnp.dot(piece, w_ref[q * lanes:(q + 1) * lanes, :], preferred_element_type=jnp.float32)
            total = term if total is None else total + term
    part_ref[...] = total


def late_kernel(idx_ref, part_ref, table_ref, wt_ref, wb_ref, bias_ref, wo_ref, pid_ref, score_ref, cost_ref,
                pool, chunks, recv, send_sems, recv_sems):
    step = pl.program_id(0)
    steps = pl.num_programs(0)
    count = recv.shape[0]
    width = recv.shape[1]
    me = lax.axis_index("edge")
    node = lax.axis_index("node")
    barrier = pltpu.get_barrier_semaphore()

    @pl.when(step == 0)
    def _():
        def greet(k, carry):
            pl.semaphore_signal(barrier, 1, device_id=(node, (me + k) % count), device_id_type=pl.DeviceIdType.MESH)
            return carry

        lax.fori_loop(1, count, greet, 0)
        pool[...] = jnp.zeros_like(pool)

    idx = idx_ref[...]
    rows = table_ref.shape[0]
    slots = lax.broadcasted_iota(jnp.int32, (LATE_TILE, rows), 1)
    preact = part_ref[...]
    for end, w_ref in ((0, wt_ref), (1, wb_ref)):
        onehot = (idx[:, end:end + 1] == slots).astype(table_ref.dtype)
        picked = jnp.dot(onehot, table_ref[...], preferred_element_type=jnp.float32).astype(table_ref.dtype)
        preact = preact + jnp.dot(picked, w_ref[...], preferred_element_type=jnp.float32)
    hidden = gelu_tanh(preact + bias_ref[...])
    scores = jnp.sum(hidden * wo_ref[0:1, :], axis=1, keepdims=True)
    score_ref[...] = jnp.broadcast_to(scores, (LATE_TILE, 128)).T[0:1, :]
    pair_range = lax.broadcasted_iota(jnp.int32, (LATE_TILE, PAIRS_ROW), 1)
    pooled = jnp.where(pid_ref[...] == pair_range, scores, 0.0)
    pool[...] += jnp.sum(pooled, axis=0, keepdims=True)

    @pl.when(step == steps - 1)
    def _():
        for t in range(count):
            chunks[t:t + 1, :] = pool[:, t * width:(t + 1) * width]
        pl.semaphore_wait(barrier, count - 1)

        def remote(target, slot):
            return pltpu.make_async_remote_copy(
                chunks.at[pl.ds(target, 1)], recv.at[pl.ds(slot, 1)], send_sems.at[target], recv_sems.at[slot],
                device_id=(node, target), device_id_type=pl.DeviceIdType.MESH)

        def send(k, carry):
            remote((me + k) % count, me).start()
            return carry

        lax.fori_loop(1, count, send, 0)

        def finish(k, carry):
            remote((me + k) % count, me).wait_send()
            source = (me + count - k) % count
            remote(source, source).wait_recv()
            return carry

        lax.fori_loop(1, count, finish, 0)
        here = lax.broadcasted_iota(jnp.int32, (count, width), 0)
        cost_ref[...] = jnp.sum(jnp.where(here == me, chunks[...], recv[...]), axis=0)


def early_products(position, mask, table, w_first):
    edges = position.shape[1]
    lanes = table.shape[1]
    width = w_first.shape[0] // 2
    parts = width // lanes
    hid = w_first.shape[1]
    grid_spec = pltpu.PrefetchScalarGridSpec(
        num_scalar_prefetch=1,
        grid=(edges // TILE,),
        in_specs=[
            pl.BlockSpec(memory_space=pl.ANY),
            pl.BlockSpec((TILE, 2), lambda i, p: (i, 0)),
            pl.BlockSpec((width, hid), lambda i, p: (0, 0)),
            pl.BlockSpec((width, hid), lambda i, p: (1, 0)),
        ],
        out_specs=pl.BlockSpec((TILE, hid), lambda i, p: (i, 0)),
        scratch_shapes=[
            pltpu.VMEM((2, 2, TILE * parts, lanes), table.dtype),
            pltpu.VMEM((TILE * parts, lanes), jnp.float32),
            pltpu.SemaphoreType.DMA((2, 2)),
        ],
    )
    return pl.pallas_call(
        functools.partial(early_kernel, edges),
        grid_spec=grid_spec,
        out_shape=jax.ShapeDtypeStruct((edges, hid), jnp.float32),
        compiler_params=pltpu.CompilerParams(dimension_semantics=("arbitrary",)),
        cost_estimate=pl.CostEstimate(
            flops=2 * edges * 2 * width * hid, transcendentals=0,
            bytes_accessed=2 * edges * width * table.dtype.itemsize + edges * hid * 4),
    )(position.reshape(2 * edges), table, mask, w_first, w_first)


def late_scores(late_index, partial, pair_ids, table, w_first, b_first, w_second, count):
    edges = late_index.shape[1]
    rows, width = table.shape
    hid = w_first.shape[1]
    share = PAIRS_ROW // count
    wo8 = jnp.broadcast_to(w_second.astype(jnp.float32)[None, :], (8, hid))
    scores, cost = pl.pallas_call(
        late_kernel,
        grid=(edges // LATE_TILE,),
        in_specs=[
            pl.BlockSpec((LATE_TILE, 2), lambda i: (i, 0)),
            pl.BlockSpec((LATE_TILE, hid), lambda i: (i, 0)),
            pl.BlockSpec((rows, width), lambda i: (0, 0)),
            pl.BlockSpec((width, hid), lambda i: (0, 0)),
            pl.BlockSpec((width, hid), lambda i: (1, 0)),
            pl.BlockSpec((1, hid), lambda i: (0, 0)),
            pl.BlockSpec((8, hid), lambda i: (0, 0)),
            pl.BlockSpec((LATE_TILE, 1), lambda i: (i, 0)),
        ],
        out_specs=[
            pl.BlockSpec((1, LATE_TILE), lambda i: (0, i)),
            pl.BlockSpec((share,), lambda i: (0,)),
        ],
        out_shape=[
            jax.ShapeDtypeStruct((1, edges), jnp.float32),
            jax.ShapeDtypeStruct((share,), jnp.float32),
        ],
        scratch_shapes=[
            pltpu.VMEM((1, PAIRS_ROW), jnp.float32),
            pltpu.VMEM((count, share), jnp.float32),
            pltpu.VMEM((count, share), jnp.float32),
            pltpu.SemaphoreType.DMA((count,)),
            pltpu.SemaphoreType.DMA((count,)),
        ],
        compiler_params=pltpu.CompilerParams(
            dimension_semantics=("arbitrary",), collective_id=0, has_side_effects=True),
        cost_estimate=pl.CostEstimate(
            flops=2 * edges * 2 * (rows + hid) * width, transcendentals=edges * hid,
            bytes_accessed=rows * width * 2 + edges * hid * 4),
    )(late_index.T, partial, table, w_first, w_first, b_first.reshape(1, hid), wo8, pair_ids)
    return scores.reshape(edges), cost


def body(embedding, send_list, edge_ends, pair_index, w_first, b_first, w_second):
    node_count = lax.axis_size("node")
    node_self = lax.axis_index("node")
    blocks_here = embedding.shape[0]
    block_rows = embedding.shape[1]
    feature_width = embedding.shape[2]
    lanes = 128
    parts = feature_width // lanes
    early_len = EARLY_ROWS * parts
    late_rows = block_rows - EARLY_ROWS
    slot_len = early_len + 8
    wanted = send_list[0, 0]
    pick = jnp.where(wanted >= 0, wanted, blocks_here)
    narrow = embedding.reshape(blocks_here, block_rows * parts, lanes)
    narrow = jnp.concatenate([narrow, jnp.zeros((1, block_rows * parts, lanes), embedding.dtype)], axis=0)
    marks = jnp.arange(blocks_here + 1, dtype=jnp.int32)
    marks = jnp.where(marks < blocks_here, marks, -1).astype(embedding.dtype)
    marks = jnp.broadcast_to(marks[:, None, None], (blocks_here + 1, 8, lanes))
    early_source = jnp.concatenate([narrow[:, :early_len], marks], axis=1)
    late_source = jnp.concatenate([embedding[:, EARLY_ROWS:], jnp.zeros((1, late_rows, feature_width), embedding.dtype)], axis=0)
    early_picked = jnp.take(early_source, pick, axis=0, mode="clip")
    late_picked = jnp.take(late_source, pick, axis=0, mode="clip")
    early_arrived = lax.all_to_all(early_picked, "node", split_axis=0, concat_axis=0, tiled=True)
    source = edge_ends // (blocks_here * block_rows)
    block_of = (edge_ends // block_rows) % blocks_here
    within = edge_ends % block_rows
    early = within < EARLY_ROWS
    early_position = source * slot_len + jnp.where(early, within, 0) * parts
    late_rows = block_rows - EARLY_ROWS
    late_spot = source * late_rows + within - EARLY_ROWS
    pair_ids = (pair_index - node_self * PAIRS_ROW).reshape(-1, 1)
    late_picked, early_arrived, early_position, late_spot, pair_ids = lax.optimization_barrier(
        (late_picked, early_arrived, early_position, late_spot, pair_ids))
    late_arrived = lax.all_to_all(late_picked, "node", split_axis=0, concat_axis=0, tiled=True)
    early_table = early_arrived.reshape(node_count * slot_len, lanes)
    late_table = late_arrived.reshape(node_count * late_rows, feature_width)
    sent = early_arrived[:, early_len, 0].astype(jnp.int32)
    located = jnp.any((source[..., None] == jnp.arange(node_count, dtype=jnp.int32))
                      & (block_of[..., None] == sent), axis=-1)
    early_mask = (located & early).T.astype(jnp.float32)
    late_index = jnp.where(located & ~early, late_spot, -1)
    partial = early_products(early_position, early_mask, early_table, w_first)
    edge_score, pair_cost = late_scores(late_index, partial, pair_ids, late_table, w_first, b_first, w_second,
                                        lax.axis_size("edge"))
    return (edge_score, pair_cost)


def solution(mesh):
    return jax.shard_map(
        body,
        mesh=mesh,
        in_specs=(
            P("node", None, None),
            P("edge", "node", None),
            P(None, ("node", "edge")),
            P(("node", "edge")),
            P(),
            P(),
            P(),
        ),
        out_specs=(P(("node", "edge")), P(("node", "edge"))),
        check_vma=False,
    )
```

```python
import functools

import jax
import jax.numpy as jnp
from jax import lax
from jax.experimental import pallas as pl
from jax.experimental.pallas import tpu as pltpu
from jax.sharding import PartitionSpec as P

PAIRS_ROW = 1024
TILE = 512
LATE_TILE = 512
EARLY_ROWS = 96


def gelu_tanh(x):
    return x * (0.5 * (1.0 + jnp.tanh(0.7978845608028654 * (x + 0.044715 * (x * x * x)))))


def early_kernel(edges, pos_ref, table, mask_ref, wt_ref, wb_ref, part_ref, buf, wide, sems):
    step = pl.program_id(0)
    steps = pl.num_programs(0)
    parts = buf.shape[2] // TILE
    lanes = buf.shape[3]

    def fetch(tile, slot):
        base = tile * TILE

        def one(r, carry):
            dst = pl.ds(pl.multiple_of(r * parts, parts), parts)
            for end in range(2):
                src = pl.ds(pl.multiple_of(pos_ref[end * edges + base + r], parts), parts)
                pltpu.make_async_copy(table.at[src], buf.at[end, slot, dst], sems.at[end, slot]).start()
            return carry

        lax.fori_loop(0, TILE, one, 0, unroll=8)

    @pl.when(step == 0)
    def _():
        fetch(0, 0)

    slot = step % 2

    @pl.when(step + 1 < steps)
    def _():
        fetch(step + 1, 1 - slot)

    for end in range(2):
        pltpu.make_async_copy(table.at[pl.ds(0, TILE * parts)], buf.at[end, slot], sems.at[end, slot]).wait()

    mask = mask_ref[...]
    total = None
    for end, w_ref in ((0, wt_ref), (1, wb_ref)):
        wide[...] = buf[end, slot].astype(jnp.float32)
        keep = mask[:, end:end + 1] > 0
        for q in range(parts):
            piece = wide[pl.ds(q, TILE, stride=parts), :]
            piece = jnp.where(keep, piece, jnp.zeros_like(piece)).astype(jnp.bfloat16)
            term = jnp.dot(piece, w_ref[q * lanes:(q + 1) * lanes, :], preferred_element_type=jnp.float32)
            total = term if total is None else total + term
    part_ref[...] = total


def late_kernel(idx_ref, part_ref, table_ref, wt_ref, wb_ref, bias_ref, wo_ref, pid_ref, score_ref, cost_ref,
                pool, chunks, recv, send_sems, recv_sems):
    step = pl.program_id(0)
    steps = pl.num_programs(0)
    count = recv.shape[0]
    width = recv.shape[1]
    me = lax.axis_index("edge")
    node = lax.axis_index("node")
    barrier = pltpu.get_barrier_semaphore()

    @pl.when(step == 0)
    def _():
        def greet(k, carry):
            pl.semaphore_signal(barrier, 1, device_id=(node, (me + k) % count), device_id_type=pl.DeviceIdType.MESH)
            return carry

        lax.fori_loop(1, count, greet, 0)
        pool[...] = jnp.zeros_like(pool)

    idx = idx_ref[...]
    rows = table_ref.shape[0]
    slots = lax.broadcasted_iota(jnp.int32, (LATE_TILE, rows), 1)
    preact = part_ref[...]
    for end, w_ref in ((0, wt_ref), (1, wb_ref)):
        onehot = (idx[:, end:end + 1] == slots).astype(table_ref.dtype)
        picked = jnp.dot(onehot, table_ref[...], preferred_element_type=jnp.float32).astype(table_ref.dtype)
        preact = preact + jnp.dot(picked, w_ref[...], preferred_element_type=jnp.float32)
    hidden = gelu_tanh(preact + bias_ref[...])
    scores = jnp.sum(hidden * wo_ref[0:1, :], axis=1, keepdims=True)
    score_ref[...] = jnp.broadcast_to(scores, (LATE_TILE, 128)).T[0:1, :]
    pair_range = lax.broadcasted_iota(jnp.int32, (LATE_TILE, PAIRS_ROW), 1)
    pooled = jnp.where(pid_ref[...] == pair_range, scores, 0.0)
    pool[...] += jnp.sum(pooled, axis=0, keepdims=True)

    @pl.when(step == steps - 1)
    def _():
        for t in range(count):
            chunks[t:t + 1, :] = pool[:, t * width:(t + 1) * width]
        pl.semaphore_wait(barrier, count - 1)

        def remote(target, slot):
            return pltpu.make_async_remote_copy(
                chunks.at[pl.ds(target, 1)], recv.at[pl.ds(slot, 1)], send_sems.at[target], recv_sems.at[slot],
                device_id=(node, target), device_id_type=pl.DeviceIdType.MESH)

        def send(k, carry):
            remote((me + k) % count, me).start()
            return carry

        lax.fori_loop(1, count, send, 0)

        def finish(k, carry):
            remote((me + k) % count, me).wait_send()
            source = (me + count - k) % count
            remote(source, source).wait_recv()
            return carry

        lax.fori_loop(1, count, finish, 0)
        here = lax.broadcasted_iota(jnp.int32, (count, width), 0)
        cost_ref[...] = jnp.sum(jnp.where(here == me, chunks[...], recv[...]), axis=0)


def early_products(position, mask, table, w_first):
    edges = position.shape[1]
    lanes = table.shape[1]
    width = w_first.shape[0] // 2
    parts = width // lanes
    hid = w_first.shape[1]
    grid_spec = pltpu.PrefetchScalarGridSpec(
        num_scalar_prefetch=1,
        grid=(edges // TILE,),
        in_specs=[
            pl.BlockSpec(memory_space=pl.ANY),
            pl.BlockSpec((TILE, 2), lambda i, p: (i, 0)),
            pl.BlockSpec((width, hid), lambda i, p: (0, 0)),
            pl.BlockSpec((width, hid), lambda i, p: (1, 0)),
        ],
        out_specs=pl.BlockSpec((TILE, hid), lambda i, p: (i, 0)),
        scratch_shapes=[
            pltpu.VMEM((2, 2, TILE * parts, lanes), table.dtype),
            pltpu.VMEM((TILE * parts, lanes), jnp.float32),
            pltpu.SemaphoreType.DMA((2, 2)),
        ],
    )
    return pl.pallas_call(
        functools.partial(early_kernel, edges),
        grid_spec=grid_spec,
        out_shape=jax.ShapeDtypeStruct((edges, hid), jnp.float32),
        compiler_params=pltpu.CompilerParams(dimension_semantics=("arbitrary",)),
        cost_estimate=pl.CostEstimate(
            flops=2 * edges * 2 * width * hid, transcendentals=0,
            bytes_accessed=2 * edges * width * table.dtype.itemsize + edges * hid * 4),
    )(position.reshape(2 * edges), table, mask, w_first, w_first)


def late_scores(late_index, partial, pair_ids, table, w_first, b_first, w_second, count):
    edges = late_index.shape[1]
    rows, width = table.shape
    hid = w_first.shape[1]
    share = PAIRS_ROW // count
    wo8 = jnp.broadcast_to(w_second.astype(jnp.float32)[None, :], (8, hid))
    scores, cost = pl.pallas_call(
        late_kernel,
        grid=(edges // LATE_TILE,),
        in_specs=[
            pl.BlockSpec((LATE_TILE, 2), lambda i: (i, 0)),
            pl.BlockSpec((LATE_TILE, hid), lambda i: (i, 0)),
            pl.BlockSpec((rows, width), lambda i: (0, 0)),
            pl.BlockSpec((width, hid), lambda i: (0, 0)),
            pl.BlockSpec((width, hid), lambda i: (1, 0)),
            pl.BlockSpec((1, hid), lambda i: (0, 0)),
            pl.BlockSpec((8, hid), lambda i: (0, 0)),
            pl.BlockSpec((LATE_TILE, 1), lambda i: (i, 0)),
        ],
        out_specs=[
            pl.BlockSpec((1, LATE_TILE), lambda i: (0, i)),
            pl.BlockSpec((share,), lambda i: (0,)),
        ],
        out_shape=[
            jax.ShapeDtypeStruct((1, edges), jnp.float32),
            jax.ShapeDtypeStruct((share,), jnp.float32),
        ],
        scratch_shapes=[
            pltpu.VMEM((1, PAIRS_ROW), jnp.float32),
            pltpu.VMEM((count, share), jnp.float32),
            pltpu.VMEM((count, share), jnp.float32),
            pltpu.SemaphoreType.DMA((count,)),
            pltpu.SemaphoreType.DMA((count,)),
        ],
        compiler_params=pltpu.CompilerParams(
            dimension_semantics=("arbitrary",), collective_id=0, has_side_effects=True),
        cost_estimate=pl.CostEstimate(
            flops=2 * edges * 2 * (rows + hid) * width, transcendentals=edges * hid,
            bytes_accessed=rows * width * 2 + edges * hid * 4),
    )(late_index.T, partial, table, w_first, w_first, b_first.reshape(1, hid), wo8, pair_ids)
    return scores.reshape(edges), cost


def body(embedding, send_list, edge_ends, pair_index, w_first, b_first, w_second):
    node_count = lax.axis_size("node")
    node_self = lax.axis_index("node")
    blocks_here = embedding.shape[0]
    block_rows = embedding.shape[1]
    feature_width = embedding.shape[2]
    lanes = 128
    parts = feature_width // lanes
    early_len = EARLY_ROWS * parts
    late_rows = block_rows - EARLY_ROWS
    slot_len = early_len + 8
    wanted = send_list[0, 0]
    pick = jnp.where(wanted >= 0, wanted, blocks_here)
    narrow = embedding[:, :EARLY_ROWS].reshape(blocks_here, early_len, lanes)
    narrow = jnp.concatenate([narrow, jnp.zeros((1, early_len, lanes), embedding.dtype)], axis=0)
    marks = jnp.arange(blocks_here + 1, dtype=jnp.int32)
    marks = jnp.where(marks < blocks_here, marks, -1).astype(embedding.dtype)
    marks = jnp.broadcast_to(marks[:, None, None], (blocks_here + 1, 8, lanes))
    early_source = jnp.concatenate([narrow, marks], axis=1)
    late_source = jnp.concatenate([embedding[:, EARLY_ROWS:], jnp.zeros((1, late_rows, feature_width), embedding.dtype)], axis=0)
    early_picked = jnp.take(early_source, pick, axis=0, mode="clip")
    late_picked = jnp.take(late_source, pick, axis=0, mode="clip")
    early_arrived = lax.all_to_all(early_picked, "node", split_axis=0, concat_axis=0, tiled=True)
    source = edge_ends // (blocks_here * block_rows)
    block_of = (edge_ends // block_rows) % blocks_here
    within = edge_ends % block_rows
    early = within < EARLY_ROWS
    early_position = source * slot_len + jnp.where(early, within, 0) * parts
    late_rows = block_rows - EARLY_ROWS
    late_spot = source * late_rows + within - EARLY_ROWS
    pair_ids = (pair_index - node_self * PAIRS_ROW).reshape(-1, 1)
    late_picked, early_arrived, early_position, late_spot, pair_ids = lax.optimization_barrier(
        (late_picked, early_arrived, early_position, late_spot, pair_ids))
    late_arrived = lax.all_to_all(late_picked, "node", split_axis=0, concat_axis=0, tiled=True)
    early_table = early_arrived.reshape(node_count * slot_len, lanes)
    late_table = late_arrived.reshape(node_count * late_rows, feature_width)
    sent = early_arrived[:, early_len, 0].astype(jnp.int32)
    located = jnp.any((source[..., None] == jnp.arange(node_count, dtype=jnp.int32))
                      & (block_of[..., None] == sent), axis=-1)
    early_mask = (located & early).T.astype(jnp.float32)
    late_index = jnp.where(located & ~early, late_spot, -1)
    partial = early_products(early_position, early_mask, early_table, w_first)
    edge_score, pair_cost = late_scores(late_index, partial, pair_ids, late_table, w_first, b_first, w_second,
                                        lax.axis_size("edge"))
    return (edge_score, pair_cost)


def solution(mesh):
    return jax.shard_map(
        body,
        mesh=mesh,
        in_specs=(
            P("node", None, None),
            P("edge", "node", None),
            P(None, ("node", "edge")),
            P(("node", "edge")),
            P(),
            P(),
            P(),
        ),
        out_specs=(P(("node", "edge")), P(("node", "edge"))),
        check_vma=False,
    )
```

```python
import functools

import jax
import jax.numpy as jnp
from jax import lax
from jax.experimental import pallas as pl
from jax.experimental.pallas import tpu as pltpu
from jax.sharding import PartitionSpec as P

PAIRS_ROW = 1024
TILE = 512
LATE_TILE = 512
EARLY_ROWS = 96


def gelu_tanh(x):
    return x * (0.5 * (1.0 + jnp.tanh(0.7978845608028654 * (x + 0.044715 * (x * x * x)))))


def early_kernel(edges, pos_ref, table, mask_ref, wt_ref, wb_ref, part_ref, buf, wide, sems):
    step = pl.program_id(0)
    steps = pl.num_programs(0)
    parts = buf.shape[2] // TILE
    lanes = buf.shape[3]

    def fetch(tile, slot):
        base = tile * TILE

        def one(r, carry):
            dst = pl.ds(pl.multiple_of(r * parts, parts), parts)
            for end in range(2):
                src = pl.ds(pl.multiple_of(pos_ref[end * edges + base + r], parts), parts)
                pltpu.make_async_copy(table.at[src], buf.at[end, slot, dst], sems.at[end, slot]).start()
            return carry

        lax.fori_loop(0, TILE, one, 0, unroll=8)

    @pl.when(step == 0)
    def _():
        fetch(0, 0)

    slot = step % 2

    @pl.when(step + 1 < steps)
    def _():
        fetch(step + 1, 1 - slot)

    for end in range(2):
        pltpu.make_async_copy(table.at[pl.ds(0, TILE * parts)], buf.at[end, slot], sems.at[end, slot]).wait()

    mask = mask_ref[...]
    total = None
    for end, w_ref in ((0, wt_ref), (1, wb_ref)):
        wide[...] = buf[end, slot].astype(jnp.float32)
        keep = mask[:, end:end + 1] > 0
        for q in range(parts):
            piece = wide[pl.ds(q, TILE, stride=parts), :]
            piece = jnp.where(keep, piece, jnp.zeros_like(piece)).astype(jnp.bfloat16)
            term = jnp.dot(piece, w_ref[q * lanes:(q + 1) * lanes, :], preferred_element_type=jnp.float32)
            total = term if total is None else total + term
    part_ref[...] = total


def late_kernel(idx_ref, part_ref, table_ref, wt_ref, wb_ref, bias_ref, wo_ref, pid_ref, score_ref, cost_ref,
                pool, chunks, recv, send_sems, recv_sems):
    step = pl.program_id(0)
    steps = pl.num_programs(0)
    count = recv.shape[0]
    width = recv.shape[1]
    me = lax.axis_index("edge")
    node = lax.axis_index("node")
    barrier = pltpu.get_barrier_semaphore()

    @pl.when(step == 0)
    def _():
        def greet(k, carry):
            pl.semaphore_signal(barrier, 1, device_id=(node, (me + k) % count), device_id_type=pl.DeviceIdType.MESH)
            return carry

        lax.fori_loop(1, count, greet, 0)
        pool[...] = jnp.zeros_like(pool)

    idx = idx_ref[...]
    rows = table_ref.shape[0]
    slots = lax.broadcasted_iota(jnp.int32, (LATE_TILE, rows), 1)
    preact = part_ref[...]
    for end, w_ref in ((0, wt_ref), (1, wb_ref)):
        onehot = (idx[:, end:end + 1] == slots).astype(table_ref.dtype)
        picked = jnp.dot(onehot, table_ref[...], preferred_element_type=jnp.float32).astype(table_ref.dtype)
        preact = preact + jnp.dot(picked, w_ref[...], preferred_element_type=jnp.float32)
    hidden = gelu_tanh(preact + bias_ref[...])
    scores = jnp.sum(hidden * wo_ref[0:1, :], axis=1, keepdims=True)
    score_ref[...] = jnp.broadcast_to(scores, (LATE_TILE, 128)).T[0:1, :]
    pair_range = lax.broadcasted_iota(jnp.int32, (LATE_TILE, PAIRS_ROW), 1)
    pooled = jnp.where(pid_ref[...] == pair_range, scores, 0.0)
    pool[...] += jnp.sum(pooled, axis=0, keepdims=True)

    @pl.when(step == steps - 1)
    def _():
        for t in range(count):
            chunks[t:t + 1, :] = pool[:, t * width:(t + 1) * width]
        pl.semaphore_wait(barrier, count - 1)

        def remote(target, slot):
            return pltpu.make_async_remote_copy(
                chunks.at[pl.ds(target, 1)], recv.at[pl.ds(slot, 1)], send_sems.at[target], recv_sems.at[slot],
                device_id=(node, target), device_id_type=pl.DeviceIdType.MESH)

        def send(k, carry):
            remote((me + k) % count, me).start()
            return carry

        lax.fori_loop(1, count, send, 0)

        def finish(k, carry):
            remote((me + k) % count, me).wait_send()
            source = (me + count - k) % count
            remote(source, source).wait_recv()
            return carry

        lax.fori_loop(1, count, finish, 0)
        here = lax.broadcasted_iota(jnp.int32, (count, width), 0)
        cost_ref[...] = jnp.sum(jnp.where(here == me, chunks[...], recv[...]), axis=0)


def early_products(position, mask, table, w_first):
    edges = position.shape[1]
    lanes = table.shape[1]
    width = w_first.shape[0] // 2
    parts = width // lanes
    hid = w_first.shape[1]
    grid_spec = pltpu.PrefetchScalarGridSpec(
        num_scalar_prefetch=1,
        grid=(edges // TILE,),
        in_specs=[
            pl.BlockSpec(memory_space=pl.ANY),
            pl.BlockSpec((TILE, 2), lambda i, p: (i, 0)),
            pl.BlockSpec((width, hid), lambda i, p: (0, 0)),
            pl.BlockSpec((width, hid), lambda i, p: (1, 0)),
        ],
        out_specs=pl.BlockSpec((TILE, hid), lambda i, p: (i, 0)),
        scratch_shapes=[
            pltpu.VMEM((2, 2, TILE * parts, lanes), table.dtype),
            pltpu.VMEM((TILE * parts, lanes), jnp.float32),
            pltpu.SemaphoreType.DMA((2, 2)),
        ],
    )
    return pl.pallas_call(
        functools.partial(early_kernel, edges),
        grid_spec=grid_spec,
        out_shape=jax.ShapeDtypeStruct((edges, hid), jnp.float32),
        compiler_params=pltpu.CompilerParams(dimension_semantics=("arbitrary",)),
        cost_estimate=pl.CostEstimate(
            flops=2 * edges * 2 * width * hid, transcendentals=0,
            bytes_accessed=2 * edges * width * table.dtype.itemsize + edges * hid * 4),
    )(position.reshape(2 * edges), table, mask, w_first, w_first)


def late_scores(late_index, partial, pair_ids, table, w_first, b_first, w_second, count):
    edges = late_index.shape[1]
    rows, width = table.shape
    hid = w_first.shape[1]
    share = PAIRS_ROW // count
    wo8 = jnp.broadcast_to(w_second.astype(jnp.float32)[None, :], (8, hid))
    scores, cost = pl.pallas_call(
        late_kernel,
        grid=(edges // LATE_TILE,),
        in_specs=[
            pl.BlockSpec((LATE_TILE, 2), lambda i: (i, 0)),
            pl.BlockSpec((LATE_TILE, hid), lambda i: (i, 0)),
            pl.BlockSpec((rows, width), lambda i: (0, 0)),
            pl.BlockSpec((width, hid), lambda i: (0, 0)),
            pl.BlockSpec((width, hid), lambda i: (1, 0)),
            pl.BlockSpec((1, hid), lambda i: (0, 0)),
            pl.BlockSpec((8, hid), lambda i: (0, 0)),
            pl.BlockSpec((LATE_TILE, 1), lambda i: (i, 0)),
        ],
        out_specs=[
            pl.BlockSpec((1, LATE_TILE), lambda i: (0, i)),
            pl.BlockSpec((share,), lambda i: (0,)),
        ],
        out_shape=[
            jax.ShapeDtypeStruct((1, edges), jnp.float32),
            jax.ShapeDtypeStruct((share,), jnp.float32),
        ],
        scratch_shapes=[
            pltpu.VMEM((1, PAIRS_ROW), jnp.float32),
            pltpu.VMEM((count, share), jnp.float32),
            pltpu.VMEM((count, share), jnp.float32),
            pltpu.SemaphoreType.DMA((count,)),
            pltpu.SemaphoreType.DMA((count,)),
        ],
        compiler_params=pltpu.CompilerParams(
            dimension_semantics=("arbitrary",), collective_id=0, has_side_effects=True),
        cost_estimate=pl.CostEstimate(
            flops=2 * edges * 2 * (rows + hid) * width, transcendentals=edges * hid,
            bytes_accessed=rows * width * 2 + edges * hid * 4),
    )(late_index.T, partial, table, w_first, w_first, b_first.reshape(1, hid), wo8, pair_ids)
    return scores.reshape(edges), cost


def body(embedding, send_list, edge_ends, pair_index, w_first, b_first, w_second):
    node_count = lax.axis_size("node")
    node_self = lax.axis_index("node")
    blocks_here = embedding.shape[0]
    block_rows = embedding.shape[1]
    feature_width = embedding.shape[2]
    lanes = 128
    parts = feature_width // lanes
    early_len = EARLY_ROWS * parts
    late_rows = block_rows - EARLY_ROWS
    slot_len = early_len + 8
    wanted = send_list[0, 0]
    pick = wanted + 1
    narrow = embedding[:, :EARLY_ROWS].reshape(blocks_here, early_len, lanes)
    narrow = jnp.concatenate([jnp.zeros((1, early_len, lanes), embedding.dtype), narrow], axis=0)
    marks = (jnp.arange(blocks_here + 1, dtype=jnp.int32) - 1).astype(embedding.dtype)
    marks = jnp.broadcast_to(marks[:, None, None], (blocks_here + 1, 8, lanes))
    early_source = jnp.concatenate([narrow, marks], axis=1)
    late_source = jnp.concatenate([jnp.zeros((1, late_rows, feature_width), embedding.dtype), embedding[:, EARLY_ROWS:]], axis=0)
    early_picked = jnp.take(early_source, pick, axis=0, mode="clip")
    late_picked = jnp.take(late_source, pick, axis=0, mode="clip")
    early_arrived = lax.all_to_all(early_picked, "node", split_axis=0, concat_axis=0, tiled=True)
    source = edge_ends // (blocks_here * block_rows)
    block_of = (edge_ends // block_rows) % blocks_here
    within = edge_ends % block_rows
    early = within < EARLY_ROWS
    early_position = source * slot_len + jnp.where(early, within, 0) * parts
    late_rows = block_rows - EARLY_ROWS
    late_spot = source * late_rows + within - EARLY_ROWS
    pair_ids = (pair_index - node_self * PAIRS_ROW).reshape(-1, 1)
    late_picked, early_arrived, early_position, late_spot, pair_ids = lax.optimization_barrier(
        (late_picked, early_arrived, early_position, late_spot, pair_ids))
    late_arrived = lax.all_to_all(late_picked, "node", split_axis=0, concat_axis=0, tiled=True)
    early_table = early_arrived.reshape(node_count * slot_len, lanes)
    late_table = late_arrived.reshape(node_count * late_rows, feature_width)
    sent = early_arrived[:, early_len, 0].astype(jnp.int32)
    located = jnp.any((source[..., None] == jnp.arange(node_count, dtype=jnp.int32))
                      & (block_of[..., None] == sent), axis=-1)
    early_mask = (located & early).T.astype(jnp.float32)
    late_index = jnp.where(located & ~early, late_spot, -1)
    partial = early_products(early_position, early_mask, early_table, w_first)
    edge_score, pair_cost = late_scores(late_index, partial, pair_ids, late_table, w_first, b_first, w_second,
                                        lax.axis_size("edge"))
    return (edge_score, pair_cost)


def solution(mesh):
    return jax.shard_map(
        body,
        mesh=mesh,
        in_specs=(
            P("node", None, None),
            P("edge", "node", None),
            P(None, ("node", "edge")),
            P(("node", "edge")),
            P(),
            P(),
            P(),
        ),
        out_specs=(P(("node", "edge")), P(("node", "edge"))),
        check_vma=False,
    )
```

```python
import functools

import jax
import jax.numpy as jnp
from jax import lax
from jax.experimental import pallas as pl
from jax.experimental.pallas import tpu as pltpu
from jax.sharding import PartitionSpec as P

PAIRS_ROW = 1024
TILE = 512
LATE_TILE = 512
EARLY_ROWS = 96


def gelu_tanh(x):
    return x * (0.5 * (1.0 + jnp.tanh(0.7978845608028654 * (x + 0.044715 * (x * x * x)))))


def early_kernel(edges, pos_ref, table, mask_ref, wt_ref, wb_ref, part_ref, buf, wide, sems):
    step = pl.program_id(0)
    steps = pl.num_programs(0)
    parts = buf.shape[2] // TILE
    lanes = buf.shape[3]

    def fetch(tile, slot):
        base = tile * TILE

        def one(r, carry):
            dst = pl.ds(pl.multiple_of(r * parts, parts), parts)
            for end in range(2):
                src = pl.ds(pl.multiple_of(pos_ref[end * edges + base + r], parts), parts)
                pltpu.make_async_copy(table.at[src], buf.at[end, slot, dst], sems.at[end, slot]).start()
            return carry

        lax.fori_loop(0, TILE, one, 0, unroll=8)

    @pl.when(step == 0)
    def _():
        fetch(0, 0)

    slot = step % 2

    @pl.when(step + 1 < steps)
    def _():
        fetch(step + 1, 1 - slot)

    for end in range(2):
        pltpu.make_async_copy(table.at[pl.ds(0, TILE * parts)], buf.at[end, slot], sems.at[end, slot]).wait()

    mask = mask_ref[...]
    total = None
    for end, w_ref in ((0, wt_ref), (1, wb_ref)):
        wide[...] = buf[end, slot].astype(jnp.float32)
        keep = mask[:, end:end + 1] > 0
        for q in range(parts):
            piece = wide[pl.ds(q, TILE, stride=parts), :]
            piece = jnp.where(keep, piece, jnp.zeros_like(piece)).astype(jnp.bfloat16)
            term = jnp.dot(piece, w_ref[q * lanes:(q + 1) * lanes, :], preferred_element_type=jnp.float32)
            total = term if total is None else total + term
    part_ref[...] = total


def late_kernel(idx_ref, part_ref, table_ref, wt_ref, wb_ref, bias_ref, wo_ref, pid_ref, score_ref, cost_ref,
                pool, chunks, recv, send_sems, recv_sems):
    step = pl.program_id(0)
    steps = pl.num_programs(0)
    count = recv.shape[0]
    width = recv.shape[1]
    me = lax.axis_index("edge")
    node = lax.axis_index("node")
    barrier = pltpu.get_barrier_semaphore()

    @pl.when(step == 0)
    def _():
        def greet(k, carry):
            pl.semaphore_signal(barrier, 1, device_id=(node, (me + k) % count), device_id_type=pl.DeviceIdType.MESH)
            return carry

        lax.fori_loop(1, count, greet, 0)
        pool[...] = jnp.zeros_like(pool)

    idx = idx_ref[...]
    rows = table_ref.shape[0]
    slots = lax.broadcasted_iota(jnp.int32, (LATE_TILE, rows), 1)
    preact = part_ref[...]
    for end, w_ref in ((0, wt_ref), (1, wb_ref)):
        onehot = jnp.where(idx[:, end:end + 1] == slots, jnp.ones((), table_ref.dtype), jnp.zeros((), table_ref.dtype))
        picked = jnp.dot(onehot, table_ref[...], preferred_element_type=jnp.float32).astype(table_ref.dtype)
        preact = preact + jnp.dot(picked, w_ref[...], preferred_element_type=jnp.float32)
    hidden = gelu_tanh(preact + bias_ref[...])
    scores = jnp.sum(hidden * wo_ref[0:1, :], axis=1, keepdims=True)
    score_ref[...] = jnp.broadcast_to(scores, (LATE_TILE, 128)).T[0:1, :]
    pair_range = lax.broadcasted_iota(jnp.int32, (LATE_TILE, PAIRS_ROW), 1)
    pooled = jnp.where(pid_ref[...] == pair_range, scores, 0.0)
    pool[...] += jnp.sum(pooled, axis=0, keepdims=True)

    @pl.when(step == steps - 1)
    def _():
        for t in range(count):
            chunks[t:t + 1, :] = pool[:, t * width:(t + 1) * width]
        pl.semaphore_wait(barrier, count - 1)

        def remote(target, slot):
            return pltpu.make_async_remote_copy(
                chunks.at[pl.ds(target, 1)], recv.at[pl.ds(slot, 1)], send_sems.at[target], recv_sems.at[slot],
                device_id=(node, target), device_id_type=pl.DeviceIdType.MESH)

        def send(k, carry):
            remote((me + k) % count, me).start()
            return carry

        lax.fori_loop(1, count, send, 0)

        def finish(k, carry):
            remote((me + k) % count, me).wait_send()
            source = (me + count - k) % count
            remote(source, source).wait_recv()
            return carry

        lax.fori_loop(1, count, finish, 0)
        here = lax.broadcasted_iota(jnp.int32, (count, width), 0)
        cost_ref[...] = jnp.sum(jnp.where(here == me, chunks[...], recv[...]), axis=0)


def early_products(position, mask, table, w_first):
    edges = position.shape[1]
    lanes = table.shape[1]
    width = w_first.shape[0] // 2
    parts = width // lanes
    hid = w_first.shape[1]
    grid_spec = pltpu.PrefetchScalarGridSpec(
        num_scalar_prefetch=1,
        grid=(edges // TILE,),
        in_specs=[
            pl.BlockSpec(memory_space=pl.ANY),
            pl.BlockSpec((TILE, 2), lambda i, p: (i, 0)),
            pl.BlockSpec((width, hid), lambda i, p: (0, 0)),
            pl.BlockSpec((width, hid), lambda i, p: (1, 0)),
        ],
        out_specs=pl.BlockSpec((TILE, hid), lambda i, p: (i, 0)),
        scratch_shapes=[
            pltpu.VMEM((2, 2, TILE * parts, lanes), table.dtype),
            pltpu.VMEM((TILE * parts, lanes), jnp.float32),
            pltpu.SemaphoreType.DMA((2, 2)),
        ],
    )
    return pl.pallas_call(
        functools.partial(early_kernel, edges),
        grid_spec=grid_spec,
        out_shape=jax.ShapeDtypeStruct((edges, hid), jnp.float32),
        compiler_params=pltpu.CompilerParams(dimension_semantics=("arbitrary",)),
        cost_estimate=pl.CostEstimate(
            flops=2 * edges * 2 * width * hid, transcendentals=0,
            bytes_accessed=2 * edges * width * table.dtype.itemsize + edges * hid * 4),
    )(position.reshape(2 * edges), table, mask, w_first, w_first)


def late_scores(late_index, partial, pair_ids, table, w_first, b_first, w_second, count):
    edges = late_index.shape[1]
    rows, width = table.shape
    hid = w_first.shape[1]
    share = PAIRS_ROW // count
    wo8 = jnp.broadcast_to(w_second.astype(jnp.float32)[None, :], (8, hid))
    scores, cost = pl.pallas_call(
        late_kernel,
        grid=(edges // LATE_TILE,),
        in_specs=[
            pl.BlockSpec((LATE_TILE, 2), lambda i: (i, 0)),
            pl.BlockSpec((LATE_TILE, hid), lambda i: (i, 0)),
            pl.BlockSpec((rows, width), lambda i: (0, 0)),
            pl.BlockSpec((width, hid), lambda i: (0, 0)),
            pl.BlockSpec((width, hid), lambda i: (1, 0)),
            pl.BlockSpec((1, hid), lambda i: (0, 0)),
            pl.BlockSpec((8, hid), lambda i: (0, 0)),
            pl.BlockSpec((LATE_TILE, 1), lambda i: (i, 0)),
        ],
        out_specs=[
            pl.BlockSpec((1, LATE_TILE), lambda i: (0, i)),
            pl.BlockSpec((share,), lambda i: (0,)),
        ],
        out_shape=[
            jax.ShapeDtypeStruct((1, edges), jnp.float32),
            jax.ShapeDtypeStruct((share,), jnp.float32),
        ],
        scratch_shapes=[
            pltpu.VMEM((1, PAIRS_ROW), jnp.float32),
            pltpu.VMEM((count, share), jnp.float32),
            pltpu.VMEM((count, share), jnp.float32),
            pltpu.SemaphoreType.DMA((count,)),
            pltpu.SemaphoreType.DMA((count,)),
        ],
        compiler_params=pltpu.CompilerParams(
            dimension_semantics=("arbitrary",), collective_id=0, has_side_effects=True),
        cost_estimate=pl.CostEstimate(
            flops=2 * edges * 2 * (rows + hid) * width, transcendentals=edges * hid,
            bytes_accessed=rows * width * 2 + edges * hid * 4),
    )(late_index.T, partial, table, w_first, w_first, b_first.reshape(1, hid), wo8, pair_ids)
    return scores.reshape(edges), cost


def body(embedding, send_list, edge_ends, pair_index, w_first, b_first, w_second):
    node_count = lax.axis_size("node")
    node_self = lax.axis_index("node")
    blocks_here = embedding.shape[0]
    block_rows = embedding.shape[1]
    feature_width = embedding.shape[2]
    lanes = 128
    parts = feature_width // lanes
    early_len = EARLY_ROWS * parts
    late_rows = block_rows - EARLY_ROWS
    slot_len = early_len + 8
    wanted = send_list[0, 0]
    pick = wanted + 1
    narrow = embedding[:, :EARLY_ROWS].reshape(blocks_here, early_len, lanes)
    narrow = jnp.concatenate([jnp.zeros((1, early_len, lanes), embedding.dtype), narrow], axis=0)
    marks = (jnp.arange(blocks_here + 1, dtype=jnp.int32) - 1).astype(embedding.dtype)
    marks = jnp.broadcast_to(marks[:, None, None], (blocks_here + 1, 8, lanes))
    early_source = jnp.concatenate([narrow, marks], axis=1)
    late_source = jnp.concatenate([jnp.zeros((1, late_rows, feature_width), embedding.dtype), embedding[:, EARLY_ROWS:]], axis=0)
    early_picked = jnp.take(early_source, pick, axis=0, mode="clip")
    late_picked = jnp.take(late_source, pick, axis=0, mode="clip")
    early_arrived = lax.all_to_all(early_picked, "node", split_axis=0, concat_axis=0, tiled=True)
    source = edge_ends // (blocks_here * block_rows)
    block_of = (edge_ends // block_rows) % blocks_here
    within = edge_ends % block_rows
    early = within < EARLY_ROWS
    early_position = source * slot_len + jnp.where(early, within, 0) * parts
    late_rows = block_rows - EARLY_ROWS
    late_spot = source * late_rows + within - EARLY_ROWS
    pair_ids = (pair_index - node_self * PAIRS_ROW).reshape(-1, 1)
    late_picked, early_arrived, early_position, late_spot, pair_ids = lax.optimization_barrier(
        (late_picked, early_arrived, early_position, late_spot, pair_ids))
    late_arrived = lax.all_to_all(late_picked, "node", split_axis=0, concat_axis=0, tiled=True)
    early_table = early_arrived.reshape(node_count * slot_len, lanes)
    late_table = late_arrived.reshape(node_count * late_rows, feature_width)
    sent = early_arrived[:, early_len, 0].astype(jnp.int32)
    located = jnp.any((source[..., None] == jnp.arange(node_count, dtype=jnp.int32))
                      & (block_of[..., None] == sent), axis=-1)
    early_mask = (located & early).T.astype(jnp.float32)
    late_index = jnp.where(located & ~early, late_spot, -1)
    partial = early_products(early_position, early_mask, early_table, w_first)
    edge_score, pair_cost = late_scores(late_index, partial, pair_ids, late_table, w_first, b_first, w_second,
                                        lax.axis_size("edge"))
    return (edge_score, pair_cost)


def solution(mesh):
    return jax.shard_map(
        body,
        mesh=mesh,
        in_specs=(
            P("node", None, None),
            P("edge", "node", None),
            P(None, ("node", "edge")),
            P(("node", "edge")),
            P(),
            P(),
            P(),
        ),
        out_specs=(P(("node", "edge")), P(("node", "edge"))),
        check_vma=False,
    )
```
